32 devices in a mesh: replica: 8 (over y, x, core), shard: 4 (over z).
Axes of the slice: x: 2, y: 2, z: 4, core: 2. Of those that a mesh axis runs over, the one named last changes fastest.
Arguments:
- tokens: bfloat16 [8192, 1536], P(('replica', 'shard')), may hold values from -8 to 8
- cotangent: bfloat16 [8192, 1536], P(('replica', 'shard')), may hold values from -6 to 6
- attn_gain: bfloat16 [1536], P('shard'), may hold values from 0.5 to 1.5
- w_query: bfloat16 [1536, 1536], P('shard'), may hold values from -0.17860863 to 0.17860863
- w_key: bfloat16 [1536, 768], P('shard'), may hold values from -0.17860863 to 0.17860863
- w_value: bfloat16 [1536, 768], P('shard'), may hold values from -0.15625 to 0.15625
- w_out: bfloat16 [1536, 1536], P('shard'), may hold values from -0.625 to 0.625
- mlp_gain: bfloat16 [1536], P('shard'), may hold values from 0.5 to 1.5
- w_gate: bfloat16 [1536, 4096], P('shard'), may hold values from -0.15625 to 0.15625
- w_up: bfloat16 [1536, 4096], P('shard'), may hold values from -0.15625 to 0.15625
- w_down: bfloat16 [4096, 1536], P('shard'), may hold values from -0.09375 to 0.09375
Outputs:
- block_output: bfloat16 [8192, 1536], P(('replica', 'shard'))
- input_grad: float32 [8192, 1536], P(('replica', 'shard'))
- attn_gain_grad: float32 [1536], P('shard')
- query_grad: float32 [1536, 1536], P('shard')
- key_grad: float32 [1536, 768], P('shard')
- value_grad: float32 [1536, 768], P('shard')
- out_grad: float32 [1536, 1536], P('shard')
- mlp_gain_grad: float32 [1536], P('shard')
- gate_grad: float32 [1536, 4096], P('shard')
- up_grad: float32 [1536, 4096], P('shard')
- down_grad: float32 [4096, 1536], P('shard')
The draws below stay inside these ranges and needn't reach their ends.
All inputs are finite; a program needn't handle non-finite values.
Results may differ from the reference program's by a relative error of at most 0.014.
Values may be sent and summed in bfloat16 or wider, within the bound.
No kernel may reach another device: no remote copies, remote signals or barrier semaphores. Data moves between devices by JAX's collectives and lax.ppermute only.
A program may use at most 384 MiB of HBM per device.

```python
import jax
import jax.numpy as jnp
from jax import lax

D = 1536
FF = 4096
KV_HEADS = 8
HEAD_DIM = 96
SEQ = 256
TOKENS = 8192


def draw_tokens(key, part):
    values = jnp.clip(jax.random.normal(jax.random.fold_in(key, 11), (TOKENS, D), jnp.float32), -6.0, 6.0)
    return values.astype(jnp.bfloat16)


def draw_w_query(key, part):
    values = jnp.clip(jax.random.normal(jax.random.fold_in(key, 21), (D, D), jnp.float32), -6.0, 6.0) * D ** (-0.5)
    return values.astype(jnp.bfloat16)


def draw_w_key(key, part):
    width = KV_HEADS * HEAD_DIM
    values = jnp.clip(jax.random.normal(jax.random.fold_in(key, 31), (D, width), jnp.float32), -6.0, 6.0) * D ** (-0.5)
    return values.astype(jnp.bfloat16)


def block_levels(rng, shape, shards, smallest, high):
    loudness = 1.0
    for axis_at, parts in shards:
        steps = jax.random.uniform(jax.random.fold_in(jax.random.fold_in(rng, 6), axis_at), (parts,), jnp.float32, smallest / len(shards), high / len(shards))
        loudness = loudness * jnp.repeat(jnp.exp(steps), shape[axis_at] // parts).reshape((-1,) + (1,) * (len(shape) - 1 - axis_at))
    return loudness


def noise(key, shape, scale, most, shards=(), kind=jnp.bfloat16):
    result = jax.random.normal(key, shape, jnp.float32) * scale
    if len(shards) > 0:
        result = block_levels(key, shape, shards, -0.22, 0.18) * result
    return jnp.clip(result, min=-most, max=most).astype(kind)


def setup_inputs(seed: int = 0) -> dict:
    seeds = jax.random.split(jax.random.key(seed), 12)
    return {
        "tokens": draw_tokens(jax.random.fold_in(seeds[11], 71), 0),
        "cotangent": noise(seeds[1], (TOKENS, D), 1.0, 6.0, ((0, 32),)),
        "attn_gain": jnp.clip(1.0 + 0.1 * jax.random.normal(seeds[2], (D,), jnp.float32), 0.5, 1.5).astype(jnp.bfloat16),
        "w_query": draw_w_query(jax.random.fold_in(seeds[11], 71), 0),
        "w_key": draw_w_key(jax.random.fold_in(seeds[11], 71), 0),
        "w_value": noise(seeds[5], (D, KV_HEADS * HEAD_DIM), D ** -0.5, 0.15625, ((0, 4),)),
        "w_out": noise(seeds[6], (D, D), (D // 16) ** -0.5, 0.625, ((0, 4),)),
        "mlp_gain": jnp.clip(1.0 + 0.1 * jax.random.normal(seeds[7], (D,), jnp.float32), 0.5, 1.5).astype(jnp.bfloat16),
        "w_gate": noise(seeds[8], (D, FF), D ** -0.5, 0.15625, ((0, 4),)),
        "w_up": noise(seeds[9], (D, FF), D ** -0.5, 0.15625, ((0, 4),)),
        "w_down": noise(seeds[10], (FF, D), FF ** -0.5, 0.09375, ((0, 4),)),
    }


NORM_EPS = 1e-05
ROPE_BASE = 100000.0

def product(form, left, right):
    return jnp.einsum(form, left.astype(jnp.float32), right.astype(jnp.float32))

def plain_dot(left, right):
    return jnp.dot(left, right, preferred_element_type=jnp.float32)

def outer_product(left, right):
    return lax.dot_general(left, right, (((0,), (0,)), ((), ())), preferred_element_type=jnp.float32)

def back_dot(left, right):
    return lax.dot_general(left, right, (((1,), (1,)), ((), ())), preferred_element_type=jnp.float32)

def rope_tables(length):
    half = HEAD_DIM // 2
    position = jnp.arange(length, dtype=jnp.float32)
    freqs = jnp.power(ROPE_BASE, -jnp.arange(half, dtype=jnp.float32) / half)
    angles = position[:, None] * freqs[None, :]
    return (jnp.cos(angles)[:, None, :], jnp.sin(angles)[:, None, :])

def rotate(values, cosine, sine):
    half = HEAD_DIM // 2
    first, second = (values[..., :half], values[..., half:])
    return jnp.concatenate([first * cosine - second * sine, second * cosine + first * sine], -1)

def unrotate(values, cosine, sine):
    half = HEAD_DIM // 2
    first, second = (values[..., :half], values[..., half:])
    return jnp.concatenate([first * cosine + second * sine, second * cosine - first * sine], -1)

def norm_forward(rows, norm_gain):
    inverse_rms = lax.rsqrt(lax.optimization_barrier(jnp.mean(rows * rows, -1, keepdims=True)) + NORM_EPS)
    return (rows * inverse_rms * norm_gain, inverse_rms)

def norm_backward(rows, inverse_rms, norm_gain, d_normed):
    scaled = d_normed * norm_gain
    d_rows = inverse_rms * scaled - rows * inverse_rms ** 3 * lax.optimization_barrier(jnp.mean(scaled * rows, -1, keepdims=True))
    return (d_rows, lax.optimization_barrier(jnp.sum(d_normed * rows * inverse_rms, 0)))

def block_scores(query_block, key_rot, block_start, key_pos):
    block_rows = query_block.shape[0]
    scores = product('qgjd,kgd->gjqk', query_block, key_rot) * HEAD_DIM ** (-0.5)
    query_pos = block_start + jnp.arange(block_rows, dtype=jnp.int32)
    causal = query_pos[:, None] >= key_pos[None, :]
    return jnp.where(causal, scores, -jnp.inf)

def attend(query_rot, key_rot, value_low):
    length, kv_heads = (key_rot.shape[0], key_rot.shape[1])
    groups = query_rot.shape[1] // kv_heads
    block_rows = min(length, 512)
    blocks = length // block_rows
    query_blocks = query_rot.reshape(blocks, block_rows, kv_heads, groups, HEAD_DIM)
    starts = jnp.arange(blocks, dtype=jnp.int32) * block_rows
    key_pos = jnp.arange(length, dtype=jnp.int32)

    def one_block(inputs):
        query_block, block_start = inputs
        scores = block_scores(query_block, key_rot, block_start, key_pos)
        row_top = lax.optimization_barrier(jnp.max(scores, -1, keepdims=True))
        log_total = row_top + jnp.log(lax.optimization_barrier(jnp.sum(jnp.exp(scores - row_top), -1, keepdims=True)))
        probs = jnp.exp(scores - log_total).astype(jnp.bfloat16)
        mixed = product('gjqk,kgd->qgjd', probs, value_low).astype(jnp.bfloat16)
        return (mixed, log_total[..., 0])
    mixed, log_totals = lax.map(one_block, (query_blocks, starts))
    return (mixed.reshape(length, kv_heads * groups * HEAD_DIM), log_totals)

def attend_back(query_rot, key_rot, value_low, d_heads, log_totals):
    length, kv_heads = (key_rot.shape[0], key_rot.shape[1])
    groups = query_rot.shape[1] // kv_heads
    block_rows = min(length, 512)
    blocks = length // block_rows
    query_blocks = query_rot.reshape(blocks, block_rows, kv_heads, groups, HEAD_DIM)
    d_blocks = d_heads.reshape(blocks, block_rows, kv_heads, groups, HEAD_DIM)
    starts = jnp.arange(blocks, dtype=jnp.int32) * block_rows
    key_pos = jnp.arange(length, dtype=jnp.int32)
    empty = jnp.zeros((length, kv_heads, HEAD_DIM), jnp.float32)

    def one_block(carry, inputs):
        query_block, d_block, log_total, block_start = inputs
        scores = block_scores(query_block, key_rot, block_start, key_pos)
        probs = jnp.exp(scores - log_total[..., None])
        d_value = carry[1] + product('gjqk,qgjd->kgd', probs.astype(jnp.bfloat16), d_block)
        d_probs = product('qgjd,kgd->gjqk', d_block, value_low)
        delta = lax.optimization_barrier(jnp.sum(probs * d_probs, -1, keepdims=True))
        d_scores = (probs * (d_probs - delta) * HEAD_DIM ** (-0.5)).astype(jnp.bfloat16)
        d_query = product('gjqk,kgd->qgjd', d_scores, key_rot)
        d_key = carry[0] + product('gjqk,qgjd->kgd', d_scores, query_block)
        return ((d_key, d_value), d_query)
    (d_key, d_value), d_query = lax.scan(one_block, (empty, empty), (query_blocks, d_blocks, log_totals, starts))
    return (d_query.reshape(length, kv_heads * groups, HEAD_DIM), d_key, d_value)

def attention_forward(seq_in, norm_gain, w_query, w_key, w_value, w_out):
    length = seq_in.shape[0]
    kv_heads = w_key.shape[1] // HEAD_DIM
    rows = seq_in.astype(jnp.float32)
    normed, inverse_rms = norm_forward(rows, norm_gain.astype(jnp.float32))
    normed_low = normed.astype(jnp.bfloat16)
    query = plain_dot(normed_low, w_query).reshape(length, -1, HEAD_DIM)
    key = plain_dot(normed_low, w_key).reshape(length, kv_heads, HEAD_DIM)
    value_low = plain_dot(normed_low, w_value).astype(jnp.bfloat16).reshape(length, kv_heads, HEAD_DIM)
    cosine, sine = rope_tables(length)
    query_rot = rotate(query, cosine, sine).astype(jnp.bfloat16)
    key_rot = rotate(key, cosine, sine).astype(jnp.bfloat16)
    heads_low, log_totals = attend(query_rot, key_rot, value_low)
    middle = rows + plain_dot(heads_low, w_out)
    return (middle, (inverse_rms, normed_low, query_rot, key_rot, value_low, heads_low, log_totals))

def mlp_forward(middle, norm_gain, w_gate, w_up, w_down):
    normed, inverse_rms = norm_forward(middle, norm_gain.astype(jnp.float32))
    normed_low = normed.astype(jnp.bfloat16)
    gate = plain_dot(normed_low, w_gate)
    upward = plain_dot(normed_low, w_up)
    active = (jax.nn.silu(gate) * upward).astype(jnp.bfloat16)
    output = (middle + plain_dot(active, w_down)).astype(jnp.bfloat16)
    return (output, (inverse_rms, normed_low, gate, upward, active))

def mlp_backward(middle, seq_cot, norm_gain, w_gate, w_up, w_down, saved):
    inverse_rms, normed_low, gate, upward, active = saved
    cot_rows = seq_cot.astype(jnp.float32)
    d_down = outer_product(active, seq_cot)
    d_active = back_dot(seq_cot, w_down)
    sigmoid_gate = jax.nn.sigmoid(gate)
    d_gate = (d_active * upward * sigmoid_gate * (1.0 + gate * (1.0 - sigmoid_gate))).astype(jnp.bfloat16)
    d_upward = (d_active * gate * sigmoid_gate).astype(jnp.bfloat16)
    d_gate_w = outer_product(normed_low, d_gate)
    d_up_w = outer_product(normed_low, d_upward)
    d_normed = back_dot(d_gate, w_gate) + back_dot(d_upward, w_up)
    d_rows, d_gain = norm_backward(middle, inverse_rms, norm_gain.astype(jnp.float32), d_normed)
    return (cot_rows + d_rows, (d_gain, d_gate_w, d_up_w, d_down))

def attention_backward(seq_in, d_middle, norm_gain, w_query, w_key, w_value, w_out, saved):
    inverse_rms, normed_low, query_rot, key_rot, value_low, heads_low, log_totals = saved
    length = seq_in.shape[0]
    rows = seq_in.astype(jnp.float32)
    d_middle_low = d_middle.astype(jnp.bfloat16)
    d_out_w = outer_product(heads_low, d_middle_low)
    d_heads = back_dot(d_middle_low, w_out).astype(jnp.bfloat16)
    d_query, d_key, d_value = attend_back(query_rot, key_rot, value_low, d_heads, log_totals)
    cosine, sine = rope_tables(length)
    d_query_low = unrotate(d_query, cosine, sine).astype(jnp.bfloat16).reshape(length, -1)
    d_key_low = unrotate(d_key, cosine, sine).astype(jnp.bfloat16).reshape(length, -1)
    d_value_low = d_value.astype(jnp.bfloat16).reshape(length, -1)
    d_query_w = outer_product(normed_low, d_query_low)
    d_key_w = outer_product(normed_low, d_key_low)
    d_value_w = outer_product(normed_low, d_value_low)
    d_normed = back_dot(d_query_low, w_query) + back_dot(d_key_low, w_key) + back_dot(d_value_low, w_value)
    d_rows, d_gain = norm_backward(rows, inverse_rms, norm_gain.astype(jnp.float32), d_normed)
    return (d_middle + d_rows, (d_gain, d_query_w, d_key_w, d_value_w, d_out_w))

def reference(tokens, cotangent, attn_gain, w_query, w_key, w_value, w_out, mlp_gain, w_gate, w_up, w_down):
    seq_tokens = tokens.reshape(-1, SEQ, D)
    seq_cots = cotangent.reshape(-1, SEQ, D)
    attn_zero = (jnp.zeros(attn_gain.shape, jnp.float32), jnp.zeros(w_query.shape, jnp.float32), jnp.zeros(w_key.shape, jnp.float32), jnp.zeros(w_value.shape, jnp.float32), jnp.zeros(w_out.shape, jnp.float32))
    mlp_zero = (jnp.zeros(mlp_gain.shape, jnp.float32), jnp.zeros(w_gate.shape, jnp.float32), jnp.zeros(w_up.shape, jnp.float32), jnp.zeros(w_down.shape, jnp.float32))

    def one_sequence(carry, inputs):
        seq_in, seq_cot = inputs
        middle, attn_saved = attention_forward(seq_in, attn_gain, w_query, w_key, w_value, w_out)
        output, mlp_saved = mlp_forward(middle, mlp_gain, w_gate, w_up, w_down)
        d_middle, mlp_grads = mlp_backward(middle, seq_cot, mlp_gain, w_gate, w_up, w_down, mlp_saved)
        d_input, attn_grads = attention_backward(seq_in, d_middle, attn_gain, w_query, w_key, w_value, w_out, attn_saved)
        attn_total = jax.tree.map(lambda left, right: left + right, carry[0], attn_grads)
        mlp_total = jax.tree.map(lambda left, right: left + right, carry[1], mlp_grads)
        return ((attn_total, mlp_total), (output, d_input))
    (attn_sums, mlp_sums), (outputs, d_inputs) = lax.scan(one_sequence, (attn_zero, mlp_zero), (seq_tokens, seq_cots))
    return (outputs.reshape(-1, D), d_inputs.reshape(-1, D), attn_sums[0], attn_sums[1], attn_sums[2], attn_sums[3], attn_sums[4], mlp_sums[0], mlp_sums[1], mlp_sums[2], mlp_sums[3])
```

```python
import functools
import math

import jax
import jax.numpy as jnp
from jax import lax
from jax.experimental import pallas as pl
from jax.experimental.pallas import tpu as pltpu
from jax.sharding import PartitionSpec as P

HEAD_DIM = 96
LANES = 128
NORM_EPS = 1e-05
ROPE_BASE = 100000.0
VMEM_BYTES = 60 * 1024 * 1024
F32 = jnp.float32
BF16 = jnp.bfloat16


def nn(left, right):
    return jnp.dot(left, right, preferred_element_type=F32)


def nt(left, right):
    return lax.dot_general(left, right, (((1,), (1,)), ((), ())), preferred_element_type=F32)


def tn(left, right):
    return lax.dot_general(left, right, (((0,), (0,)), ((), ())), preferred_element_type=F32)


def swap(x, bit):
    size = lax.axis_size("replica")
    return lax.ppermute(x, "replica", [(i, i ^ bit) for i in range(size)])


def gather_high(x, high):
    if len(high) == 2:
        a, b = high
        rows = x.shape[0] // 2
        from_a, from_b = swap(x, a), swap(x, b)
        far = [swap(from_b[:rows], a), swap(from_a[rows:], b)]
        return far + [from_a, from_b, x]
    blocks = [x]
    for bit in high:
        blocks = [swap(y, bit) for y in blocks] + blocks
    return blocks


def high_order(high):
    if len(high) == 2:
        return [high[0] ^ high[1], high[0], high[1], 0]
    order = [0]
    for bit in high:
        order = [j ^ bit for j in order] + order
    return order


def plane_gather(x, high):
    even = jnp.concatenate(gather_high(x, high), 0)
    return swap(even, 1), even


def plane_scatter(odd, even, high, rows):
    arrived = swap(odd, 1)
    total = [
        even[k * rows : (k + 1) * rows].astype(F32) + arrived[k * rows : (k + 1) * rows].astype(F32)
        for k in range(even.shape[0] // rows)
    ]
    if len(high) == 2:
        a, b = high
        cut = rows // 2
        far, near_a, near_b, own = total
        far = far.astype(BF16)
        via_a, via_b = swap(far[:cut], a), swap(far[cut:], b)
        first_a = swap(near_a[:cut].astype(BF16), a)
        first_b = swap(near_b[cut:].astype(BF16), b)
        last_a = swap((near_a[cut:] + via_b.astype(F32)).astype(BF16), a)
        last_b = swap((near_b[:cut] + via_a.astype(F32)).astype(BF16), b)
        got_a = jnp.concatenate([first_a, last_a], 0).astype(F32)
        got_b = jnp.concatenate([last_b, first_b], 0).astype(F32)
        return own + got_a + got_b
    for bit in reversed(high):
        cut = len(total) // 2
        total = [
            mine + swap(theirs.astype(BF16), bit).astype(F32)
            for theirs, mine in zip(total[:cut], total[cut:])
        ]
    return total[0]


def rope_tables(length):
    half = HEAD_DIM // 2
    position = jnp.arange(length, dtype=F32)
    freqs = jnp.power(ROPE_BASE, -jnp.arange(half, dtype=F32) / half)
    angles = position[:, None] * freqs[None, :]
    pad = ((0, 0), (0, LANES // 2 - half))
    cosine, sine = jnp.pad(jnp.cos(angles), pad), jnp.pad(jnp.sin(angles), pad)
    return jnp.concatenate([cosine, cosine], 1), jnp.concatenate([-sine, sine], 1)


def turn(values, cosine, sine):
    return values * cosine + pltpu.roll(values, LANES // 2, 1) * sine


def turn_back(values, cosine, sine):
    return values * cosine - pltpu.roll(values, LANES // 2, 1) * sine


def head_probs(query, key):
    length = query.shape[0]
    scores = nt(query, key) * HEAD_DIM ** (-0.5)
    rows = lax.broadcasted_iota(jnp.int32, (length, length), 0)
    columns = lax.broadcasted_iota(jnp.int32, (length, length), 1)
    scores = jnp.where(rows >= columns, scores, -jnp.inf)
    raised = jnp.exp(scores - jnp.max(scores, -1, keepdims=True))
    return raised / jnp.sum(raised, -1, keepdims=True)


def head_span(k):
    return slice(k * LANES, (k + 1) * LANES)


def attn_forward_kernel(
    queries, keys, x_ref, gain_ref, w_ref, wo_ref, cos_ref, sin_ref, part_ref, qkv_ref, o_ref
):
    x = x_ref[...].astype(F32)
    inverse = lax.rsqrt(jnp.mean(x * x, -1, keepdims=True) + NORM_EPS)
    normed = (x * inverse * gain_ref[...]).astype(BF16)
    mixed = nn(normed, w_ref[...])
    cosine, sine = cos_ref[...], sin_ref[...]
    for k in range(queries + keys):
        qkv_ref[:, head_span(k)] = turn(mixed[:, head_span(k)], cosine, sine).astype(BF16)
    for k in range(queries + keys, queries + 2 * keys):
        qkv_ref[:, head_span(k)] = mixed[:, head_span(k)].astype(BF16)
    for k in range(queries):
        at = k * keys // queries
        probs = head_probs(qkv_ref[:, head_span(k)], qkv_ref[:, head_span(queries + at)])
        value = qkv_ref[:, head_span(queries + keys + at)]
        o_ref[:, head_span(k)] = nn(probs.astype(BF16), value).astype(BF16)
    part_ref[...] = nn(o_ref[...], wo_ref[...]).astype(BF16)


def whole(array):
    return pl.BlockSpec(array.shape, lambda i: (0,) * array.ndim)


def rows_of(rows, array):
    return pl.BlockSpec((rows, array.shape[1]), lambda i: (i, 0))


def params():
    return pltpu.CompilerParams(
        dimension_semantics=("arbitrary",), vmem_limit_bytes=VMEM_BYTES
    )


def attn_forward(x, gain, w, wo, tables, length, queries, keys):
    rows, width = x.shape
    wide = (queries + 2 * keys) * LANES
    return pl.pallas_call(
        functools.partial(attn_forward_kernel, queries, keys),
        grid=(rows // length,),
        in_specs=[rows_of(length, x), whole(gain), whole(w), whole(wo), whole(tables[0]), whole(tables[1])],
        out_specs=[
            pl.BlockSpec((length, width), lambda i: (i, 0)),
            pl.BlockSpec((length, wide), lambda i: (i, 0)),
            pl.BlockSpec((length, queries * LANES), lambda i: (i, 0)),
        ],
        out_shape=[
            jax.ShapeDtypeStruct((rows, width), BF16),
            jax.ShapeDtypeStruct((rows, wide), BF16),
            jax.ShapeDtypeStruct((rows, queries * LANES), BF16),
        ],
        compiler_params=params(),
        cost_estimate=pl.CostEstimate(
            flops=2 * rows * width * (wide + queries * LANES) + 4 * rows * length * queries * LANES,
            bytes_accessed=rows * width * 4 + width * wide * 2,
            transcendentals=rows * length * queries,
        ),
        name="attn_forward",
    )(x, gain, w, wo, tables[0], tables[1])


def mlp_kernel(h_ref, c_ref, wgu_ref, wd_ref, *rest):
    *sums, out_ref, dh_ref, ggu_ref, gd_ref, sgu, sd, at_ref, a_ref, dgu_ref = rest
    step = pl.program_id(0)

    @pl.when(step == 0)
    def _():
        if sums:
            sgu[...] = sums[0][...]
            sd[...] = sums[1][...]
        else:
            sgu[...] = jnp.zeros_like(sgu)
            sd[...] = jnp.zeros_like(sd)

    hidden, width = wd_ref.shape
    tile = min(hidden, 2 * LANES)

    def first(k, carry):
        at = pl.multiple_of(k * tile, tile)
        over = pl.multiple_of(hidden + k * tile, tile)
        gate = nn(h_ref[...], wgu_ref[:, pl.ds(at, tile)])
        upward = nn(h_ref[...], wgu_ref[:, pl.ds(over, tile)])
        d_active = nt(c_ref[...], wd_ref[pl.ds(at, tile), :])
        sigmoid = jax.nn.sigmoid(gate)
        silu = gate * sigmoid
        active = (silu * upward).astype(BF16)
        a_ref[:, pl.ds(at, tile)] = active
        at_ref[pl.ds(at, tile), :] = active.T
        d_gate = d_active * upward * sigmoid * (1.0 + gate * (1.0 - sigmoid))
        dgu_ref[:, pl.ds(at, tile)] = d_gate.astype(BF16)
        dgu_ref[:, pl.ds(over, tile)] = (d_active * silu).astype(BF16)
        return carry

    lax.fori_loop(0, hidden // tile, first, 0)
    wtile = 2 * LANES

    def second(k, carry):
        at = pl.ds(pl.multiple_of(k * wtile, wtile), wtile)
        out_ref[:, at] = nn(a_ref[...], wd_ref[:, at]).astype(BF16)
        dh_ref[:, at] = nt(dgu_ref[...], wgu_ref[at, :]).astype(BF16)
        sgu[at, :] += tn(h_ref[:, at], dgu_ref[...])
        sd[:, at] += nn(at_ref[...], c_ref[:, at])
        return carry

    lax.fori_loop(0, width // wtile, second, 0)

    @pl.when(step == pl.num_programs(0) - 1)
    def _():
        ggu_ref[...] = sgu[...].astype(ggu_ref.dtype)
        gd_ref[...] = sd[...].astype(gd_ref.dtype)


def mlp_both(h, c, wgu, wd, rows, sums, kind):
    total, width = h.shape
    hidden = wd.shape[0]
    return pl.pallas_call(
        mlp_kernel,
        grid=(total // rows,),
        in_specs=[rows_of(rows, h), rows_of(rows, c), whole(wgu), whole(wd)] + [whole(s) for s in sums],
        out_specs=[rows_of(rows, h), rows_of(rows, c), whole(wgu), whole(wd)],
        out_shape=[
            jax.ShapeDtypeStruct(h.shape, BF16),
            jax.ShapeDtypeStruct(h.shape, BF16),
            jax.ShapeDtypeStruct(wgu.shape, kind),
            jax.ShapeDtypeStruct(wd.shape, kind),
        ],
        scratch_shapes=[
            pltpu.VMEM(wgu.shape, F32),
            pltpu.VMEM(wd.shape, F32),
            pltpu.VMEM((hidden, rows), BF16),
            pltpu.VMEM((rows, hidden), BF16),
            pltpu.VMEM((rows, 2 * hidden), BF16),
        ],
        compiler_params=params(),
        cost_estimate=pl.CostEstimate(
            flops=18 * total * width * hidden,
            bytes_accessed=total * width * 8 + width * hidden * 18,
            transcendentals=total * hidden,
        ),
        name="mlp_both",
    )(h, c, wgu, wd, *sums)


def attn_backward_kernel(queries, keys, x_ref, dm_ref, qkv_ref, o_ref, gain_ref, w_ref, wo_ref, cos_ref, sin_ref, *rest):
    *sums, dh_ref, gw_ref, go_ref, gg_ref, sw, so, sg, h_ref, ot_ref, dqkv_ref = rest
    step = pl.program_id(0)

    @pl.when(step == 0)
    def _():
        if sums:
            sw[...] = sums[0][...]
            so[...] = sums[1][...]
            sg[...] = sums[2][...]
        else:
            sw[...] = jnp.zeros_like(sw)
            so[...] = jnp.zeros_like(so)
            sg[...] = jnp.zeros_like(sg)

    x = x_ref[...].astype(F32)
    inverse = lax.rsqrt(jnp.mean(x * x, -1, keepdims=True) + NORM_EPS)
    h_ref[...] = (x * inverse * gain_ref[...]).astype(BF16)
    ot_ref[...] = o_ref[...].T
    d_heads = nt(dm_ref[...], wo_ref[...]).astype(BF16)
    cosine, sine = cos_ref[...], sin_ref[...]
    each = queries // keys
    for at in range(keys):
        key = qkv_ref[:, head_span(queries + at)]
        value = qkv_ref[:, head_span(queries + keys + at)]
        d_key, d_value = 0.0, 0.0
        for k in range(at * each, (at + 1) * each):
            query = qkv_ref[:, head_span(k)]
            d_head = d_heads[:, head_span(k)]
            probs = head_probs(query, key)
            d_value += tn(probs.astype(BF16), d_head)
            d_probs = nt(d_head, value)
            delta = jnp.sum(probs * d_probs, -1, keepdims=True)
            d_scores = (probs * (d_probs - delta) * HEAD_DIM ** (-0.5)).astype(BF16)
            d_query = nn(d_scores, key)
            d_key += tn(d_scores, query)
            dqkv_ref[:, head_span(k)] = turn_back(d_query, cosine, sine).astype(BF16)
        dqkv_ref[:, head_span(queries + at)] = turn_back(d_key, cosine, sine).astype(BF16)
        dqkv_ref[:, head_span(queries + keys + at)] = d_value.astype(BF16)

    wtile = 2 * LANES

    def second(k, carry):
        at = pl.ds(pl.multiple_of(k * wtile, wtile), wtile)
        d_normed = nt(dqkv_ref[...], w_ref[at, :])
        dh_ref[:, at] = d_normed.astype(BF16)
        sg[:, at] += jnp.sum(d_normed * (x_ref[:, at].astype(F32) * inverse), 0, keepdims=True)
        sw[at, :] += tn(h_ref[:, at], dqkv_ref[...])
        so[:, at] += nn(ot_ref[...], dm_ref[:, at])
        return carry

    lax.fori_loop(0, x_ref.shape[1] // wtile, second, 0)

    @pl.when(step == pl.num_programs(0) - 1)
    def _():
        gw_ref[...] = sw[...].astype(gw_ref.dtype)
        go_ref[...] = so[...].astype(go_ref.dtype)
        gg_ref[...] = sg[...]


def attn_backward(x, dm, qkv, o, gain, w, wo, tables, length, queries, keys, sums, kind):
    rows, width = x.shape
    wide = w.shape[1]
    return pl.pallas_call(
        functools.partial(attn_backward_kernel, queries, keys),
        grid=(rows // length,),
        in_specs=[rows_of(length, x), rows_of(length, dm), rows_of(length, qkv), rows_of(length, o)]
        + [whole(y) for y in (gain, w, wo, tables[0], tables[1], *sums)],
        out_specs=[rows_of(length, x), whole(w), whole(wo), whole(gain)],
        out_shape=[
            jax.ShapeDtypeStruct(x.shape, BF16),
            jax.ShapeDtypeStruct(w.shape, kind),
            jax.ShapeDtypeStruct(wo.shape, kind),
            jax.ShapeDtypeStruct(gain.shape, F32),
        ],
        scratch_shapes=[
            pltpu.VMEM(w.shape, F32),
            pltpu.VMEM(wo.shape, F32),
            pltpu.VMEM(gain.shape, F32),
            pltpu.VMEM((length, width), BF16),
            pltpu.VMEM((queries * LANES, length), BF16),
            pltpu.VMEM((length, wide), BF16),
        ],
        compiler_params=params(),
        cost_estimate=pl.CostEstimate(
            flops=4 * rows * width * (wide + queries * LANES) + 10 * rows * length * queries * LANES,
            bytes_accessed=rows * width * 6 + width * wide * 4,
            transcendentals=rows * length * queries,
        ),
        name="attn_backward",
    )(x, dm, qkv, o, gain, w, wo, tables[0], tables[1], *sums)


def spread_kernel(at_ref, gate_ref, up_ref, down_ref, gate_out, up_out, down_out):
    gate_out[...] = gate_ref[0].astype(F32)
    up_out[...] = up_ref[0].astype(F32)
    down_out[...] = down_ref[0].astype(F32)


def spread(at, gate_up, down, parts):
    count, width, wide = gate_up.shape
    tile = wide // 2 // parts
    short = down.shape[1] // parts
    spec = pltpu.PrefetchScalarGridSpec(
        num_scalar_prefetch=1,
        grid=(count, parts),
        in_specs=[
            pl.BlockSpec((1, width, tile), lambda a, s, at: (a ^ at[0], 0, s)),
            pl.BlockSpec((1, width, tile), lambda a, s, at: (a ^ at[0], 0, parts + s)),
            pl.BlockSpec((1, short, down.shape[2]), lambda a, s, at: (a ^ at[0], s, 0)),
        ],
        out_specs=[
            pl.BlockSpec((width, tile), lambda a, s, at: (0, s * count + a)),
            pl.BlockSpec((width, tile), lambda a, s, at: (0, s * count + a)),
            pl.BlockSpec((short, down.shape[2]), lambda a, s, at: (a * parts + s, 0)),
        ],
    )
    return pl.pallas_call(
        spread_kernel,
        grid_spec=spec,
        out_shape=[
            jax.ShapeDtypeStruct((width, count * wide // 2), F32),
            jax.ShapeDtypeStruct((width, count * wide // 2), F32),
            jax.ShapeDtypeStruct((count * down.shape[1], down.shape[2]), F32),
        ],
        compiler_params=pltpu.CompilerParams(dimension_semantics=("arbitrary", "arbitrary")),
        cost_estimate=pl.CostEstimate(
            flops=0, bytes_accessed=6 * (gate_up.size + down.size), transcendentals=0
        ),
        name="spread",
    )(at, gate_up, gate_up, down)


def norm_backward(rows, inverse_rms, norm_gain, d_normed):
    scaled = d_normed * norm_gain
    return inverse_rms * scaled - rows * inverse_rms**3 * jnp.mean(scaled * rows, -1, keepdims=True)


def pad_turned(block, heads):
    half = HEAD_DIM // 2
    split = block.reshape(block.shape[0], heads, 2, half)
    split = jnp.pad(split, ((0, 0), (0, 0), (0, 0), (0, LANES // 2 - half)))
    return split.reshape(block.shape[0], heads * LANES)


def unpad_turned(block, heads):
    half = HEAD_DIM // 2
    split = block.reshape(*block.shape[:-1], heads, 2, LANES // 2)[..., :half]
    return split.reshape(*block.shape[:-1], heads * HEAD_DIM)


def pad_plain(block, heads):
    split = block.reshape(block.shape[0], heads, HEAD_DIM)
    split = jnp.pad(split, ((0, 0), (0, 0), (0, LANES - HEAD_DIM)))
    return split.reshape(block.shape[0], heads * LANES)


def unpad_plain(block, heads):
    split = block.reshape(*block.shape[:-1], heads, LANES)[..., :HEAD_DIM]
    return split.reshape(*block.shape[:-1], heads * HEAD_DIM)


def gather_shard(x):
    return lax.all_gather(x, "shard", axis=0, tiled=True)


def scatter_shard(x):
    return lax.psum_scatter(x, "shard", scatter_dimension=0, tiled=True)


def on_device(
    tokens, cotangent, attn_gain, w_query, w_key, w_value, w_out, mlp_gain, w_gate, w_up, w_down
):
    replicas, shards = lax.axis_size("replica"), lax.axis_size("shard")
    length, width = tokens.shape
    slab = w_query.shape[0]
    kv_heads = w_key.shape[1] // HEAD_DIM
    group = math.gcd(replicas, kv_heads)
    keys = kv_heads // group
    queries = w_query.shape[1] // HEAD_DIM // group
    high = [1 << k for k in range(1, group.bit_length() - 1)]
    distances = [j ^ 1 for j in high_order(high)] + high_order(high)
    place = lax.axis_index("replica") % group
    hidden = w_down.shape[0] // group

    x_odd, x_even = plane_gather(tokens, high)
    c_odd, c_even = plane_gather(cotangent, high)

    wq = lax.dynamic_slice_in_dim(w_query, place * queries * HEAD_DIM, queries * HEAD_DIM, 1)
    wk = lax.dynamic_slice_in_dim(w_key, place * keys * HEAD_DIM, keys * HEAD_DIM, 1)
    wv = lax.dynamic_slice_in_dim(w_value, place * keys * HEAD_DIM, keys * HEAD_DIM, 1)
    wqkv = jnp.concatenate([pad_turned(wq, queries), pad_turned(wk, keys), pad_plain(wv, keys)], 1)
    wide = wqkv.shape[1]
    spare = 16
    gain_rows = -(-slab // wide)
    gains = jnp.stack([attn_gain, mlp_gain])
    gains = jnp.pad(gains, ((0, 0), (0, gain_rows * wide - slab))).reshape(2 * gain_rows, wide)
    gains = jnp.pad(gains, ((0, spare - 2 * gain_rows), (0, 0)))
    both = gather_shard(jnp.concatenate([wqkv, gains], 0)).reshape(shards, slab + spare, wide)
    wqkv = both[:, :slab].reshape(width, wide)
    gains = both[:, slab : slab + 2 * gain_rows].reshape(shards, 2, gain_rows * wide)[:, :, :slab]
    gains = jnp.moveaxis(gains, 1, 0).reshape(2, 1, width).astype(F32)
    gain_a, gain_m = gains[0], gains[1]

    turns = group // shards
    chunk = w_out.shape[0] // group
    forth = []
    for i in range(replicas):
        base, q = i - i % group, i % group
        for z in range(shards):
            forth.append((i * shards + z, (base + z * turns + q // shards) * shards + q % shards))
    back = [(b, a) for a, b in forth]
    wo = lax.dynamic_slice_in_dim(w_out, place * chunk, chunk, 0)
    wo = gather_shard(lax.ppermute(wo, ("replica", "shard"), forth))
    wo = pad_plain(wo.T, queries).T

    tile = hidden
    wgu = jnp.concatenate(
        [
            lax.dynamic_slice_in_dim(w, s * group * tile + place * tile, tile, 1)
            for w in (w_gate, w_up)
            for s in range(shards)
        ],
        1,
    )
    wgu = gather_shard(wgu)
    wd = gather_shard(lax.dynamic_slice_in_dim(w_down, place * hidden, hidden, 0))

    tables = rope_tables(length)
    forward = functools.partial(
        attn_forward, gain=gain_a, w=wqkv, wo=wo, tables=tables, length=length, queries=queries, keys=keys
    )
    part_odd, qkv_odd, o_odd = forward(x_odd)
    part_even, qkv_even, o_even = forward(x_even)
    rows = tokens.astype(F32)
    middle = rows + plane_scatter(part_odd, part_even, high, length)
    inverse_m = lax.rsqrt(jnp.mean(middle * middle, -1, keepdims=True) + NORM_EPS)
    h_odd, h_even = plane_gather((middle * inverse_m * gain_m).astype(BF16), high)

    step_rows = 2 * length
    out_odd, dh_odd, sum_gu, sum_d = mlp_both(h_odd, c_odd, wgu, wd, step_rows, (), F32)
    out_even, dh_even, g_gu, g_d = mlp_both(h_even, c_even, wgu, wd, step_rows, (sum_gu, sum_d), BF16)
    d_normed = plane_scatter(dh_odd, dh_even, high, length)
    d_middle = cotangent.astype(F32) + norm_backward(middle, inverse_m, gain_m, d_normed)
    gain_m_term = jnp.sum(d_normed * middle * inverse_m, 0, keepdims=True)
    dm_odd, dm_even = plane_gather(d_middle.astype(BF16), high)
    block_output = (middle + plane_scatter(out_odd, out_even, high, length)).astype(BF16)

    backward = functools.partial(
        attn_backward, gain=gain_a, w=wqkv, wo=wo, tables=tables, length=length, queries=queries, keys=keys
    )
    da_odd, sum_w, sum_o, sum_g = backward(x_odd, dm_odd, qkv_odd, o_odd, sums=(), kind=F32)
    da_even, g_w, g_o, gain_a_term = backward(
        x_even, dm_even, qkv_even, o_even, sums=(sum_w, sum_o, sum_g), kind=BF16
    )
    d_normed = plane_scatter(da_odd, da_even, high, length)
    inverse_a = lax.rsqrt(jnp.mean(rows * rows, -1, keepdims=True) + NORM_EPS)
    input_grad = d_middle + norm_backward(rows, inverse_a, gain_a, d_normed)

    terms = jnp.concatenate([gain_a_term, gain_m_term], 0).reshape(2, shards, slab)
    upper = terms.astype(BF16)
    lower = (terms - upper.astype(F32)).astype(BF16)
    terms = jnp.moveaxis(jnp.concatenate([upper, lower], 0), 1, 0)
    terms = jnp.pad(terms, ((0, 0), (0, 0), (0, gain_rows * wide - slab)))
    terms = terms.reshape(shards, 4 * gain_rows, wide)
    terms = jnp.pad(terms, ((0, 0), (0, spare - 4 * gain_rows), (0, 0)))
    g_w = jnp.concatenate([g_w.reshape(shards, slab, wide), terms], 1)
    g_gu, g_d = scatter_shard(g_gu), scatter_shard(g_d)
    g_w = scatter_shard(g_w.reshape(shards * (slab + spare), wide))
    g_o = scatter_shard(unpad_plain(g_o.T, queries).T)
    g_o = lax.ppermute(g_o, ("replica", "shard"), back)
    bit = group
    while bit < replicas:
        g_gu, g_d, g_w, g_o = (g + swap(g, bit) for g in (g_gu, g_d, g_w, g_o))
        bit *= 2

    order = [distances.index(j) for j in range(group)]

    def stacked(g):
        odd, even = plane_gather(g, high)
        blocks = jnp.concatenate([odd, even], 0).reshape(group, *g.shape)
        return jnp.stack([blocks[k] for k in order])

    gate_grad, up_grad, down_grad = spread(place.reshape(1), stacked(g_gu), stacked(g_d), shards)
    absolute = jnp.arange(group) ^ place
    all_w = stacked(g_w)[absolute].astype(F32)
    all_o = stacked(g_o)[absolute].astype(F32)
    out_grad = all_o.reshape(group * chunk, width)
    qkv = jnp.moveaxis(all_w[:, :slab], 0, 1)
    cuts = (queries * LANES, (queries + keys) * LANES)
    query_grad = unpad_turned(qkv[..., : cuts[0]], queries).reshape(slab, -1)
    key_grad = unpad_turned(qkv[..., cuts[0] : cuts[1]], keys).reshape(slab, -1)
    value_grad = unpad_plain(qkv[..., cuts[1] :], keys).reshape(slab, -1)
    terms = jnp.sum(all_w[:, slab : slab + 4 * gain_rows], 0).reshape(2, 2, gain_rows * wide)
    terms = jnp.sum(terms, 0)[:, :slab]
    return (
        block_output,
        input_grad,
        terms[0],
        query_grad,
        key_grad,
        value_grad,
        out_grad,
        terms[1],
        gate_grad,
        up_grad,
        down_grad,
    )


def solution(mesh):
    tokens, weights, gains = P(("replica", "shard"), None), P("shard", None), P("shard")
    return jax.shard_map(
        on_device,
        mesh=mesh,
        in_specs=(tokens, tokens, gains, weights, weights, weights, weights, gains, weights, weights, weights),
        out_specs=(tokens, tokens, gains, weights, weights, weights, weights, gains, weights, weights, weights),
        check_vma=False,
    )
```

```python
import functools
import math

import jax
import jax.numpy as jnp
from jax import lax
from jax.experimental import pallas as pl
from jax.experimental.pallas import tpu as pltpu
from jax.sharding import PartitionSpec as P

HEAD_DIM = 96
LANES = 128
NORM_EPS = 1e-05
ROPE_BASE = 100000.0
VMEM_BYTES = 40 * 1024 * 1024
F32 = jnp.float32
BF16 = jnp.bfloat16


def nn(left, right):
    return jnp.dot(left, right, preferred_element_type=F32)


def nt(left, right):
    return lax.dot_general(left, right, (((1,), (1,)), ((), ())), preferred_element_type=F32)


def tn(left, right):
    return lax.dot_general(left, right, (((0,), (0,)), ((), ())), preferred_element_type=F32)


def swap(x, bit):
    size = lax.axis_size("replica")
    return lax.ppermute(x, "replica", [(i, i ^ bit) for i in range(size)])


def plane_gather(x, high):
    cut = x.shape[0] // 2
    got = {0: (x,)}
    if len(high) == 2:
        a, b = high
        from_a, from_b = swap(x, a), swap(x, b)
        got[a], got[b] = (from_a,), (from_b,)
        got[1] = (swap(x, 1),)
        got[a ^ b] = (swap(from_b[:cut], a), swap(from_a[cut:], b))
    else:
        for bit in high:
            got.update({j ^ bit: tuple(swap(p, bit) for p in got[j]) for j in list(got)})
    for j in list(got):
        if j ^ 1 not in got:
            got[j ^ 1] = tuple(swap(p, 1) for p in got[j])
    return got


def plane_scatter(parts, high):
    cut = parts[0].shape[0] // 2
    even = [j for j in parts if j % 2 == 0]
    both = {j: (parts[j], swap(parts[j ^ 1], 1)) for j in even}

    def total(terms, rows):
        return sum(t[rows].astype(F32) for t in terms).astype(BF16)

    low, top, full = slice(0, cut), slice(cut, 2 * cut), slice(0, 2 * cut)
    if len(high) == 2:
        a, b = high
        far, near_a, near_b = both[a ^ b], both[a], both[b]
        via_a, via_b = swap(total(far, low), a), swap(total(far, top), b)
        first_a, first_b = swap(total(near_a, low), a), swap(total(near_b, top), b)
        last_a = swap((total32(near_a, top) + via_b.astype(F32)).astype(BF16), a)
        last_b = swap((total32(near_b, low) + via_a.astype(F32)).astype(BF16), b)
        return both[0], (first_a, last_b), (last_a, first_b)
    sums = {j: total(both[j], full) for j in even}
    for bit in reversed(high):
        sums = {
            j: total((sums[j], swap(sums[j ^ bit], bit)), full) for j in sums if not j & bit
        }
    return (sums[0],), (), ()


def total32(terms, rows):
    return sum(t[rows].astype(F32) for t in terms)


def flat(terms):
    return [y for group in terms for y in group]


def call(kernel, name, inputs, outputs, scratch=(), flops=0, exps=0):
    outputs = [jax.ShapeDtypeStruct(shape, kind) for shape, kind in outputs]
    moved = sum(math.prod(y.shape) * y.dtype.itemsize for y in [*inputs, *outputs])
    return pl.pallas_call(
        kernel,
        out_shape=outputs,
        scratch_shapes=list(scratch),
        compiler_params=pltpu.CompilerParams(vmem_limit_bytes=VMEM_BYTES),
        cost_estimate=pl.CostEstimate(flops=flops, bytes_accessed=moved, transcendentals=exps),
        name=name,
    )(*inputs)


def rope_tables(length):
    half = HEAD_DIM // 2
    position = jnp.arange(length, dtype=F32)
    freqs = jnp.power(ROPE_BASE, -jnp.arange(half, dtype=F32) / half)
    angles = position[:, None] * freqs[None, :]
    pad = ((0, 0), (0, LANES // 2 - half))
    cosine, sine = jnp.pad(jnp.cos(angles), pad), jnp.pad(jnp.sin(angles), pad)
    return jnp.concatenate([cosine, cosine], 1), jnp.concatenate([-sine, sine], 1)


def turn(values, cosine, sine):
    return values * cosine + pltpu.roll(values, LANES // 2, 1) * sine


def turn_back(values, cosine, sine):
    return values * cosine - pltpu.roll(values, LANES // 2, 1) * sine


def head_probs(query, key):
    length = query.shape[0]
    scores = nt(query, key) * HEAD_DIM ** (-0.5)
    rows = lax.broadcasted_iota(jnp.int32, (length, length), 0)
    columns = lax.broadcasted_iota(jnp.int32, (length, length), 1)
    scores = jnp.where(rows >= columns, scores, -jnp.inf)
    raised = jnp.exp(scores - jnp.max(scores, -1, keepdims=True))
    return raised / jnp.sum(raised, -1, keepdims=True)


def head_span(k):
    return slice(k * LANES, (k + 1) * LANES)


def load(refs):
    parts = [r[...] for r in refs]
    return parts[0] if len(parts) == 1 else jnp.concatenate(parts, 0)


def take(refs, counts):
    refs, out = list(refs), []
    for count in counts:
        out.append(refs[:count])
        refs = refs[count:]
    return out, refs


def inverse_rms(rows):
    return lax.rsqrt(jnp.mean(rows * rows, -1, keepdims=True) + NORM_EPS)


def attn_forward_kernel(queries, keys, counts, *refs):
    blocks, rest = take(refs, counts)
    gain_ref, w_ref, wo_ref, pick_ref, cos_ref, sin_ref = rest[:6]
    parts, (h_ref, qkv_ref, o_ref) = rest[6 : 6 + len(blocks)], rest[6 + len(blocks) :]
    cosine, sine = cos_ref[...], sin_ref[...]
    length = cosine.shape[0]
    for n, block in enumerate(blocks):
        at_rows = slice(n * length, (n + 1) * length)
        x = load(block).astype(F32)
        normed = (x * inverse_rms(x) * gain_ref[...]).astype(BF16)
        h_ref[at_rows, :] = normed
        mixed = nn(normed, w_ref[...])
        made = []
        for k in range(queries + 2 * keys):
            piece = mixed[:, head_span(k)]
            made.append((turn(piece, cosine, sine) if k < queries + keys else piece).astype(BF16))
            qkv_ref[at_rows, head_span(k)] = made[k]
        heads = []
        for k in range(queries):
            at = k * keys // queries
            probs = head_probs(made[k], made[queries + at])
            heads.append(nn(probs.astype(BF16), made[queries + keys + at]).astype(BF16))
        heads = nn(jnp.concatenate(heads, 1), pick_ref[...]).astype(BF16)
        o_ref[at_rows, :] = heads
        parts[n][...] = nn(heads, wo_ref[...]).astype(BF16)


def attn_forward(blocks, gain, w, wo, pick, tables, queries, keys):
    counts = [len(b) for b in blocks]
    length, width = tables[0].shape[0], w.shape[0]
    rows = length * len(blocks)
    *parts, h, qkv, o = call(
        functools.partial(attn_forward_kernel, queries, keys, counts),
        "attn_forward",
        [*flat(blocks), gain, w, wo, pick, *tables],
        [((length, width), BF16)] * len(blocks)
        + [((rows, width), BF16), ((rows, w.shape[1]), BF16), ((rows, wo.shape[0]), BF16)],
        flops=2 * rows * width * (w.shape[1] + wo.shape[0]) + 4 * rows * length * queries * LANES,
        exps=rows * length * queries,
    )
    return parts, (h, qkv, o)


def mlp_kernel(counts, *refs):
    blocks, rest = take(refs, counts)
    half = len(blocks) // 2
    wgu_ref, wd_ref = rest[:2]
    outs, dhs = rest[2 : 2 + half], rest[2 + half : 2 + 2 * half]
    dgu_ref, at_ref, h_ref, c_ref, a_ref = rest[2 + 2 * half :]
    length = outs[0].shape[0]
    for n in range(half):
        h_ref[n * length : (n + 1) * length, :] = load(blocks[n])
        c_ref[n * length : (n + 1) * length, :] = load(blocks[half + n])
    hidden, width = wd_ref.shape
    tile = min(hidden, 2 * LANES)

    def first(k, carry):
        at = pl.multiple_of(k * tile, tile)
        over = pl.multiple_of(hidden + k * tile, tile)
        gate = nn(h_ref[...], wgu_ref[:, pl.ds(at, tile)])
        upward = nn(h_ref[...], wgu_ref[:, pl.ds(over, tile)])
        d_active = nt(c_ref[...], wd_ref[pl.ds(at, tile), :])
        sigmoid = jax.nn.sigmoid(gate)
        silu = gate * sigmoid
        active = (silu * upward).astype(BF16)
        a_ref[:, pl.ds(at, tile)] = active
        at_ref[pl.ds(at, tile), :] = active.T
        d_gate = d_active * upward * sigmoid * (1.0 + gate * (1.0 - sigmoid))
        dgu_ref[:, pl.ds(at, tile)] = d_gate.astype(BF16)
        dgu_ref[:, pl.ds(over, tile)] = (d_active * silu).astype(BF16)
        return carry

    lax.fori_loop(0, hidden // tile, first, 0)
    wtile = 2 * LANES

    def second(k, carry):
        at = pl.ds(pl.multiple_of(k * wtile, wtile), wtile)
        d_normed = nt(dgu_ref[...], wgu_ref[at, :]).astype(BF16)
        output = nn(a_ref[...], wd_ref[:, at]).astype(BF16)
        for n in range(half):
            dhs[n][:, at] = d_normed[n * length : (n + 1) * length]
            outs[n][:, at] = output[n * length : (n + 1) * length]
        return carry

    lax.fori_loop(0, width // wtile, second, 0)


def mlp_both(h, c, wgu, wd):
    counts = [len(b) for b in [*h, *c]]
    half = len(h)
    length, width, hidden = sum(p.shape[0] for p in h[0]), wgu.shape[0], wd.shape[0]
    rows = half * length
    made = call(
        functools.partial(mlp_kernel, counts),
        "mlp_both",
        [*flat(h), *flat(c), wgu, wd],
        [((length, width), BF16)] * (2 * half)
        + [((rows, 2 * hidden), BF16), ((hidden, rows), BF16)],
        scratch=[
            pltpu.VMEM((rows, width), BF16),
            pltpu.VMEM((rows, width), BF16),
            pltpu.VMEM((rows, hidden), BF16),
        ],
        flops=12 * rows * width * hidden,
        exps=rows * hidden,
    )
    return made[:half], made[half : 2 * half], made[2 * half], made[2 * half + 1]


def mlp_grads_kernel(pieces, pairs, *refs):
    hs, cs, dgus, ats = (refs[k : k + n] for k, n in zip(
        (0, pieces, 2 * pieces, 2 * pieces + pairs), (pieces, pieces, pairs, pairs)))
    ggu_ref, gd_ref, h_all, c_all, dgu_all, at_all = refs[2 * pieces + 2 * pairs :]

    @pl.when(pl.program_id(0) == 0)
    def _():
        at = 0
        for dgu, across in zip(dgus, ats):
            rows = dgu.shape[0]
            dgu_all[at : at + rows, :] = dgu[...]
            at_all[:, at : at + rows] = across[...]
            at += rows

    at = 0
    for h, c in zip(hs, cs):
        rows = h.shape[0]
        h_all[at : at + rows, :] = h[...]
        c_all[at : at + rows, :] = c[...]
        at += rows
    ggu_ref[...] = tn(h_all[...], dgu_all[...]).astype(BF16)
    gd_ref[...] = nn(at_all[...], c_all[...]).astype(BF16)


def mlp_grads(h, c, dgu, across):
    width, wide, hidden = h[0].shape[1], dgu[0].shape[1], across[0].shape[0]
    rows = sum(y.shape[0] for y in h)
    tile = 2 * LANES
    whole = lambda y: pl.BlockSpec(y.shape, lambda i: (0, 0), pipeline_mode=pl.Buffered(1))
    part = lambda y: pl.BlockSpec((y.shape[0], tile), lambda i: (0, i))
    return pl.pallas_call(
        functools.partial(mlp_grads_kernel, len(h), len(dgu)),
        grid=(width // tile,),
        in_specs=[part(y) for y in [*h, *c]] + [whole(y) for y in [*dgu, *across]],
        out_specs=[
            pl.BlockSpec((tile, wide), lambda i: (i, 0)),
            pl.BlockSpec((hidden, tile), lambda i: (0, i)),
        ],
        out_shape=[
            jax.ShapeDtypeStruct((width, wide), BF16),
            jax.ShapeDtypeStruct((hidden, width), BF16),
        ],
        scratch_shapes=[
            pltpu.VMEM((rows, tile), BF16),
            pltpu.VMEM((rows, tile), BF16),
            pltpu.VMEM((rows, wide), BF16),
            pltpu.VMEM((hidden, rows), BF16),
        ],
        compiler_params=pltpu.CompilerParams(
            dimension_semantics=("arbitrary",), vmem_limit_bytes=VMEM_BYTES
        ),
        cost_estimate=pl.CostEstimate(
            flops=6 * rows * width * hidden,
            bytes_accessed=4 * rows * width + 4 * rows * wide + 3 * width * wide,
            transcendentals=0,
        ),
        name="mlp_grads",
    )(*h, *c, *dgu, *across)


def attn_backward_kernel(queries, keys, counts, *refs):
    blocks, rest = take(refs, counts)
    qkv_ref, w_ref, wo_ref, pick_ref, cos_ref, sin_ref = rest[:6]
    dhs, (dqkv_ref,) = rest[6 : 6 + len(blocks)], rest[6 + len(blocks) :]
    cosine, sine = cos_ref[...], sin_ref[...]
    length = cosine.shape[0]
    each = queries // keys
    scale = HEAD_DIM ** (-0.5)
    for n, block in enumerate(blocks):
        at_rows = slice(n * length, (n + 1) * length)
        d_heads = nt(load(block), wo_ref[...]).astype(BF16)
        d_heads = nt(d_heads, pick_ref[...]).astype(BF16)
        for at in range(keys):
            key = qkv_ref[at_rows, head_span(queries + at)]
            value = qkv_ref[at_rows, head_span(queries + keys + at)]
            d_key, d_value = 0.0, 0.0
            for k in range(at * each, (at + 1) * each):
                query = qkv_ref[at_rows, head_span(k)]
                d_head = d_heads[:, head_span(k)]
                probs = head_probs(query, key)
                d_value += tn(probs.astype(BF16), d_head)
                d_probs = nt(d_head, value)
                delta = jnp.sum(probs * d_probs, -1, keepdims=True)
                d_scores = (probs * (d_probs - delta) * scale).astype(BF16)
                d_query = nn(d_scores, key)
                d_key += tn(d_scores, query)
                dqkv_ref[at_rows, head_span(k)] = turn_back(d_query, cosine, sine).astype(BF16)
            dqkv_ref[at_rows, head_span(queries + at)] = turn_back(d_key, cosine, sine).astype(BF16)
            dqkv_ref[at_rows, head_span(queries + keys + at)] = d_value.astype(BF16)
    wtile = 2 * LANES

    def second(k, carry):
        at = pl.ds(pl.multiple_of(k * wtile, wtile), wtile)
        d_normed = nt(dqkv_ref[...], w_ref[at, :]).astype(BF16)
        for n in range(len(blocks)):
            dhs[n][:, at] = d_normed[n * length : (n + 1) * length]
        return carry

    lax.fori_loop(0, w_ref.shape[0] // wtile, second, 0)


def attn_backward(blocks, qkv, w, wo, pick, tables, queries, keys):
    counts = [len(b) for b in blocks]
    length, width = tables[0].shape[0], w.shape[0]
    rows = length * len(blocks)
    *dhs, dqkv = call(
        functools.partial(attn_backward_kernel, queries, keys, counts),
        "attn_backward",
        [*flat(blocks), qkv, w, wo, pick, *tables],
        [((length, width), BF16)] * len(blocks) + [((rows, w.shape[1]), BF16)],
        flops=2 * rows * width * (w.shape[1] + wo.shape[0]) + 10 * rows * length * queries * LANES,
        exps=rows * length * queries,
    )
    return dhs, dqkv


def attn_grads_kernel(count, *refs):
    hs, ds, pick_ref = refs[:count], refs[count : 2 * count], refs[2 * count]
    g_ref, h_all, d_all = refs[2 * count + 1 :]

    @pl.when(pl.program_id(0) == 0)
    def _():
        at = 0
        for d in ds:
            d_all[at : at + d.shape[0], :] = d[...]
            at += d.shape[0]

    at = 0
    for h in hs:
        h_all[at : at + h.shape[0], :] = h[...]
        at += h.shape[0]
    grad = tn(h_all[...], d_all[...]).astype(BF16)
    g_ref[...] = nt(grad, pick_ref[...]).astype(BF16)


def out_grads_kernel(count, pieces, *refs):
    os, ms = refs[:count], refs[count : count + pieces]
    g_ref, o_all, m_all = refs[count + pieces :]

    @pl.when(pl.program_id(0) == 0)
    def _():
        at = 0
        for o in os:
            o_all[at : at + o.shape[0], :] = o[...]
            at += o.shape[0]

    at = 0
    for m in ms:
        m_all[at : at + m.shape[0], :] = m[...]
        at += m.shape[0]
    g_ref[...] = tn(o_all[...], m_all[...]).astype(BF16)


def grads_call(kernel, name, tiled, fixed, consts, out, along, flops):
    tile = 2 * LANES
    rows, width = sum(y.shape[0] for y in tiled), tiled[0].shape[1]
    whole = lambda y: pl.BlockSpec(y.shape, lambda i: (0, 0), pipeline_mode=pl.Buffered(1))
    part = lambda y: pl.BlockSpec((y.shape[0], tile), lambda i: (0, i))
    if along == 0:
        inputs, specs = [*tiled, *fixed, *consts], [part(y) for y in tiled] + [whole(y) for y in [*fixed, *consts]]
        out_spec = pl.BlockSpec((tile, out[1]), lambda i: (i, 0))
        scratch = [pltpu.VMEM((rows, tile), BF16), pltpu.VMEM((rows, fixed[0].shape[1]), BF16)]
    else:
        inputs, specs = [*fixed, *tiled], [whole(y) for y in fixed] + [part(y) for y in tiled]
        out_spec = pl.BlockSpec((out[0], tile), lambda i: (0, i))
        scratch = [pltpu.VMEM((rows, fixed[0].shape[1]), BF16), pltpu.VMEM((rows, tile), BF16)]
    return pl.pallas_call(
        kernel,
        grid=(width // tile,),
        in_specs=specs,
        out_specs=out_spec,
        out_shape=jax.ShapeDtypeStruct(out, BF16),
        scratch_shapes=scratch,
        compiler_params=pltpu.CompilerParams(
            dimension_semantics=("arbitrary",), vmem_limit_bytes=VMEM_BYTES
        ),
        cost_estimate=pl.CostEstimate(flops=flops, bytes_accessed=3 * rows * width, transcendentals=0),
        name=name,
    )(*inputs)


def finish_kernel(kind, counts, *refs):
    (whole, low, top), rest = take(refs, counts)
    length = whole[0].shape[0]
    cut = length // 2
    halves = []
    for half, extra in ((0, low), (1, top)):
        rows = slice(half * cut, (half + 1) * cut)
        total = sum(t[rows, :].astype(F32) for t in whole)
        halves.append(sum((t[...].astype(F32) for t in extra), total))
    total = jnp.concatenate(halves, 0)
    if kind == "middle":
        x_ref, gain_ref, middle_ref, h_ref = rest
        middle = x_ref[...].astype(F32) + total
        middle_ref[...] = middle
        h_ref[...] = (middle * inverse_rms(middle) * gain_ref[...]).astype(BF16)
    elif kind == "output":
        middle_ref, out_ref = rest
        out_ref[...] = (middle_ref[...] + total).astype(BF16)
    else:
        rows_ref, base_ref, gain_ref, *outs = rest
        rows = rows_ref[...].astype(F32)
        inverse = inverse_rms(rows)
        scaled = total * gain_ref[...]
        mean = jnp.mean(scaled * rows, -1, keepdims=True)
        made = base_ref[...].astype(F32) + inverse * scaled - rows * inverse**3 * mean
        for out in outs:
            out[...] = made.astype(out.dtype)


def finish(kind, terms, extras, kinds):
    counts = [len(t) for t in terms]
    shape = terms[0][0].shape
    return call(
        functools.partial(finish_kernel, kind, counts),
        "finish_" + kind,
        [*flat(terms), *extras],
        [(shape, k) for k in kinds],
        flops=16 * math.prod(shape),
    )


def spread_kernel(at_ref, gate_ref, up_ref, down_ref, wg_ref, wu_ref, gate_out, up_out, down_out, gain_out):
    gate, upward = gate_ref[0].astype(F32), up_ref[0].astype(F32)
    gate_out[...] = gate
    up_out[...] = upward
    down_out[...] = down_ref[0].astype(F32)

    @pl.when((pl.program_id(0) == 0) & (pl.program_id(1) == 0))
    def _():
        gain_out[...] = jnp.zeros_like(gain_out)

    gain_out[...] += gate * wg_ref[...].astype(F32) + upward * wu_ref[...].astype(F32)


def spread(at, gate_up, down, w_gate, w_up, parts):
    count, width, wide = gate_up.shape
    tile = wide // 2 // parts
    short = down.shape[1] // parts
    columns = pl.BlockSpec((width, tile), lambda a, s, at: (0, s * count + a))
    spec = pltpu.PrefetchScalarGridSpec(
        num_scalar_prefetch=1,
        grid=(count, parts),
        in_specs=[
            pl.BlockSpec((1, width, tile), lambda a, s, at: (a ^ at[0], 0, s)),
            pl.BlockSpec((1, width, tile), lambda a, s, at: (a ^ at[0], 0, parts + s)),
            pl.BlockSpec((1, short, down.shape[2]), lambda a, s, at: (a ^ at[0], s, 0)),
            columns,
            columns,
        ],
        out_specs=[
            columns,
            columns,
            pl.BlockSpec((short, down.shape[2]), lambda a, s, at: (a * parts + s, 0)),
            pl.BlockSpec((width, tile), lambda a, s, at: (0, 0)),
        ],
    )
    return pl.pallas_call(
        spread_kernel,
        grid_spec=spec,
        out_shape=[
            jax.ShapeDtypeStruct((width, count * wide // 2), F32),
            jax.ShapeDtypeStruct((width, count * wide // 2), F32),
            jax.ShapeDtypeStruct((count * down.shape[1], down.shape[2]), F32),
            jax.ShapeDtypeStruct((width, tile), F32),
        ],
        compiler_params=pltpu.CompilerParams(dimension_semantics=("arbitrary", "arbitrary")),
        cost_estimate=pl.CostEstimate(
            flops=0, bytes_accessed=6 * (gate_up.size + down.size), transcendentals=0
        ),
        name="spread",
    )(at, gate_up, gate_up, down, w_gate, w_up)


def head_columns(queries, keys):
    half, lane = HEAD_DIM // 2, jnp.arange(LANES)
    place = lane % (LANES // 2)
    turned = jnp.where(place < half, (lane // (LANES // 2)) * half + place, -1)
    plain = jnp.where(lane < HEAD_DIM, lane, -1)
    columns = []
    for k in range(queries + 2 * keys):
        inside = turned if k < queries + keys else plain
        columns.append(jnp.where(inside >= 0, inside + k * HEAD_DIM, -1))
    return jnp.concatenate(columns)


def gather_shard(x):
    return lax.all_gather(x, "shard", axis=0, tiled=True)


def scatter_shard(x):
    return lax.psum_scatter(x, "shard", scatter_dimension=0, tiled=True)


def after(x, *others):
    return lax.optimization_barrier((x, *others))[0]


def on_device(
    tokens, cotangent, attn_gain, w_query, w_key, w_value, w_out, mlp_gain, w_gate, w_up, w_down
):
    replicas, shards = lax.axis_size("replica"), lax.axis_size("shard")
    length, width = tokens.shape
    slab = w_query.shape[0]
    kv_heads = w_key.shape[1] // HEAD_DIM
    group = math.gcd(replicas, kv_heads)
    keys = kv_heads // group
    queries = w_query.shape[1] // HEAD_DIM // group
    high = [1 << k for k in range(1, group.bit_length() - 1)]
    place = lax.axis_index("replica") % group
    hidden = w_down.shape[0] // group
    narrow = (queries + 2 * keys) * HEAD_DIM

    turns = group // shards
    chunk = w_out.shape[0] // group
    forth = []
    for i in range(replicas):
        base, q = i - i % group, i % group
        for z in range(shards):
            forth.append((i * shards + z, (base + z * turns + q // shards) * shards + q % shards))
    back = [(b, a) for a, b in forth]
    wo = lax.dynamic_slice_in_dim(w_out, place * chunk, chunk, 0)
    wo = lax.ppermute(wo, ("replica", "shard"), forth)

    x = plane_gather(tokens, high)

    wq = lax.dynamic_slice_in_dim(w_query, place * queries * HEAD_DIM, queries * HEAD_DIM, 1)
    wk = lax.dynamic_slice_in_dim(w_key, place * keys * HEAD_DIM, keys * HEAD_DIM, 1)
    wv = lax.dynamic_slice_in_dim(w_value, place * keys * HEAD_DIM, keys * HEAD_DIM, 1)
    spare = 16
    gain_rows = -(-slab // narrow)
    gains = jnp.stack([attn_gain, mlp_gain])
    gains = jnp.pad(gains, ((0, 0), (0, gain_rows * narrow - slab))).reshape(2 * gain_rows, narrow)
    gains = jnp.pad(gains, ((0, spare - 2 * gain_rows), (0, 0)))
    wo_rows = chunk * width // narrow
    sent = jnp.concatenate(
        [jnp.concatenate([wq, wk, wv], 1), gains, wo.reshape(wo_rows, narrow)], 0
    )
    both = gather_shard(sent).reshape(shards, slab + spare + wo_rows, narrow)
    columns = head_columns(queries, keys)
    pick = (jnp.arange(narrow)[:, None] == columns[None, :]).astype(BF16)
    wqkv = nn(both[:, :slab].reshape(width, narrow), pick).astype(BF16)
    gains = both[:, slab : slab + 2 * gain_rows].reshape(shards, 2, gain_rows * narrow)[:, :, :slab]
    gains = jnp.moveaxis(gains, 1, 0).reshape(2, 1, width).astype(F32)
    gain_a, gain_m = gains[0], gains[1]
    wo = both[:, slab + spare :].reshape(shards * chunk, width)
    lanes = jnp.arange(queries * LANES)
    heads = (lanes // LANES) * HEAD_DIM + lanes % LANES
    heads = jnp.where(lanes % LANES < HEAD_DIM, heads, -1)
    pick_o = (jnp.arange(queries * HEAD_DIM)[None, :] == heads[:, None]).astype(BF16)

    wgu = jnp.concatenate(
        [
            lax.dynamic_slice_in_dim(w, s * group * hidden + place * hidden, hidden, 1)
            for w in (w_gate, w_up)
            for s in range(shards)
        ],
        1,
    )
    wd = lax.dynamic_slice_in_dim(w_down, place * hidden, hidden, 0)
    wgu = gather_shard(after(wgu, sent))
    wd = gather_shard(after(wd, sent))

    c = plane_gather(after(cotangent, *x[high[-1]]), high)

    pairs = [j for j in sorted(x, reverse=True) if j % 2 == 0]
    tables = rope_tables(length)
    parts, saved = {}, {}
    for j in pairs:
        (parts[j ^ 1], parts[j]), saved[j] = attn_forward(
            [x[j ^ 1], x[j]], gain_a, wqkv, wo, pick_o, tables, queries, keys
        )
    middle, h_own = finish(
        "middle", plane_scatter(parts, high), [tokens, gain_m], [F32, BF16]
    )
    h = plane_gather(h_own, high)

    order = list(reversed(pairs))
    order = order[:-2] + [order[-1], order[-2]] if len(order) > 2 else order
    outs, dhs, dgus, acrosses = {}, {}, [], []
    for j in order:
        (outs[j ^ 1], outs[j]), (dhs[j ^ 1], dhs[j]), dgu, across = mlp_both(
            [h[j ^ 1], h[j]], [c[j ^ 1], c[j]], wgu, wd
        )
        dgus.append(dgu)
        acrosses.append(across)
    d_middle, dm_own = finish(
        "back", plane_scatter(dhs, high), [middle, cotangent, gain_m], [F32, BF16]
    )
    all_h = flat(h[k] for j in order for k in (j ^ 1, j))
    all_c = flat(c[k] for j in order for k in (j ^ 1, j))
    g_gu, g_d = mlp_grads(all_h, all_c, dgus, acrosses)
    g_gu, g_d = scatter_shard(g_gu), scatter_shard(g_d)
    dm = plane_gather(dm_own, high)

    g_o = grads_call(
        functools.partial(out_grads_kernel, len(pairs), len(flat(dm.values()))),
        "out_grads",
        flat(dm[k] for j in order for k in (j ^ 1, j)),
        [saved[j][2] for j in order],
        [],
        wo.shape,
        1,
        2 * group * length * width * wo.shape[0],
    )
    g_o = lax.ppermute(scatter_shard(g_o), ("replica", "shard"), back)

    das, dqkvs = {}, []
    for j in order:
        (das[j ^ 1], das[j]), dqkv = attn_backward(
            [dm[j ^ 1], dm[j]], saved[j][1], wqkv, wo, pick_o, tables, queries, keys
        )
        dqkvs.append(dqkv)
    g_w = grads_call(
        functools.partial(attn_grads_kernel, len(pairs)),
        "attn_grads",
        [saved[j][0] for j in order],
        dqkvs,
        [pick],
        (width, narrow),
        0,
        2 * group * length * width * pick.shape[1],
    )
    g_w = scatter_shard(g_w)
    (input_grad,) = finish("back", plane_scatter(das, high), [tokens, d_middle, gain_a], [F32])

    held = flat(dm.values())
    outs = dict(zip(outs, (after(y, *held) for y in outs.values())))
    (block_output,) = finish("output", plane_scatter(outs, high), [middle], [BF16])

    bit = group
    while bit < replicas:
        g_gu, g_d, g_w, g_o = (g + swap(g, bit) for g in (g_gu, g_d, g_w, g_o))
        bit *= 2

    def stacked(g):
        got = plane_gather(g, high)
        return jnp.concatenate(flat(got[j] for j in range(group)), 0).reshape(group, *g.shape)

    gate_grad, up_grad, down_grad, gain_terms = spread(
        place.reshape(1), stacked(g_gu), stacked(g_d), w_gate, w_up, shards
    )
    mlp_gain_grad = jnp.sum(gain_terms, 1) / mlp_gain.astype(F32)
    absolute = jnp.arange(group) ^ place
    out_grad = stacked(g_o)[absolute].astype(F32).reshape(group * chunk, width)
    qkv = jnp.moveaxis(stacked(g_w)[absolute], 0, 1).astype(F32)
    cuts = (queries * HEAD_DIM, (queries + keys) * HEAD_DIM)
    query_grad = qkv[..., : cuts[0]].reshape(slab, -1)
    key_grad = qkv[..., cuts[0] : cuts[1]].reshape(slab, -1)
    value_grad = qkv[..., cuts[1] :].reshape(slab, -1)
    attn_gain_grad = sum(
        jnp.sum(g * w.astype(F32), 1)
        for g, w in ((query_grad, w_query), (key_grad, w_key), (value_grad, w_value))
    ) / attn_gain.astype(F32)
    return (
        block_output,
        input_grad,
        attn_gain_grad,
        query_grad,
        key_grad,
        value_grad,
        out_grad,
        mlp_gain_grad,
        gate_grad,
        up_grad,
        down_grad,
    )


def solution(mesh):
    tokens, weights, gains = P(("replica", "shard"), None), P("shard", None), P("shard")
    return jax.shard_map(
        on_device,
        mesh=mesh,
        in_specs=(tokens, tokens, gains, weights, weights, weights, weights, gains, weights, weights, weights),
        out_specs=(tokens, tokens, gains, weights, weights, weights, weights, gains, weights, weights, weights),
        check_vma=False,
    )
```

```python
import functools
import math

import jax
import jax.numpy as jnp
from jax import lax
from jax.experimental import pallas as pl
from jax.experimental.pallas import tpu as pltpu
from jax.sharding import PartitionSpec as P


HEAD_DIM = 96
LANES = 128
NORM_EPS = 1e-05
ROPE_BASE = 100000.0
VMEM_BYTES = 60 * 1024 * 1024
MLP_VMEM_BYTES = 40 * 1024 * 1024
F32 = jnp.float32
BF16 = jnp.bfloat16


def nn(left, right):
    return jnp.dot(left, right, preferred_element_type=F32)


def nt(left, right):
    return lax.dot_general(left, right, (((1,), (1,)), ((), ())), preferred_element_type=F32)


def tn(left, right):
    return lax.dot_general(left, right, (((0,), (0,)), ((), ())), preferred_element_type=F32)


def swap(x, bit):
    size = lax.axis_size("replica")
    return lax.ppermute(x, "replica", [(i, i ^ bit) for i in range(size)])


def plane_gather(x, high):
    cut = x.shape[0] // 2
    got = {0: (x,)}
    if len(high) == 2:
        a, b = high
        from_a, from_b = swap(x, a), swap(x, b)
        got[a], got[b] = (from_a,), (from_b,)
        got[1] = (swap(x, 1),)
        far = swap(from_b[:cut], a), swap(from_a[cut:], b)
        got[a ^ b] = far
    else:
        for bit in high:
            more = {j ^ bit: tuple(swap(p, bit) for p in got[j]) for j in list(got)}
            got.update(more)
    for j in list(got):
        if j ^ 1 not in got:
            got[j ^ 1] = tuple(swap(p, 1) for p in got[j])
    return got


def plane_scatter(parts, high):
    cut = parts[0].shape[0] // 2
    even = [j for j in parts if j % 2 == 0]
    both = {j: (parts[j], swap(parts[j ^ 1], 1)) for j in even}

    def total(terms, rows):
        return sum(t[rows].astype(F32) for t in terms).astype(BF16)

    low, top, full = slice(0, cut), slice(cut, 2 * cut), slice(0, 2 * cut)
    if len(high) == 2:
        a, b = high
        far, near_a, near_b = both[a ^ b], both[a], both[b]
        via_a = swap(total(far, low), a)
        via_b = swap(total(far, top), b)
        first_a = swap(total(near_a, low), a)
        first_b = swap(total(near_b, top), b)
        last_a = (total32(near_a, top) + via_b.astype(F32)).astype(BF16)
        last_b = (total32(near_b, low) + via_a.astype(F32)).astype(BF16)
        last_a, last_b = swap(last_a, a), swap(last_b, b)
        return both[0], (first_a, last_b), (last_a, first_b)
    sums = {j: total(both[j], full) for j in even}
    for bit in reversed(high):
        sums = {j: total((sums[j], swap(sums[j ^ bit], bit)), full) for j in sums if not j & bit}
    return (sums[0],), (), ()


def total32(terms, rows):
    return sum(t[rows].astype(F32) for t in terms)


def flat(terms):
    return [y for group in terms for y in group]


def call(kernel, inputs, outputs, scratch=(), flops=0, exps=0, limit=VMEM_BYTES):
    outputs = [jax.ShapeDtypeStruct(shape, kind) for shape, kind in outputs]
    moved = sum(math.prod(y.shape) * y.dtype.itemsize for y in [*inputs, *outputs])
    return pl.pallas_call(
        kernel,
        out_shape=outputs,
        scratch_shapes=list(scratch),
        compiler_params=pltpu.CompilerParams(vmem_limit_bytes=limit),
        cost_estimate=pl.CostEstimate(flops=flops, bytes_accessed=moved, transcendentals=exps),
    )(*inputs)


def rope_tables(length):
    half = HEAD_DIM // 2
    position = jnp.arange(length, dtype=F32)
    freqs = jnp.power(ROPE_BASE, -jnp.arange(half, dtype=F32) / half)
    angles = position[:, None] * freqs[None, :]
    pad = ((0, 0), (0, LANES // 2 - half))
    cosine, sine = jnp.pad(jnp.cos(angles), pad), jnp.pad(jnp.sin(angles), pad)
    return jnp.concatenate([cosine, cosine], 1), jnp.concatenate([-sine, sine], 1)


def turn(values, cosine, sine):
    return values * cosine + pltpu.roll(values, LANES // 2, 1) * sine


def turn_back(values, cosine, sine):
    return values * cosine - pltpu.roll(values, LANES // 2, 1) * sine


def head_probs(query, key):
    length = query.shape[0]
    scores = nt(query, key) * HEAD_DIM ** (-0.5)
    rows = lax.broadcasted_iota(jnp.int32, (length, length), 0)
    columns = lax.broadcasted_iota(jnp.int32, (length, length), 1)
    scores = jnp.where(rows >= columns, scores, -jnp.inf)
    raised = jnp.exp(scores - jnp.max(scores, -1, keepdims=True))
    return raised / jnp.sum(raised, -1, keepdims=True)


def head_span(k):
    return slice(k * LANES, (k + 1) * LANES)


def load(refs):
    parts = [r[...] for r in refs]
    return parts[0] if len(parts) == 1 else jnp.concatenate(parts, 0)


def take(refs, counts):
    refs, out = list(refs), []
    for count in counts:
        out.append(refs[:count])
        refs = refs[count:]
    return out, refs


def inverse_rms(rows):
    return lax.rsqrt(jnp.mean(rows * rows, -1, keepdims=True) + NORM_EPS)


def attn_forward_kernel(queries, keys, counts, *refs):
    blocks, rest = take(refs, counts)
    gain_ref, w_ref, wo_ref, pick_ref, cos_ref, sin_ref = rest[:6]
    parts, (h_ref, qkv_ref, o_ref) = rest[6 : 6 + len(blocks)], rest[6 + len(blocks) :]
    cosine, sine = cos_ref[...], sin_ref[...]
    length = cosine.shape[0]
    for n, block in enumerate(blocks):
        at_rows = slice(n * length, (n + 1) * length)
        x = load(block).astype(F32)
        normed = (x * inverse_rms(x) * gain_ref[...]).astype(BF16)
        h_ref[at_rows, :] = normed
        mixed = nn(normed, w_ref[...])
        made = []
        for k in range(queries + 2 * keys):
            piece = mixed[:, head_span(k)]
            made.append((turn(piece, cosine, sine) if k < queries + keys else piece).astype(BF16))
            qkv_ref[at_rows, head_span(k)] = made[k]
        heads = []
        for k in range(queries):
            at = k * keys // queries
            probs = head_probs(made[k], made[queries + at])
            heads.append(nn(probs.astype(BF16), made[queries + keys + at]).astype(BF16))
        heads = nn(jnp.concatenate(heads, 1), pick_ref[...]).astype(BF16)
        o_ref[at_rows, :] = heads
        parts[n][...] = nn(heads, wo_ref[...]).astype(BF16)


def attn_forward(blocks, gain, w, wo, pick, tables, queries, keys):
    counts = [len(b) for b in blocks]
    length, width = tables[0].shape[0], w.shape[0]
    rows = length * len(blocks)
    *parts, h, qkv, o = call(
        functools.partial(attn_forward_kernel, queries, keys, counts),
        [*flat(blocks), gain, w, wo, pick, *tables],
        [((length, width), BF16)] * len(blocks)
        + [((rows, width), BF16), ((rows, w.shape[1]), BF16), ((rows, wo.shape[0]), BF16)],
        flops=2 * rows * width * (w.shape[1] + wo.shape[0]) + 4 * rows * length * queries * LANES,
        exps=rows * length * queries,
    )
    return parts, (h, qkv, o)


def mlp_kernel(counts, *refs):
    blocks, rest = take(refs, counts)
    half = len(blocks) // 2
    wgu_ref, wd_ref = rest[:2]
    outs, dhs = rest[2 : 2 + half], rest[2 + half : 2 + 2 * half]
    dgu_ref, at_ref, h_ref, c_ref, a_ref = rest[2 + 2 * half :]
    length = outs[0].shape[0]
    for n in range(half):
        h_ref[n * length : (n + 1) * length, :] = load(blocks[n])
        c_ref[n * length : (n + 1) * length, :] = load(blocks[half + n])
    hidden, width = wd_ref.shape
    tile = min(hidden, 2 * LANES)

    def first(k, carry):
        at = pl.multiple_of(k * tile, tile)
        over = pl.multiple_of(hidden + k * tile, tile)
        gate = nn(h_ref[...], wgu_ref[:, pl.ds(at, tile)])
        upward = nn(h_ref[...], wgu_ref[:, pl.ds(over, tile)])
        d_active = nt(c_ref[...], wd_ref[pl.ds(at, tile), :])
        sigmoid = jax.nn.sigmoid(gate)
        silu = gate * sigmoid
        active = (silu * upward).astype(BF16)
        a_ref[:, pl.ds(at, tile)] = active
        at_ref[pl.ds(at, tile), :] = active.T
        d_gate = d_active * upward * sigmoid * (1.0 + gate * (1.0 - sigmoid))
        dgu_ref[:, pl.ds(at, tile)] = d_gate.astype(BF16)
        dgu_ref[:, pl.ds(over, tile)] = (d_active * silu).astype(BF16)
        return carry

    lax.fori_loop(0, hidden // tile, first, 0)
    wtile = 2 * LANES

    def second(k, carry):
        at = pl.ds(pl.multiple_of(k * wtile, wtile), wtile)
        d_normed = nt(dgu_ref[...], wgu_ref[at, :]).astype(BF16)
        output = nn(a_ref[...], wd_ref[:, at]).astype(BF16)
        for n in range(half):
            dhs[n][:, at] = d_normed[n * length : (n + 1) * length]
            outs[n][:, at] = output[n * length : (n + 1) * length]
        return carry

    lax.fori_loop(0, width // wtile, second, 0)


def mlp_both(h, c, wgu, wd):
    counts = [len(b) for b in [*h, *c]]
    half = len(h)
    length, width, hidden = sum(p.shape[0] for p in h[0]), wgu.shape[0], wd.shape[0]
    rows = half * length
    made = call(
        functools.partial(mlp_kernel, counts),
        [*flat(h), *flat(c), wgu, wd],
        [((length, width), BF16)] * (2 * half)
        + [((rows, 2 * hidden), BF16), ((hidden, rows), BF16)],
        scratch=[
            pltpu.VMEM((rows, width), BF16),
            pltpu.VMEM((rows, width), BF16),
            pltpu.VMEM((rows, hidden), BF16),
        ],
        flops=12 * rows * width * hidden,
        exps=rows * hidden,
        limit=MLP_VMEM_BYTES,
    )
    return made[:half], made[half : 2 * half], made[2 * half], made[2 * half + 1]


def stack_rows(parts, out):
    at = 0
    for part in parts:
        out[at : at + part.shape[0], :] = part[...]
        at += part.shape[0]


def wide_grads_kernel(count, pieces, *refs):
    hs, ds, (g_ref, h_all, d_all) = refs[:pieces], refs[pieces : pieces + count], refs[pieces + count :]

    @pl.when(pl.program_id(0) == 0)
    def _():
        stack_rows(ds, d_all)

    stack_rows(hs, h_all)
    g_ref[...] = tn(h_all[...], d_all[...]).astype(BF16)


def down_grads_kernel(count, pieces, *refs):
    ats, cs, (g_ref, at_all, c_all) = refs[:count], refs[count : count + pieces], refs[count + pieces :]

    @pl.when(pl.program_id(0) == 0)
    def _():
        at = 0
        for across in ats:
            at_all[:, at : at + across.shape[1]] = across[...]
            at += across.shape[1]

    stack_rows(cs, c_all)
    g_ref[...] = nn(at_all[...], c_all[...]).astype(BF16)


def attn_backward_kernel(queries, keys, counts, *refs):
    blocks, rest = take(refs, counts)
    qkv_ref, w_ref, wo_ref, pick_ref, cos_ref, sin_ref = rest[:6]
    dhs, (dqkv_ref,) = rest[6 : 6 + len(blocks)], rest[6 + len(blocks) :]
    cosine, sine = cos_ref[...], sin_ref[...]
    length = cosine.shape[0]
    each = queries // keys
    scale = HEAD_DIM ** (-0.5)
    for n, block in enumerate(blocks):
        at_rows = slice(n * length, (n + 1) * length)
        d_heads = nt(load(block), wo_ref[...]).astype(BF16)
        d_heads = nt(d_heads, pick_ref[...]).astype(BF16)
        for at in range(keys):
            key = qkv_ref[at_rows, head_span(queries + at)]
            value = qkv_ref[at_rows, head_span(queries + keys + at)]
            d_key, d_value = 0.0, 0.0
            for k in range(at * each, (at + 1) * each):
                query = qkv_ref[at_rows, head_span(k)]
                d_head = d_heads[:, head_span(k)]
                probs = head_probs(query, key)
                d_value += tn(probs.astype(BF16), d_head)
                d_probs = nt(d_head, value)
                delta = jnp.sum(probs * d_probs, -1, keepdims=True)
                d_scores = (probs * (d_probs - delta) * scale).astype(BF16)
                d_query = nn(d_scores, key)
                d_key += tn(d_scores, query)
                dqkv_ref[at_rows, head_span(k)] = turn_back(d_query, cosine, sine).astype(BF16)
            dqkv_ref[at_rows, head_span(queries + at)] = turn_back(d_key, cosine, sine).astype(BF16)
            dqkv_ref[at_rows, head_span(queries + keys + at)] = d_value.astype(BF16)
    wtile = 2 * LANES

    def second(k, carry):
        at = pl.ds(pl.multiple_of(k * wtile, wtile), wtile)
        d_normed = nt(dqkv_ref[...], w_ref[at, :]).astype(BF16)
        for n in range(len(blocks)):
            dhs[n][:, at] = d_normed[n * length : (n + 1) * length]
        return carry

    lax.fori_loop(0, w_ref.shape[0] // wtile, second, 0)


def attn_backward(blocks, qkv, w, wo, pick, tables, queries, keys):
    counts = [len(b) for b in blocks]
    length, width = tables[0].shape[0], w.shape[0]
    rows = length * len(blocks)
    *dhs, dqkv = call(
        functools.partial(attn_backward_kernel, queries, keys, counts),
        [*flat(blocks), qkv, w, wo, pick, *tables],
        [((length, width), BF16)] * len(blocks) + [((rows, w.shape[1]), BF16)],
        flops=2 * rows * width * (w.shape[1] + wo.shape[0]) + 10 * rows * length * queries * LANES,
        exps=rows * length * queries,
    )
    return dhs, dqkv


def attn_grads_kernel(count, *refs):
    hs, ds, pick_ref = refs[:count], refs[count : 2 * count], refs[2 * count]
    g_ref, h_all, d_all = refs[2 * count + 1 :]

    @pl.when(pl.program_id(0) == 0)
    def _():
        stack_rows(ds, d_all)

    stack_rows(hs, h_all)
    grad = tn(h_all[...], d_all[...]).astype(BF16)
    g_ref[...] = nt(grad, pick_ref[...]).astype(BF16)


def out_grads_kernel(count, pieces, *refs):
    os, ms, (g_ref, o_all, m_all) = refs[:count], refs[count : count + pieces], refs[count + pieces :]

    @pl.when(pl.program_id(0) == 0)
    def _():
        stack_rows(os, o_all)

    stack_rows(ms, m_all)
    g_ref[...] = tn(o_all[...], m_all[...]).astype(BF16)


def grads_call(kernel, tiled, fixed, consts, out, along, flops, held=None):
    tile = 2 * LANES
    rows, width = sum(y.shape[0] for y in tiled), tiled[0].shape[1]
    held = held or (rows, fixed[0].shape[1])
    whole = lambda y: pl.BlockSpec(y.shape, lambda i: (0, 0), pipeline_mode=pl.Buffered(1))
    part = lambda y: pl.BlockSpec((y.shape[0], tile), lambda i: (0, i))
    moving, resident = pltpu.VMEM((rows, tile), BF16), pltpu.VMEM(held, BF16)
    if along == 0:
        inputs = [*tiled, *fixed, *consts]
        specs = [part(y) for y in tiled] + [whole(y) for y in [*fixed, *consts]]
        out_spec = pl.BlockSpec((tile, out[1]), lambda i: (i, 0))
        scratch = [moving, resident]
    else:
        inputs, specs = [*fixed, *tiled], [whole(y) for y in fixed] + [part(y) for y in tiled]
        out_spec = pl.BlockSpec((out[0], tile), lambda i: (0, i))
        scratch = [resident, moving]
    return pl.pallas_call(
        kernel,
        grid=(width // tile,),
        in_specs=specs,
        out_specs=out_spec,
        out_shape=jax.ShapeDtypeStruct(out, BF16),
        scratch_shapes=scratch,
        compiler_params=pltpu.CompilerParams(
            dimension_semantics=("arbitrary",), vmem_limit_bytes=VMEM_BYTES
        ),
        cost_estimate=pl.CostEstimate(flops=flops, bytes_accessed=3 * rows * width, transcendentals=0),
    )(*inputs)


def finish_kernel(kind, counts, *refs):
    (whole, low, top), rest = take(refs, counts)
    length = whole[0].shape[0]
    cut = length // 2
    halves = []
    for half, extra in ((0, low), (1, top)):
        rows = slice(half * cut, (half + 1) * cut)
        total = sum(t[rows, :].astype(F32) for t in whole)
        halves.append(sum((t[...].astype(F32) for t in extra), total))
    total = jnp.concatenate(halves, 0)
    if kind == "middle":
        x_ref, gain_ref, middle_ref, h_ref = rest
        middle = x_ref[...].astype(F32) + total
        middle_ref[...] = middle
        h_ref[...] = (middle * inverse_rms(middle) * gain_ref[...]).astype(BF16)
    elif kind == "output":
        middle_ref, out_ref = rest
        out_ref[...] = (middle_ref[...] + total).astype(BF16)
    else:
        rows_ref, base_ref, gain_ref, *outs = rest
        rows = rows_ref[...].astype(F32)
        inverse = inverse_rms(rows)
        scaled = total * gain_ref[...]
        mean = jnp.mean(scaled * rows, -1, keepdims=True)
        made = base_ref[...].astype(F32) + inverse * scaled - rows * inverse**3 * mean
        for out in outs:
            out[...] = made.astype(out.dtype)


def finish(kind, terms, extras, kinds):
    counts = [len(t) for t in terms]
    shape = terms[0][0].shape
    return call(
        functools.partial(finish_kernel, kind, counts),
        [*flat(terms), *extras],
        [(shape, k) for k in kinds],
        flops=16 * math.prod(shape),
    )


def spread_kernel(at_ref, gate_ref, up_ref, down_ref, wg_ref, wu_ref, gate_out, up_out, down_out, gain_out):
    gate, upward = gate_ref[0].astype(F32), up_ref[0].astype(F32)
    gate_out[...] = gate
    up_out[...] = upward
    down_out[...] = down_ref[0].astype(F32)

    @pl.when((pl.program_id(0) == 0) & (pl.program_id(1) == 0))
    def _():
        gain_out[...] = jnp.zeros_like(gain_out)

    gain_out[...] += gate * wg_ref[...].astype(F32) + upward * wu_ref[...].astype(F32)


def spread(at, gate_up, down, w_gate, w_up, parts):
    count, width, wide = gate_up.shape
    tile = wide // 2 // parts
    short = down.shape[1] // parts
    columns = pl.BlockSpec((width, tile), lambda a, s, at: (0, s * count + a))
    spec = pltpu.PrefetchScalarGridSpec(
        num_scalar_prefetch=1,
        grid=(count, parts),
        in_specs=[
            pl.BlockSpec((1, width, tile), lambda a, s, at: (a ^ at[0], 0, s)),
            pl.BlockSpec((1, width, tile), lambda a, s, at: (a ^ at[0], 0, parts + s)),
            pl.BlockSpec((1, short, down.shape[2]), lambda a, s, at: (a ^ at[0], s, 0)),
            columns,
            columns,
        ],
        out_specs=[
            columns,
            columns,
            pl.BlockSpec((short, down.shape[2]), lambda a, s, at: (a * parts + s, 0)),
            pl.BlockSpec((width, tile), lambda a, s, at: (0, 0)),
        ],
    )
    return pl.pallas_call(
        spread_kernel,
        grid_spec=spec,
        out_shape=[
            jax.ShapeDtypeStruct((width, count * wide // 2), F32),
            jax.ShapeDtypeStruct((width, count * wide // 2), F32),
            jax.ShapeDtypeStruct((count * down.shape[1], down.shape[2]), F32),
            jax.ShapeDtypeStruct((width, tile), F32),
        ],
        compiler_params=pltpu.CompilerParams(dimension_semantics=("arbitrary", "arbitrary")),
        cost_estimate=pl.CostEstimate(
            flops=0, bytes_accessed=6 * (gate_up.size + down.size), transcendentals=0
        ),
        name="spread",
    )(at, gate_up, gate_up, down, w_gate, w_up)


def spread_attn_kernel(count, cuts, at_ref, *refs):
    blocks, (wq_ref, wk_ref, wv_ref), (q_out, k_out, v_out, gain_out) = refs[:count], refs[count : count + 3], refs[count + 3 :]

    @pl.when(pl.program_id(0) == 0)
    def _():
        gain_out[...] = jnp.zeros_like(gain_out)

    total = 0.0
    spans = ((0, cuts[0]), (cuts[0], cuts[1]), (cuts[1], blocks[0].shape[2]))
    for (low, high), out, w_ref in zip(spans, (q_out, k_out, v_out), (wq_ref, wk_ref, wv_ref)):
        made = jnp.concatenate([b[0, :, low:high].astype(F32) for b in blocks], 1)
        out[...] = made
        total += jnp.sum(made * w_ref[...].astype(F32), 1, keepdims=True)
    gain_out[...] += total


def spread_attn(at, stack, weights, cuts):
    group, slab, narrow = stack.shape
    count = LANES // math.gcd(LANES, HEAD_DIM)
    count = math.gcd(group, count)
    widths = (cuts[0], cuts[1] - cuts[0], narrow - cuts[1])
    columns = [pl.BlockSpec((slab, count * w), lambda p, at: (0, p)) for w in widths]

    def block(i):
        return pl.BlockSpec((1, slab, narrow), lambda p, at: ((p * count + i) ^ at[0], 0, 0))

    return pl.pallas_call(
        functools.partial(spread_attn_kernel, count, cuts),
        grid_spec=pltpu.PrefetchScalarGridSpec(
            num_scalar_prefetch=1,
            grid=(group // count,),
            in_specs=[block(i) for i in range(count)] + columns,
            out_specs=columns + [pl.BlockSpec((slab, 1), lambda p, at: (0, 0))],
        ),
        out_shape=[jax.ShapeDtypeStruct((slab, group * w), F32) for w in widths]
        + [jax.ShapeDtypeStruct((slab, 1), F32)],
        compiler_params=pltpu.CompilerParams(dimension_semantics=("arbitrary",)),
        cost_estimate=pl.CostEstimate(flops=0, bytes_accessed=8 * stack.size, transcendentals=0),
        name="spread_attn",
    )(at, *[stack] * count, *weights)


def head_columns(queries, keys):
    half, lane = HEAD_DIM // 2, jnp.arange(LANES)
    place = lane % (LANES // 2)
    turned = jnp.where(place < half, (lane // (LANES // 2)) * half + place, -1)
    plain = jnp.where(lane < HEAD_DIM, lane, -1)
    columns = []
    for k in range(queries + 2 * keys):
        inside = turned if k < queries + keys else plain
        columns.append(jnp.where(inside >= 0, inside + k * HEAD_DIM, -1))
    return jnp.concatenate(columns)


def gather_shard(x):
    return lax.all_gather(x, "shard", axis=0, tiled=True)


def scatter_shard(x):
    return lax.psum_scatter(x, "shard", scatter_dimension=0, tiled=True)


def after(x, *others):
    return lax.optimization_barrier((x, *others))[0]


def layer(
    tokens, cotangent, attn_gain, w_query, w_key, w_value, w_out, mlp_gain, w_gate, w_up, w_down
):
    replicas, shards = lax.axis_size("replica"), lax.axis_size("shard")
    length, width = tokens.shape
    slab = w_query.shape[0]
    kv_heads = w_key.shape[1] // HEAD_DIM
    group = math.gcd(replicas, kv_heads)
    keys = kv_heads // group
    queries = w_query.shape[1] // HEAD_DIM // group
    high = [1 << k for k in range(1, group.bit_length() - 1)]
    place = lax.axis_index("replica") % group
    hidden = w_down.shape[0] // group
    narrow = (queries + 2 * keys) * HEAD_DIM

    x = plane_gather(tokens, high)

    wq = lax.dynamic_slice_in_dim(w_query, place * queries * HEAD_DIM, queries * HEAD_DIM, 1)
    wk = lax.dynamic_slice_in_dim(w_key, place * keys * HEAD_DIM, keys * HEAD_DIM, 1)
    wv = lax.dynamic_slice_in_dim(w_value, place * keys * HEAD_DIM, keys * HEAD_DIM, 1)
    spare = 16
    gain_rows = -(-slab // narrow)
    gains = jnp.stack([attn_gain, mlp_gain])
    gains = jnp.pad(gains, ((0, 0), (0, gain_rows * narrow - slab))).reshape(2 * gain_rows, narrow)
    gains = jnp.pad(gains, ((0, spare - 2 * gain_rows), (0, 0)))
    sent = jnp.concatenate([jnp.concatenate([wq, wk, wv], 1), gains], 0)
    both = gather_shard(sent).reshape(shards, slab + spare, narrow)
    w_out, w_gate_s, w_up_s, w_down_s, _ = lax.optimization_barrier((w_out, w_gate, w_up, w_down, sent))

    turns = group // shards
    chunk = w_out.shape[0] // group
    mine = lax.dynamic_slice_in_dim(w_out, place * chunk, chunk, 0)
    routes = []
    for turn_by in range(shards):
        route = []
        for i in range(replicas):
            base, q = i - i % group, i % group
            for z in range(shards):
                to = (base + z * turns + q // shards) * shards + (q + turn_by) % shards
                route.append((i * shards + z, to))
        routes.append(route)
    back = [(b, a) for a, b in routes[0]]
    came = []
    for route in routes:
        came.append(lax.ppermute(mine, ("replica", "shard"), route))
    here = lax.axis_index("shard")
    came = jnp.stack(came)[(here - jnp.arange(shards)) % shards]
    wo = came.reshape(shards * chunk, width)

    columns = head_columns(queries, keys)
    pick = (jnp.arange(narrow)[:, None] == columns[None, :]).astype(BF16)
    wqkv = nn(both[:, :slab].reshape(width, narrow), pick).astype(BF16)
    gains = both[:, slab : slab + 2 * gain_rows].reshape(shards, 2, gain_rows * narrow)[:, :, :slab]
    gains = jnp.moveaxis(gains, 1, 0).reshape(2, 1, width).astype(F32)
    gain_a, gain_m = gains[0], gains[1]
    lanes = jnp.arange(queries * LANES)
    heads = (lanes // LANES) * HEAD_DIM + lanes % LANES
    heads = jnp.where(lanes % LANES < HEAD_DIM, heads, -1)
    pick_o = (jnp.arange(queries * HEAD_DIM)[None, :] == heads[:, None]).astype(BF16)

    wgu = jnp.concatenate(
        [
            lax.dynamic_slice_in_dim(w, s * group * hidden + place * hidden, hidden, 1)
            for w in (w_gate_s, w_up_s)
            for s in range(shards)
        ],
        1,
    )
    wd = lax.dynamic_slice_in_dim(w_down_s, place * hidden, hidden, 0)
    wgu = gather_shard(wgu)
    wd = gather_shard(wd)

    c = plane_gather(after(cotangent, *x[high[0]], *x[high[-1]]), high)

    pairs = [j for j in sorted(x, reverse=True) if j % 2 == 0]
    tables = rope_tables(length)
    parts, saved = {}, {}
    for j in pairs:
        (parts[j ^ 1], parts[j]), saved[j] = attn_forward(
            [x[j ^ 1], x[j]], gain_a, wqkv, wo, pick_o, tables, queries, keys
        )
    middle, h_own = finish("middle", plane_scatter(parts, high), [tokens, gain_m], [F32, BF16])
    h = plane_gather(h_own, high)

    order = list(reversed(pairs))
    order = order[:-2] + [order[-1], order[-2]] if len(order) > 2 else order
    outs, dhs, dgus, acrosses = {}, {}, [], []
    for j in order:
        (outs[j ^ 1], outs[j]), (dhs[j ^ 1], dhs[j]), dgu, across = mlp_both(
            [h[j ^ 1], h[j]], [c[j ^ 1], c[j]], wgu, wd
        )
        dgus.append(dgu)
        acrosses.append(across)
    d_middle, dm_own = finish(
        "back", plane_scatter(dhs, high), [middle, cotangent, gain_m], [F32, BF16]
    )
    all_h = flat(h[k] for j in order for k in (j ^ 1, j))
    all_c = flat(c[k] for j in order for k in (j ^ 1, j))
    rows = group * length
    g_gu = grads_call(
        functools.partial(wide_grads_kernel, len(dgus), len(all_h)),
        all_h, dgus, [], wgu.shape, 0, 2 * rows * width * wgu.shape[1],
    )
    g_d = grads_call(
        functools.partial(down_grads_kernel, len(acrosses), len(all_c)),
        all_c, acrosses, [], wd.shape, 1, 2 * rows * width * wd.shape[0],
        (wd.shape[0], rows),
    )
    g_gu, g_d = scatter_shard(g_gu), scatter_shard(g_d)
    dm = plane_gather(dm_own, high)
    all_dm = flat(dm[k] for j in order for k in (j ^ 1, j))
    g_o = grads_call(
        functools.partial(out_grads_kernel, len(pairs), len(all_dm)),
        all_dm, [saved[j][2] for j in order], [], wo.shape, 1,
        2 * rows * width * wo.shape[0],
    )
    g_o = lax.ppermute(scatter_shard(g_o), ("replica", "shard"), back)

    das, dqkvs = {}, []
    for j in order:
        (das[j ^ 1], das[j]), dqkv = attn_backward(
            [dm[j ^ 1], dm[j]], saved[j][1], wqkv, wo, pick_o, tables, queries, keys
        )
        dqkvs.append(dqkv)
    g_w = grads_call(
        functools.partial(attn_grads_kernel, len(pairs)),
        [saved[j][0] for j in order], dqkvs, [pick], (width, narrow), 0,
        2 * rows * width * pick.shape[1],
    )
    g_w = scatter_shard(g_w)
    (input_grad,) = finish("back", plane_scatter(das, high), [tokens, d_middle, gain_a], [F32])

    outs = dict(zip(outs, (after(y, *all_dm) for y in outs.values())))
    (block_output,) = finish("output", plane_scatter(outs, high), [middle], [BF16])

    bit = group
    while bit < replicas:
        g_gu, g_d, g_w, g_o = (g + swap(g, bit) for g in (g_gu, g_d, g_w, g_o))
        bit *= 2

    def stacked(g):
        got = plane_gather(g, high)
        return jnp.concatenate(flat(got[j] for j in range(group)), 0).reshape(group, *g.shape)

    gate_grad, up_grad, down_grad, gain_terms = spread(
        place.reshape(1), stacked(g_gu), stacked(g_d), w_gate, w_up, shards
    )
    mlp_gain_grad = jnp.sum(gain_terms, 1) / mlp_gain.astype(F32)
    absolute = jnp.arange(group) ^ place
    out_grad = stacked(g_o)[absolute].astype(F32).reshape(group * chunk, width)
    cuts = (queries * HEAD_DIM, (queries + keys) * HEAD_DIM)
    query_grad, key_grad, value_grad, gain_terms = spread_attn(
        place.reshape(1), stacked(g_w), (w_query, w_key, w_value), cuts
    )
    attn_gain_grad = gain_terms[:, 0] / attn_gain.astype(F32)
    return (
        block_output,
        input_grad,
        attn_gain_grad,
        query_grad,
        key_grad,
        value_grad,
        out_grad,
        mlp_gain_grad,
        gate_grad,
        up_grad,
        down_grad,
    )


def solution(mesh):
    tokens, weights, gains = P(("replica", "shard"), None), P("shard", None), P("shard")
    return jax.shard_map(
        layer,
        mesh=mesh,
        in_specs=(tokens, tokens, gains, weights, weights, weights, weights, gains, weights, weights, weights),
        out_specs=(tokens, tokens, gains, weights, weights, weights, weights, gains, weights, weights, weights),
        check_vma=False,
    )
```

```python
import functools
import math

import jax
import jax.numpy as jnp
from jax import lax
from jax.experimental import pallas as pl
from jax.experimental.pallas import tpu as pltpu
from jax.sharding import PartitionSpec as P


HEAD_DIM = 96
LANES = 128
NORM_EPS = 1e-05
ROPE_BASE = 100000.0
VMEM_BYTES = 40 * 1024 * 1024
MLP_VMEM_BYTES = 40 * 1024 * 1024
F32 = jnp.float32
BF16 = jnp.bfloat16


def nn(left, right):
    return jnp.dot(left, right, preferred_element_type=F32)


def nt(left, right):
    return lax.dot_general(left, right, (((1,), (1,)), ((), ())), preferred_element_type=F32)


def tn(left, right):
    return lax.dot_general(left, right, (((0,), (0,)), ((), ())), preferred_element_type=F32)


def swap(x, bit):
    size = lax.axis_size("replica")
    return lax.ppermute(x, "replica", [(i, i ^ bit) for i in range(size)])


def plane_gather(x, high):
    cut = x.shape[0] // 2
    got = {0: (x,)}
    if len(high) == 2:
        a, b = high
        from_a, from_b = swap(x, a), swap(x, b)
        got[a], got[b] = (from_a,), (from_b,)
        got[1] = (swap(x, 1),)
        far = swap(from_b[:cut], a), swap(from_a[cut:], b)
        got[a ^ b] = far
    else:
        for bit in high:
            more = {j ^ bit: tuple(swap(p, bit) for p in got[j]) for j in list(got)}
            got.update(more)
    for j in list(got):
        if j ^ 1 not in got:
            got[j ^ 1] = tuple(swap(p, 1) for p in got[j])
    return got


def plane_scatter(parts, high):
    cut = parts[0].shape[0] // 2
    even = [j for j in parts if j % 2 == 0]
    both = {j: (parts[j], swap(parts[j ^ 1], 1)) for j in even}

    def total(terms, rows):
        return sum(t[rows].astype(F32) for t in terms).astype(BF16)

    low, top, full = slice(0, cut), slice(cut, 2 * cut), slice(0, 2 * cut)
    if len(high) == 2:
        a, b = high
        far, near_a, near_b = both[a ^ b], both[a], both[b]
        via_a = swap(total(far, low), a)
        via_b = swap(total(far, top), b)
        first_a = swap(total(near_a, low), a)
        first_b = swap(total(near_b, top), b)
        last_a = (total32(near_a, top) + via_b.astype(F32)).astype(BF16)
        last_b = (total32(near_b, low) + via_a.astype(F32)).astype(BF16)
        last_a, last_b = swap(last_a, a), swap(last_b, b)
        return both[0], (first_a, last_b), (last_a, first_b)
    sums = {j: total(both[j], full) for j in even}
    for bit in reversed(high):
        sums = {j: total((sums[j], swap(sums[j ^ bit], bit)), full) for j in sums if not j & bit}
    return (sums[0],), (), ()


def total32(terms, rows):
    return sum(t[rows].astype(F32) for t in terms)


def flat(terms):
    return [y for group in terms for y in group]


def call(kernel, inputs, outputs, scratch=(), flops=0, exps=0, limit=VMEM_BYTES):
    outputs = [jax.ShapeDtypeStruct(shape, kind) for shape, kind in outputs]
    moved = sum(math.prod(y.shape) * y.dtype.itemsize for y in [*inputs, *outputs])
    return pl.pallas_call(
        kernel,
        out_shape=outputs,
        scratch_shapes=list(scratch),
        compiler_params=pltpu.CompilerParams(vmem_limit_bytes=limit),
        cost_estimate=pl.CostEstimate(flops=flops, bytes_accessed=moved, transcendentals=exps),
    )(*inputs)


def rope_tables(length):
    half = HEAD_DIM // 2
    position = jnp.arange(length, dtype=F32)
    freqs = jnp.power(ROPE_BASE, -jnp.arange(half, dtype=F32) / half)
    angles = position[:, None] * freqs[None, :]
    pad = ((0, 0), (0, LANES // 2 - half))
    cosine, sine = jnp.pad(jnp.cos(angles), pad), jnp.pad(jnp.sin(angles), pad)
    return jnp.concatenate([cosine, cosine], 1), jnp.concatenate([-sine, sine], 1)


def turn(values, cosine, sine):
    return values * cosine + pltpu.roll(values, LANES // 2, 1) * sine


def turn_back(values, cosine, sine):
    return values * cosine - pltpu.roll(values, LANES // 2, 1) * sine


def head_probs(query, key):
    length = query.shape[0]
    scores = nt(query, key) * HEAD_DIM ** (-0.5)
    rows = lax.broadcasted_iota(jnp.int32, (length, length), 0)
    columns = lax.broadcasted_iota(jnp.int32, (length, length), 1)
    scores = jnp.where(rows >= columns, scores, -jnp.inf)
    raised = jnp.exp(scores - jnp.max(scores, -1, keepdims=True))
    return raised / jnp.sum(raised, -1, keepdims=True)


def head_span(k):
    return slice(k * LANES, (k + 1) * LANES)


def load(refs):
    parts = [r[...] for r in refs]
    return parts[0] if len(parts) == 1 else jnp.concatenate(parts, 0)


def take(refs, counts):
    refs, out = list(refs), []
    for count in counts:
        out.append(refs[:count])
        refs = refs[count:]
    return out, refs


def inverse_rms(rows):
    return lax.rsqrt(jnp.mean(rows * rows, -1, keepdims=True) + NORM_EPS)


def attn_forward_kernel(queries, keys, counts, *refs):
    blocks, rest = take(refs, counts)
    gain_ref, w_ref, wo_ref, pick_ref, cos_ref, sin_ref = rest[:6]
    parts, (h_ref, qkv_ref, o_ref) = rest[6 : 6 + len(blocks)], rest[6 + len(blocks) :]
    cosine, sine = cos_ref[...], sin_ref[...]
    length = cosine.shape[0]
    for n, block in enumerate(blocks):
        at_rows = slice(n * length, (n + 1) * length)
        x = load(block).astype(F32)
        normed = (x * inverse_rms(x) * gain_ref[...]).astype(BF16)
        h_ref[at_rows, :] = normed
        mixed = nn(normed, w_ref[...])
        made = []
        for k in range(queries + 2 * keys):
            piece = mixed[:, head_span(k)]
            made.append((turn(piece, cosine, sine) if k < queries + keys else piece).astype(BF16))
            qkv_ref[at_rows, head_span(k)] = made[k]
        heads = []
        for k in range(queries):
            at = k * keys // queries
            probs = head_probs(made[k], made[queries + at])
            heads.append(nn(probs.astype(BF16), made[queries + keys + at]).astype(BF16))
        heads = nn(jnp.concatenate(heads, 1), pick_ref[...]).astype(BF16)
        o_ref[at_rows, :] = heads
        parts[n][...] = nn(heads, wo_ref[...]).astype(BF16)


def attn_forward(blocks, gain, w, wo, pick, tables, queries, keys):
    counts = [len(b) for b in blocks]
    length, width = tables[0].shape[0], w.shape[0]
    rows = length * len(blocks)
    *parts, h, qkv, o = call(
        functools.partial(attn_forward_kernel, queries, keys, counts),
        [*flat(blocks), gain, w, wo, pick, *tables],
        [((length, width), BF16)] * len(blocks)
        + [((rows, width), BF16), ((rows, w.shape[1]), BF16), ((rows, wo.shape[0]), BF16)],
        flops=2 * rows * width * (w.shape[1] + wo.shape[0]) + 4 * rows * length * queries * LANES,
        exps=rows * length * queries,
    )
    return parts, (h, qkv, o)


def mlp_kernel(counts, *refs):
    blocks, rest = take(refs, counts)
    half = len(blocks) // 2
    wgu_ref, wd_ref = rest[:2]
    outs, dhs = rest[2 : 2 + half], rest[2 + half : 2 + 2 * half]
    dgu_ref, at_ref, h_ref, c_ref, a_ref = rest[2 + 2 * half :]
    length = outs[0].shape[0]
    for n in range(half):
        h_ref[n * length : (n + 1) * length, :] = load(blocks[n])
        c_ref[n * length : (n + 1) * length, :] = load(blocks[half + n])
    hidden, width = wd_ref.shape
    tile = min(hidden, 2 * LANES)

    def first(k, carry):
        at = pl.multiple_of(k * tile, tile)
        over = pl.multiple_of(hidden + k * tile, tile)
        gate = nn(h_ref[...], wgu_ref[:, pl.ds(at, tile)])
        upward = nn(h_ref[...], wgu_ref[:, pl.ds(over, tile)])
        d_active = nt(c_ref[...], wd_ref[pl.ds(at, tile), :])
        sigmoid = jax.nn.sigmoid(gate)
        silu = gate * sigmoid
        active = (silu * upward).astype(BF16)
        a_ref[:, pl.ds(at, tile)] = active
        at_ref[pl.ds(at, tile), :] = active.T
        d_gate = d_active * upward * sigmoid * (1.0 + gate * (1.0 - sigmoid))
        dgu_ref[:, pl.ds(at, tile)] = d_gate.astype(BF16)
        dgu_ref[:, pl.ds(over, tile)] = (d_active * silu).astype(BF16)
        return carry

    lax.fori_loop(0, hidden // tile, first, 0)
    wtile = 2 * LANES

    def second(k, carry):
        at = pl.ds(pl.multiple_of(k * wtile, wtile), wtile)
        d_normed = nt(dgu_ref[...], wgu_ref[at, :]).astype(BF16)
        output = nn(a_ref[...], wd_ref[:, at]).astype(BF16)
        for n in range(half):
            dhs[n][:, at] = d_normed[n * length : (n + 1) * length]
            outs[n][:, at] = output[n * length : (n + 1) * length]
        return carry

    lax.fori_loop(0, width // wtile, second, 0)


def mlp_both(h, c, wgu, wd):
    counts = [len(b) for b in [*h, *c]]
    half = len(h)
    length, width, hidden = sum(p.shape[0] for p in h[0]), wgu.shape[0], wd.shape[0]
    rows = half * length
    made = call(
        functools.partial(mlp_kernel, counts),
        [*flat(h), *flat(c), wgu, wd],
        [((length, width), BF16)] * (2 * half)
        + [((rows, 2 * hidden), BF16), ((hidden, rows), BF16)],
        scratch=[
            pltpu.VMEM((rows, width), BF16),
            pltpu.VMEM((rows, width), BF16),
            pltpu.VMEM((rows, hidden), BF16),
        ],
        flops=12 * rows * width * hidden,
        exps=rows * hidden,
        limit=MLP_VMEM_BYTES,
    )
    return made[:half], made[half : 2 * half], made[2 * half], made[2 * half + 1]


def stack_rows(parts, out):
    at = 0
    for part in parts:
        out[at : at + part.shape[0], :] = part[...]
        at += part.shape[0]


def wide_grads_kernel(count, pieces, *refs):
    hs, ds, (g_ref, h_all, d_all) = refs[:pieces], refs[pieces : pieces + count], refs[pieces + count :]

    @pl.when(pl.program_id(0) == 0)
    def _():
        stack_rows(ds, d_all)

    stack_rows(hs, h_all)
    g_ref[...] = tn(h_all[...], d_all[...]).astype(BF16)


def down_grads_kernel(count, pieces, *refs):
    ats, cs, (g_ref, at_all, c_all) = refs[:count], refs[count : count + pieces], refs[count + pieces :]

    @pl.when(pl.program_id(0) == 0)
    def _():
        at = 0
        for across in ats:
            at_all[:, at : at + across.shape[1]] = across[...]
            at += across.shape[1]

    stack_rows(cs, c_all)
    g_ref[...] = nn(at_all[...], c_all[...]).astype(BF16)


def attn_backward_kernel(queries, keys, counts, *refs):
    blocks, rest = take(refs, counts)
    qkv_ref, w_ref, wo_ref, pick_ref, cos_ref, sin_ref = rest[:6]
    dhs, (dqkv_ref,) = rest[6 : 6 + len(blocks)], rest[6 + len(blocks) :]
    cosine, sine = cos_ref[...], sin_ref[...]
    length = cosine.shape[0]
    each = queries // keys
    scale = HEAD_DIM ** (-0.5)
    for n, block in enumerate(blocks):
        at_rows = slice(n * length, (n + 1) * length)
        d_heads = nt(load(block), wo_ref[...]).astype(BF16)
        d_heads = nt(d_heads, pick_ref[...]).astype(BF16)
        for at in range(keys):
            key = qkv_ref[at_rows, head_span(queries + at)]
            value = qkv_ref[at_rows, head_span(queries + keys + at)]
            d_key, d_value = 0.0, 0.0
            for k in range(at * each, (at + 1) * each):
                query = qkv_ref[at_rows, head_span(k)]
                d_head = d_heads[:, head_span(k)]
                probs = head_probs(query, key)
                d_value += tn(probs.astype(BF16), d_head)
                d_probs = nt(d_head, value)
                delta = jnp.sum(probs * d_probs, -1, keepdims=True)
                d_scores = (probs * (d_probs - delta) * scale).astype(BF16)
                d_query = nn(d_scores, key)
                d_key += tn(d_scores, query)
                dqkv_ref[at_rows, head_span(k)] = turn_back(d_query, cosine, sine).astype(BF16)
            dqkv_ref[at_rows, head_span(queries + at)] = turn_back(d_key, cosine, sine).astype(BF16)
            dqkv_ref[at_rows, head_span(queries + keys + at)] = d_value.astype(BF16)
    wtile = 2 * LANES

    def second(k, carry):
        at = pl.ds(pl.multiple_of(k * wtile, wtile), wtile)
        d_normed = nt(dqkv_ref[...], w_ref[at, :]).astype(BF16)
        for n in range(len(blocks)):
            dhs[n][:, at] = d_normed[n * length : (n + 1) * length]
        return carry

    lax.fori_loop(0, w_ref.shape[0] // wtile, second, 0)


def attn_backward(blocks, qkv, w, wo, pick, tables, queries, keys):
    counts = [len(b) for b in blocks]
    length, width = tables[0].shape[0], w.shape[0]
    rows = length * len(blocks)
    *dhs, dqkv = call(
        functools.partial(attn_backward_kernel, queries, keys, counts),
        [*flat(blocks), qkv, w, wo, pick, *tables],
        [((length, width), BF16)] * len(blocks) + [((rows, w.shape[1]), BF16)],
        flops=2 * rows * width * (w.shape[1] + wo.shape[0]) + 10 * rows * length * queries * LANES,
        exps=rows * length * queries,
    )
    return dhs, dqkv


def attn_grads_kernel(count, *refs):
    hs, ds, pick_ref = refs[:count], refs[count : 2 * count], refs[2 * count]
    g_ref, h_all, d_all = refs[2 * count + 1 :]

    @pl.when(pl.program_id(0) == 0)
    def _():
        stack_rows(ds, d_all)

    stack_rows(hs, h_all)
    grad = tn(h_all[...], d_all[...]).astype(BF16)
    g_ref[...] = nt(grad, pick_ref[...]).astype(BF16)


def out_grads_kernel(count, pieces, *refs):
    os, ms, (g_ref, o_all, m_all) = refs[:count], refs[count : count + pieces], refs[count + pieces :]

    @pl.when(pl.program_id(0) == 0)
    def _():
        stack_rows(os, o_all)

    stack_rows(ms, m_all)
    g_ref[...] = tn(o_all[...], m_all[...]).astype(BF16)


def grads_call(kernel, tiled, fixed, consts, out, along, flops, held=None):
    tile = 2 * LANES
    rows, width = sum(y.shape[0] for y in tiled), tiled[0].shape[1]
    held = held or (rows, fixed[0].shape[1])
    whole = lambda y: pl.BlockSpec(y.shape, lambda i: (0, 0), pipeline_mode=pl.Buffered(1))
    part = lambda y: pl.BlockSpec((y.shape[0], tile), lambda i: (0, i))
    moving, resident = pltpu.VMEM((rows, tile), BF16), pltpu.VMEM(held, BF16)
    if along == 0:
        inputs = [*tiled, *fixed, *consts]
        specs = [part(y) for y in tiled] + [whole(y) for y in [*fixed, *consts]]
        out_spec = pl.BlockSpec((tile, out[1]), lambda i: (i, 0))
        scratch = [moving, resident]
    else:
        inputs, specs = [*fixed, *tiled], [whole(y) for y in fixed] + [part(y) for y in tiled]
        out_spec = pl.BlockSpec((out[0], tile), lambda i: (0, i))
        scratch = [resident, moving]
    return pl.pallas_call(
        kernel,
        grid=(width // tile,),
        in_specs=specs,
        out_specs=out_spec,
        out_shape=jax.ShapeDtypeStruct(out, BF16),
        scratch_shapes=scratch,
        compiler_params=pltpu.CompilerParams(
            dimension_semantics=("arbitrary",), vmem_limit_bytes=VMEM_BYTES
        ),
        cost_estimate=pl.CostEstimate(flops=flops, bytes_accessed=3 * rows * width, transcendentals=0),
    )(*inputs)


def finish_kernel(kind, counts, *refs):
    (whole, low, top), rest = take(refs, counts)
    length = whole[0].shape[0]
    cut = length // 2
    halves = []
    for half, extra in ((0, low), (1, top)):
        rows = slice(half * cut, (half + 1) * cut)
        total = sum(t[rows, :].astype(F32) for t in whole)
        halves.append(sum((t[...].astype(F32) for t in extra), total))
    total = jnp.concatenate(halves, 0)
    if kind == "middle":
        x_ref, gain_ref, middle_ref, h_ref = rest
        middle = x_ref[...].astype(F32) + total
        middle_ref[...] = middle
        h_ref[...] = (middle * inverse_rms(middle) * gain_ref[...]).astype(BF16)
    elif kind == "output":
        middle_ref, out_ref = rest
        out_ref[...] = (middle_ref[...] + total).astype(BF16)
    else:
        rows_ref, base_ref, gain_ref, *outs = rest
        rows = rows_ref[...].astype(F32)
        inverse = inverse_rms(rows)
        scaled = total * gain_ref[...]
        mean = jnp.mean(scaled * rows, -1, keepdims=True)
        made = base_ref[...].astype(F32) + inverse * scaled - rows * inverse**3 * mean
        for out in outs:
            out[...] = made.astype(out.dtype)


def finish(kind, terms, extras, kinds):
    counts = [len(t) for t in terms]
    shape = terms[0][0].shape
    return call(
        functools.partial(finish_kernel, kind, counts),
        [*flat(terms), *extras],
        [(shape, k) for k in kinds],
        flops=16 * math.prod(shape),
    )


def spread_wide_kernel(counts, at_ref, *refs):
    blocks, (wg_ref, wu_ref, gate_out, up_out, gain_out) = take(refs, counts)
    j, part = pl.program_id(0), pl.program_id(1)
    tile, parts = gate_out.shape[1], pl.num_programs(1)

    @pl.when((j == 0) & (part == 0))
    def _():
        gain_out[...] = jnp.zeros_like(gain_out)

    here = pl.multiple_of(part * tile, tile)
    over = pl.multiple_of((parts + part) * tile, tile)
    for k, block in enumerate(blocks):

        @pl.when(j == k)
        def _(block=block):
            at = 0
            for piece in block:
                rows = slice(at, at + piece.shape[0])
                gate_out[rows, :] = piece[:, pl.ds(here, tile)].astype(F32)
                up_out[rows, :] = piece[:, pl.ds(over, tile)].astype(F32)
                at += piece.shape[0]

    gain_out[...] += gate_out[...] * wg_ref[...].astype(F32) + up_out[...] * wu_ref[...].astype(F32)


def spread_wide(at, blocks, w_gate, w_up, parts):
    counts, pieces, count = [len(b) for b in blocks], flat(blocks), len(blocks)
    width, total = w_gate.shape
    tile = total // count // parts
    columns = pl.BlockSpec((width, tile), lambda j, s, at: (0, s * count + (j ^ at[0])))
    return pl.pallas_call(
        functools.partial(spread_wide_kernel, counts),
        grid_spec=pltpu.PrefetchScalarGridSpec(
            num_scalar_prefetch=1,
            grid=(count, parts),
            in_specs=[
                pl.BlockSpec(p.shape, lambda j, s, at: (0, 0), pipeline_mode=pl.Buffered(1))
                for p in pieces
            ]
            + [columns, columns],
            out_specs=[columns, columns, pl.BlockSpec((width, tile), lambda j, s, at: (0, 0))],
        ),
        out_shape=[
            jax.ShapeDtypeStruct((width, total), F32),
            jax.ShapeDtypeStruct((width, total), F32),
            jax.ShapeDtypeStruct((width, tile), F32),
        ],
        compiler_params=pltpu.CompilerParams(
            dimension_semantics=("arbitrary", "arbitrary"), vmem_limit_bytes=VMEM_BYTES
        ),
        cost_estimate=pl.CostEstimate(flops=0, bytes_accessed=16 * width * total, transcendentals=0),
        name="spread_wide",
    )(at, *pieces, w_gate, w_up)


def spread_rows_kernel(counts, at_ref, *refs):
    blocks, (down_out, o_out) = take(refs, counts)
    j, short = pl.program_id(0), down_out.shape[0]
    for k, block in enumerate(blocks):

        @pl.when(j == k)
        def _(block=block):
            values = load(block).astype(F32)
            down_out[...] = values[:short]
            o_out[...] = values[short:]


def spread_rows(at, blocks, short):
    counts, pieces, count = [len(b) for b in blocks], flat(blocks), len(blocks)
    rows, width = sum(p.shape[0] for p in blocks[0]), pieces[0].shape[1]
    place = lambda j, at: (j ^ at[0], 0)
    return pl.pallas_call(
        functools.partial(spread_rows_kernel, counts),
        grid_spec=pltpu.PrefetchScalarGridSpec(
            num_scalar_prefetch=1,
            grid=(count,),
            in_specs=[
                pl.BlockSpec(p.shape, lambda j, at: (0, 0), pipeline_mode=pl.Buffered(1))
                for p in pieces
            ],
            out_specs=[pl.BlockSpec((short, width), place), pl.BlockSpec((rows - short, width), place)],
        ),
        out_shape=[
            jax.ShapeDtypeStruct((count * short, width), F32),
            jax.ShapeDtypeStruct((count * (rows - short), width), F32),
        ],
        compiler_params=pltpu.CompilerParams(
            dimension_semantics=("arbitrary",), vmem_limit_bytes=VMEM_BYTES
        ),
        cost_estimate=pl.CostEstimate(flops=0, bytes_accessed=6 * count * rows * width, transcendentals=0),
        name="spread_rows",
    )(at, *pieces)


def spread_attn_kernel(counts, count, cuts, at_ref, *refs):
    blocks, rest = take(refs, counts)
    (wq_ref, wk_ref, wv_ref), (q_out, k_out, v_out, gain_out, stack) = rest[:3], rest[3:]
    step = pl.program_id(0)

    @pl.when(step == 0)
    def _():
        gain_out[...] = jnp.zeros_like(gain_out)
        for j, block in enumerate(blocks):
            stack[j ^ at_ref[0]] = load(block)

    total = 0.0
    spans = ((0, cuts[0]), (cuts[0], cuts[1]), (cuts[1], stack.shape[2]))
    held = [stack[step * count + i].astype(F32) for i in range(count)]
    for (low, high), out, w_ref in zip(spans, (q_out, k_out, v_out), (wq_ref, wk_ref, wv_ref)):
        made = jnp.concatenate([b[:, low:high] for b in held], 1)
        out[...] = made
        total += jnp.sum(made * w_ref[...].astype(F32), 1, keepdims=True)
    gain_out[...] += total


def spread_attn(at, blocks, weights, cuts):
    counts, pieces, group = [len(b) for b in blocks], flat(blocks), len(blocks)
    slab, narrow = weights[0].shape[0], pieces[0].shape[1]
    count = math.gcd(group, LANES // math.gcd(LANES, HEAD_DIM))
    widths = (cuts[0], cuts[1] - cuts[0], narrow - cuts[1])
    columns = [pl.BlockSpec((slab, count * w), lambda p, at: (0, p)) for w in widths]
    return pl.pallas_call(
        functools.partial(spread_attn_kernel, counts, count, cuts),
        grid_spec=pltpu.PrefetchScalarGridSpec(
            num_scalar_prefetch=1,
            grid=(group // count,),
            in_specs=[
                pl.BlockSpec(p.shape, lambda p_, at: (0, 0), pipeline_mode=pl.Buffered(1))
                for p in pieces
            ]
            + columns,
            out_specs=columns + [pl.BlockSpec((slab, 1), lambda p, at: (0, 0))],
            scratch_shapes=[pltpu.VMEM((group, slab, narrow), BF16)],
        ),
        out_shape=[jax.ShapeDtypeStruct((slab, group * w), F32) for w in widths]
        + [jax.ShapeDtypeStruct((slab, 1), F32)],
        compiler_params=pltpu.CompilerParams(
            dimension_semantics=("arbitrary",), vmem_limit_bytes=VMEM_BYTES
        ),
        cost_estimate=pl.CostEstimate(
            flops=0, bytes_accessed=8 * group * slab * narrow, transcendentals=0
        ),
        name="spread_attn",
    )(at, *pieces, *weights)


def head_columns(queries, keys):
    half, lane = HEAD_DIM // 2, jnp.arange(LANES)
    place = lane % (LANES // 2)
    turned = jnp.where(place < half, (lane // (LANES // 2)) * half + place, -1)
    plain = jnp.where(lane < HEAD_DIM, lane, -1)
    columns = []
    for k in range(queries + 2 * keys):
        inside = turned if k < queries + keys else plain
        columns.append(jnp.where(inside >= 0, inside + k * HEAD_DIM, -1))
    return jnp.concatenate(columns)


def gather_shard(x):
    return lax.all_gather(x, "shard", axis=0, tiled=True)


def scatter_shard(x):
    return lax.psum_scatter(x, "shard", scatter_dimension=0, tiled=True)


def after(x, *others):
    return lax.optimization_barrier((x, *others))[0]


def layer(
    tokens, cotangent, attn_gain, w_query, w_key, w_value, w_out, mlp_gain, w_gate, w_up, w_down
):
    replicas, shards = lax.axis_size("replica"), lax.axis_size("shard")
    length, width = tokens.shape
    slab = w_query.shape[0]
    kv_heads = w_key.shape[1] // HEAD_DIM
    group = math.gcd(replicas, kv_heads)
    keys = kv_heads // group
    queries = w_query.shape[1] // HEAD_DIM // group
    high = [1 << k for k in range(1, group.bit_length() - 1)]
    place = lax.axis_index("replica") % group
    hidden = w_down.shape[0] // group
    narrow = (queries + 2 * keys) * HEAD_DIM

    x = plane_gather(tokens, high)

    wq = lax.dynamic_slice_in_dim(w_query, place * queries * HEAD_DIM, queries * HEAD_DIM, 1)
    wk = lax.dynamic_slice_in_dim(w_key, place * keys * HEAD_DIM, keys * HEAD_DIM, 1)
    wv = lax.dynamic_slice_in_dim(w_value, place * keys * HEAD_DIM, keys * HEAD_DIM, 1)
    spare = 16
    gain_rows = -(-slab // narrow)
    gains = jnp.stack([attn_gain, mlp_gain])
    gains = jnp.pad(gains, ((0, 0), (0, gain_rows * narrow - slab))).reshape(2 * gain_rows, narrow)
    gains = jnp.pad(gains, ((0, spare - 2 * gain_rows), (0, 0)))
    sent = jnp.concatenate([jnp.concatenate([wq, wk, wv], 1), gains], 0)
    both = gather_shard(sent).reshape(shards, slab + spare, narrow)
    w_out, w_gate_s, w_up_s, w_down_s, _ = lax.optimization_barrier((w_out, w_gate, w_up, w_down, sent))

    turns = group // shards
    chunk = w_out.shape[0] // group
    mine = lax.dynamic_slice_in_dim(w_out, place * chunk, chunk, 0)
    routes = []
    for turn_by in range(shards):
        route = []
        for i in range(replicas):
            base, q = i - i % group, i % group
            for z in range(shards):
                to = (base + z * turns + q // shards) * shards + (q + turn_by) % shards
                route.append((i * shards + z, to))
        routes.append(route)
    back = [(b, a) for a, b in routes[0]]
    came = []
    for route in routes:
        came.append(lax.ppermute(mine, ("replica", "shard"), route))
    here = lax.axis_index("shard")
    came = jnp.stack(came)[(here - jnp.arange(shards)) % shards]
    wo = came.reshape(shards * chunk, width)

    columns = head_columns(queries, keys)
    pick = (jnp.arange(narrow)[:, None] == columns[None, :]).astype(BF16)
    wqkv = nn(both[:, :slab].reshape(width, narrow), pick).astype(BF16)
    gains = both[:, slab : slab + 2 * gain_rows].reshape(shards, 2, gain_rows * narrow)[:, :, :slab]
    gains = jnp.moveaxis(gains, 1, 0).reshape(2, 1, width).astype(F32)
    gain_a, gain_m = gains[0], gains[1]
    lanes = jnp.arange(queries * LANES)
    heads = (lanes // LANES) * HEAD_DIM + lanes % LANES
    heads = jnp.where(lanes % LANES < HEAD_DIM, heads, -1)
    pick_o = (jnp.arange(queries * HEAD_DIM)[None, :] == heads[:, None]).astype(BF16)

    wgu = jnp.concatenate(
        [
            lax.dynamic_slice_in_dim(w, s * group * hidden + place * hidden, hidden, 1)
            for w in (w_gate_s, w_up_s)
            for s in range(shards)
        ],
        1,
    )
    wd = lax.dynamic_slice_in_dim(w_down_s, place * hidden, hidden, 0)
    wgu = gather_shard(wgu)
    wd = gather_shard(wd)

    c = plane_gather(after(cotangent, *x[high[0]], *x[high[-1]]), high)

    pairs = [j for j in sorted(x, reverse=True) if j % 2 == 0]
    tables = rope_tables(length)
    parts, saved = {}, {}
    for j in pairs:
        (parts[j ^ 1], parts[j]), saved[j] = attn_forward(
            [x[j ^ 1], x[j]], gain_a, wqkv, wo, pick_o, tables, queries, keys
        )
    middle, h_own = finish("middle", plane_scatter(parts, high), [tokens, gain_m], [F32, BF16])
    h = plane_gather(h_own, high)

    order = list(reversed(pairs))
    order = order[:-2] + [order[-1], order[-2]] if len(order) > 2 else order
    outs, dhs, dgus, acrosses = {}, {}, [], []
    for j in order:
        (outs[j ^ 1], outs[j]), (dhs[j ^ 1], dhs[j]), dgu, across = mlp_both(
            [h[j ^ 1], h[j]], [c[j ^ 1], c[j]], wgu, wd
        )
        dgus.append(dgu)
        acrosses.append(across)
    d_middle, dm_own = finish(
        "back", plane_scatter(dhs, high), [middle, cotangent, gain_m], [F32, BF16]
    )
    all_h = flat(h[k] for j in order for k in (j ^ 1, j))
    all_c = flat(c[k] for j in order for k in (j ^ 1, j))
    rows = group * length
    g_gu = grads_call(
        functools.partial(wide_grads_kernel, len(dgus), len(all_h)),
        all_h, dgus, [], wgu.shape, 0, 2 * rows * width * wgu.shape[1],
    )
    g_d = grads_call(
        functools.partial(down_grads_kernel, len(acrosses), len(all_c)),
        all_c, acrosses, [], wd.shape, 1, 2 * rows * width * wd.shape[0],
        (wd.shape[0], rows),
    )
    g_gu = scatter_shard(g_gu)
    dm = plane_gather(dm_own, high)
    all_dm = flat(dm[k] for j in order for k in (j ^ 1, j))
    g_o = grads_call(
        functools.partial(out_grads_kernel, len(pairs), len(all_dm)),
        all_dm, [saved[j][2] for j in order], [], wo.shape, 1,
        2 * rows * width * wo.shape[0],
    )
    g_rows = [g.reshape(shards, -1, width) for g in (g_d, g_o)]
    g_rows = scatter_shard(jnp.concatenate(g_rows, 1).reshape(-1, width))
    g_o = lax.ppermute(g_rows[hidden:], ("replica", "shard"), back)
    g_rows = jnp.concatenate([g_rows[:hidden], g_o], 0)

    das, dqkvs = {}, []
    for j in order:
        (das[j ^ 1], das[j]), dqkv = attn_backward(
            [dm[j ^ 1], dm[j]], saved[j][1], wqkv, wo, pick_o, tables, queries, keys
        )
        dqkvs.append(dqkv)
    g_w = grads_call(
        functools.partial(attn_grads_kernel, len(pairs)),
        [saved[j][0] for j in order], dqkvs, [pick], (width, narrow), 0,
        2 * rows * width * pick.shape[1],
    )
    g_w = scatter_shard(g_w)
    (input_grad,) = finish("back", plane_scatter(das, high), [tokens, d_middle, gain_a], [F32])

    outs = dict(zip(outs, (after(y, *all_dm) for y in outs.values())))
    (block_output,) = finish("output", plane_scatter(outs, high), [middle], [BF16])

    bit = group
    while bit < replicas:
        g_gu, g_rows, g_w = (g + swap(g, bit) for g in (g_gu, g_rows, g_w))
        bit *= 2

    def blocks(g):
        got = plane_gather(g, high)
        return [got[j] for j in range(group)]

    here = place.reshape(1)
    gate_grad, up_grad, gain_terms = spread_wide(here, blocks(g_gu), w_gate, w_up, shards)
    mlp_gain_grad = jnp.sum(gain_terms, 1) / mlp_gain.astype(F32)
    down_grad, out_grad = spread_rows(here, blocks(g_rows), hidden)
    cuts = (queries * HEAD_DIM, (queries + keys) * HEAD_DIM)
    query_grad, key_grad, value_grad, gain_terms = spread_attn(
        here, blocks(g_w), (w_query, w_key, w_value), cuts
    )
    attn_gain_grad = gain_terms[:, 0] / attn_gain.astype(F32)
    return (
        block_output,
        input_grad,
        attn_gain_grad,
        query_grad,
        key_grad,
        value_grad,
        out_grad,
        mlp_gain_grad,
        gate_grad,
        up_grad,
        down_grad,
    )


def solution(mesh):
    tokens, weights, gains = P(("replica", "shard"), None), P("shard", None), P("shard")
    return jax.shard_map(
        layer,
        mesh=mesh,
        in_specs=(tokens, tokens, gains, weights, weights, weights, weights, gains, weights, weights, weights),
        out_specs=(tokens, tokens, gains, weights, weights, weights, weights, gains, weights, weights, weights),
        check_vma=False,
    )
```

```python
import functools
import math

import jax
import jax.numpy as jnp
from jax import lax
from jax.experimental import pallas as pl
from jax.experimental.pallas import tpu as pltpu
from jax.sharding import PartitionSpec as P


HEAD_DIM = 96
LANES = 128
NORM_EPS = 1e-05
ROPE_BASE = 100000.0
VMEM_BYTES = 40 * 1024 * 1024
MLP_VMEM_BYTES = 40 * 1024 * 1024
GRADS_VMEM_BYTES = 60 * 1024 * 1024
F32 = jnp.float32
BF16 = jnp.bfloat16


def nn(left, right):
    return jnp.dot(left, right, preferred_element_type=F32)


def nt(left, right):
    return lax.dot_general(left, right, (((1,), (1,)), ((), ())), preferred_element_type=F32)


def tn(left, right):
    return lax.dot_general(left, right, (((0,), (0,)), ((), ())), preferred_element_type=F32)


def swap(x, bit):
    size = lax.axis_size("replica")
    return lax.ppermute(x, "replica", [(i, i ^ bit) for i in range(size)])


def plane_gather(x, high):
    cut = x.shape[0] // 2
    got = {0: (x,)}
    if len(high) == 2:
        a, b = high
        from_a, from_b = swap(x, a), swap(x, b)
        got[a], got[b] = (from_a,), (from_b,)
        got[1] = (swap(x, 1),)
        far = swap(from_b[:cut], a), swap(from_a[cut:], b)
        got[a ^ b] = far
    else:
        for bit in high:
            more = {j ^ bit: tuple(swap(p, bit) for p in got[j]) for j in list(got)}
            got.update(more)
    for j in list(got):
        if j ^ 1 not in got:
            got[j ^ 1] = tuple(swap(p, 1) for p in got[j])
    return got


def plane_scatter(parts, high):
    cut = parts[0].shape[0] // 2
    even = [j for j in parts if j % 2 == 0]
    both = {j: (parts[j], swap(parts[j ^ 1], 1)) for j in even}

    def total(terms, rows):
        return sum(t[rows].astype(F32) for t in terms).astype(BF16)

    low, top, full = slice(0, cut), slice(cut, 2 * cut), slice(0, 2 * cut)
    if len(high) == 2:
        a, b = high
        far, near_a, near_b = both[a ^ b], both[a], both[b]
        via_a = swap(total(far, low), a)
        via_b = swap(total(far, top), b)
        first_a = swap(total(near_a, low), a)
        first_b = swap(total(near_b, top), b)
        last_a = (total32(near_a, top) + via_b.astype(F32)).astype(BF16)
        last_b = (total32(near_b, low) + via_a.astype(F32)).astype(BF16)
        last_a, last_b = swap(last_a, a), swap(last_b, b)
        return both[0], (first_a, last_b), (last_a, first_b)
    sums = {j: total(both[j], full) for j in even}
    for bit in reversed(high):
        sums = {j: total((sums[j], swap(sums[j ^ bit], bit)), full) for j in sums if not j & bit}
    return (sums[0],), (), ()


def total32(terms, rows):
    return sum(t[rows].astype(F32) for t in terms)


def flat(terms):
    return [y for group in terms for y in group]


def call(kernel, inputs, outputs, scratch=(), flops=0, exps=0, limit=VMEM_BYTES):
    outputs = [jax.ShapeDtypeStruct(shape, kind) for shape, kind in outputs]
    moved = sum(math.prod(y.shape) * y.dtype.itemsize for y in [*inputs, *outputs])
    return pl.pallas_call(
        kernel,
        out_shape=outputs,
        scratch_shapes=list(scratch),
        compiler_params=pltpu.CompilerParams(vmem_limit_bytes=limit),
        cost_estimate=pl.CostEstimate(flops=flops, bytes_accessed=moved, transcendentals=exps),
    )(*inputs)


def rope_tables(length):
    half = HEAD_DIM // 2
    position = jnp.arange(length, dtype=F32)
    freqs = jnp.power(ROPE_BASE, -jnp.arange(half, dtype=F32) / half)
    angles = position[:, None] * freqs[None, :]
    pad = ((0, 0), (0, LANES // 2 - half))
    cosine, sine = jnp.pad(jnp.cos(angles), pad), jnp.pad(jnp.sin(angles), pad)
    return jnp.concatenate([cosine, cosine], 1), jnp.concatenate([-sine, sine], 1)


def turn(values, cosine, sine):
    return values * cosine + pltpu.roll(values, LANES // 2, 1) * sine


def turn_back(values, cosine, sine):
    return values * cosine - pltpu.roll(values, LANES // 2, 1) * sine


def head_probs(query, key):
    length = query.shape[0]
    scores = nt(query, key) * HEAD_DIM ** (-0.5)
    rows = lax.broadcasted_iota(jnp.int32, (length, length), 0)
    columns = lax.broadcasted_iota(jnp.int32, (length, length), 1)
    scores = jnp.where(rows >= columns, scores, -jnp.inf)
    raised = jnp.exp(scores - jnp.max(scores, -1, keepdims=True))
    return raised / jnp.sum(raised, -1, keepdims=True)


def head_span(k):
    return slice(k * LANES, (k + 1) * LANES)


def load(refs):
    parts = [r[...] for r in refs]
    return parts[0] if len(parts) == 1 else jnp.concatenate(parts, 0)


def take(refs, counts):
    refs, out = list(refs), []
    for count in counts:
        out.append(refs[:count])
        refs = refs[count:]
    return out, refs


def inverse_rms(rows):
    return lax.rsqrt(jnp.mean(rows * rows, -1, keepdims=True) + NORM_EPS)


def attn_forward_kernel(queries, keys, counts, *refs):
    blocks, rest = take(refs, counts)
    gain_ref, w_ref, wo_ref, pick_ref, cos_ref, sin_ref = rest[:6]
    parts, (h_ref, qkv_ref, o_ref) = rest[6 : 6 + len(blocks)], rest[6 + len(blocks) :]
    cosine, sine = cos_ref[...], sin_ref[...]
    length = cosine.shape[0]
    for n, block in enumerate(blocks):
        at_rows = slice(n * length, (n + 1) * length)
        x = load(block).astype(F32)
        normed = (x * inverse_rms(x) * gain_ref[...]).astype(BF16)
        h_ref[at_rows, :] = normed
        mixed = nn(normed, w_ref[...])
        made = []
        for k in range(queries + 2 * keys):
            piece = mixed[:, head_span(k)]
            made.append((turn(piece, cosine, sine) if k < queries + keys else piece).astype(BF16))
            qkv_ref[at_rows, head_span(k)] = made[k]
        heads = []
        for k in range(queries):
            at = k * keys // queries
            probs = head_probs(made[k], made[queries + at])
            heads.append(nn(probs.astype(BF16), made[queries + keys + at]).astype(BF16))
        heads = nn(jnp.concatenate(heads, 1), pick_ref[...]).astype(BF16)
        o_ref[at_rows, :] = heads
        parts[n][...] = nn(heads, wo_ref[...]).astype(BF16)


def attn_forward(blocks, gain, w, wo, pick, tables, queries, keys):
    counts = [len(b) for b in blocks]
    length, width = tables[0].shape[0], w.shape[0]
    rows = length * len(blocks)
    *parts, h, qkv, o = call(
        functools.partial(attn_forward_kernel, queries, keys, counts),
        [*flat(blocks), gain, w, wo, pick, *tables],
        [((length, width), BF16)] * len(blocks)
        + [((rows, width), BF16), ((rows, w.shape[1]), BF16), ((rows, wo.shape[0]), BF16)],
        flops=2 * rows * width * (w.shape[1] + wo.shape[0]) + 4 * rows * length * queries * LANES,
        exps=rows * length * queries,
    )
    return parts, (h, qkv, o)


def mlp_kernel(counts, *refs):
    blocks, rest = take(refs, counts)
    half = len(blocks) // 2
    wgu_ref, wd_ref = rest[:2]
    outs, dhs = rest[2 : 2 + half], rest[2 + half : 2 + 2 * half]
    dgu_ref, at_ref, h_ref, c_ref, a_ref = rest[2 + 2 * half :]
    length = outs[0].shape[0]
    for n in range(half):
        h_ref[n * length : (n + 1) * length, :] = load(blocks[n])
        c_ref[n * length : (n + 1) * length, :] = load(blocks[half + n])
    hidden, width = wd_ref.shape
    tile = min(hidden, 2 * LANES)

    def first(k, carry):
        at = pl.multiple_of(k * tile, tile)
        over = pl.multiple_of(hidden + k * tile, tile)
        gate = nn(h_ref[...], wgu_ref[:, pl.ds(at, tile)])
        upward = nn(h_ref[...], wgu_ref[:, pl.ds(over, tile)])
        d_active = nt(c_ref[...], wd_ref[pl.ds(at, tile), :])
        sigmoid = jax.nn.sigmoid(gate)
        silu = gate * sigmoid
        active = (silu * upward).astype(BF16)
        a_ref[:, pl.ds(at, tile)] = active
        at_ref[pl.ds(at, tile), :] = active.T
        d_gate = d_active * upward * sigmoid * (1.0 + gate * (1.0 - sigmoid))
        dgu_ref[:, pl.ds(at, tile)] = d_gate.astype(BF16)
        dgu_ref[:, pl.ds(over, tile)] = (d_active * silu).astype(BF16)
        return carry

    lax.fori_loop(0, hidden // tile, first, 0)
    wtile = 2 * LANES

    def second(k, carry):
        at = pl.ds(pl.multiple_of(k * wtile, wtile), wtile)
        d_normed = nt(dgu_ref[...], wgu_ref[at, :]).astype(BF16)
        output = nn(a_ref[...], wd_ref[:, at]).astype(BF16)
        for n in range(half):
            dhs[n][:, at] = d_normed[n * length : (n + 1) * length]
            outs[n][:, at] = output[n * length : (n + 1) * length]
        return carry

    lax.fori_loop(0, width // wtile, second, 0)


def mlp_both(h, c, wgu, wd):
    counts = [len(b) for b in [*h, *c]]
    half = len(h)
    length, width, hidden = sum(p.shape[0] for p in h[0]), wgu.shape[0], wd.shape[0]
    rows = half * length
    made = call(
        functools.partial(mlp_kernel, counts),
        [*flat(h), *flat(c), wgu, wd],
        [((length, width), BF16)] * (2 * half)
        + [((rows, 2 * hidden), BF16), ((hidden, rows), BF16)],
        scratch=[
            pltpu.VMEM((rows, width), BF16),
            pltpu.VMEM((rows, width), BF16),
            pltpu.VMEM((rows, hidden), BF16),
        ],
        flops=12 * rows * width * hidden,
        exps=rows * hidden,
        limit=MLP_VMEM_BYTES,
    )
    return made[:half], made[half : 2 * half], made[2 * half], made[2 * half + 1]


def stack_rows(parts, out):
    at = 0
    for part in parts:
        out[at : at + part.shape[0], :] = part[...]
        at += part.shape[0]


def wide_grads_kernel(count, pieces, *refs):
    hs, ds, (g_ref, h_all, d_all) = refs[:pieces], refs[pieces : pieces + count], refs[pieces + count :]

    @pl.when(pl.program_id(0) == 0)
    def _():
        stack_rows(ds, d_all)

    stack_rows(hs, h_all)
    g_ref[...] = tn(h_all[...], d_all[...]).astype(BF16)


def down_grads_kernel(count, pieces, *refs):
    ats, cs, (g_ref, at_all, c_all) = refs[:count], refs[count : count + pieces], refs[count + pieces :]

    @pl.when(pl.program_id(0) == 0)
    def _():
        at = 0
        for across in ats:
            at_all[:, at : at + across.shape[1]] = across[...]
            at += across.shape[1]

    stack_rows(cs, c_all)
    g_ref[...] = nn(at_all[...], c_all[...]).astype(BF16)


def attn_backward_kernel(queries, keys, counts, *refs):
    blocks, rest = take(refs, counts)
    qkv_ref, w_ref, wo_ref, pick_ref, cos_ref, sin_ref = rest[:6]
    dhs, (dqkv_ref,) = rest[6 : 6 + len(blocks)], rest[6 + len(blocks) :]
    cosine, sine = cos_ref[...], sin_ref[...]
    length = cosine.shape[0]
    each = queries // keys
    scale = HEAD_DIM ** (-0.5)
    for n, block in enumerate(blocks):
        at_rows = slice(n * length, (n + 1) * length)
        d_heads = nt(load(block), wo_ref[...]).astype(BF16)
        d_heads = nt(d_heads, pick_ref[...]).astype(BF16)
        for at in range(keys):
            key = qkv_ref[at_rows, head_span(queries + at)]
            value = qkv_ref[at_rows, head_span(queries + keys + at)]
            d_key, d_value = 0.0, 0.0
            for k in range(at * each, (at + 1) * each):
                query = qkv_ref[at_rows, head_span(k)]
                d_head = d_heads[:, head_span(k)]
                probs = head_probs(query, key)
                d_value += tn(probs.astype(BF16), d_head)
                d_probs = nt(d_head, value)
                delta = jnp.sum(probs * d_probs, -1, keepdims=True)
                d_scores = (probs * (d_probs - delta) * scale).astype(BF16)
                d_query = nn(d_scores, key)
                d_key += tn(d_scores, query)
                dqkv_ref[at_rows, head_span(k)] = turn_back(d_query, cosine, sine).astype(BF16)
            dqkv_ref[at_rows, head_span(queries + at)] = turn_back(d_key, cosine, sine).astype(BF16)
            dqkv_ref[at_rows, head_span(queries + keys + at)] = d_value.astype(BF16)
    wtile = 2 * LANES

    def second(k, carry):
        at = pl.ds(pl.multiple_of(k * wtile, wtile), wtile)
        d_normed = nt(dqkv_ref[...], w_ref[at, :]).astype(BF16)
        for n in range(len(blocks)):
            dhs[n][:, at] = d_normed[n * length : (n + 1) * length]
        return carry

    lax.fori_loop(0, w_ref.shape[0] // wtile, second, 0)


def attn_backward(blocks, qkv, w, wo, pick, tables, queries, keys):
    counts = [len(b) for b in blocks]
    length, width = tables[0].shape[0], w.shape[0]
    rows = length * len(blocks)
    *dhs, dqkv = call(
        functools.partial(attn_backward_kernel, queries, keys, counts),
        [*flat(blocks), qkv, w, wo, pick, *tables],
        [((length, width), BF16)] * len(blocks) + [((rows, w.shape[1]), BF16)],
        flops=2 * rows * width * (w.shape[1] + wo.shape[0]) + 10 * rows * length * queries * LANES,
        exps=rows * length * queries,
    )
    return dhs, dqkv


def attn_grads_kernel(count, *refs):
    hs, ds, pick_ref = refs[:count], refs[count : 2 * count], refs[2 * count]
    g_ref, h_all, d_all = refs[2 * count + 1 :]

    @pl.when(pl.program_id(0) == 0)
    def _():
        stack_rows(ds, d_all)

    stack_rows(hs, h_all)
    grad = tn(h_all[...], d_all[...]).astype(BF16)
    g_ref[...] = nt(grad, pick_ref[...]).astype(BF16)


def out_grads_kernel(count, pieces, *refs):
    os, ms, (g_ref, o_all, m_all) = refs[:count], refs[count : count + pieces], refs[count + pieces :]

    @pl.when(pl.program_id(0) == 0)
    def _():
        stack_rows(os, o_all)

    stack_rows(ms, m_all)
    g_ref[...] = tn(o_all[...], m_all[...]).astype(BF16)


def grads_call(kernel, tiled, fixed, consts, out, along, flops, held=None):
    tile = 2 * LANES
    rows, width = sum(y.shape[0] for y in tiled), tiled[0].shape[1]
    held = held or (rows, fixed[0].shape[1])
    whole = lambda y: pl.BlockSpec(y.shape, lambda i: (0, 0), pipeline_mode=pl.Buffered(1))
    part = lambda y: pl.BlockSpec((y.shape[0], tile), lambda i: (0, i))
    moving, resident = pltpu.VMEM((rows, tile), BF16), pltpu.VMEM(held, BF16)
    if along == 0:
        inputs = [*tiled, *fixed, *consts]
        specs = [part(y) for y in tiled] + [whole(y) for y in [*fixed, *consts]]
        out_spec = pl.BlockSpec((tile, out[1]), lambda i: (i, 0))
        scratch = [moving, resident]
    else:
        inputs, specs = [*fixed, *tiled], [whole(y) for y in fixed] + [part(y) for y in tiled]
        out_spec = pl.BlockSpec((out[0], tile), lambda i: (0, i))
        scratch = [resident, moving]
    return pl.pallas_call(
        kernel,
        grid=(width // tile,),
        in_specs=specs,
        out_specs=out_spec,
        out_shape=jax.ShapeDtypeStruct(out, BF16),
        scratch_shapes=scratch,
        compiler_params=pltpu.CompilerParams(
            dimension_semantics=("arbitrary",), vmem_limit_bytes=GRADS_VMEM_BYTES
        ),
        cost_estimate=pl.CostEstimate(flops=flops, bytes_accessed=3 * rows * width, transcendentals=0),
    )(*inputs)


def finish_kernel(kind, counts, *refs):
    (whole, low, top), rest = take(refs, counts)
    length = whole[0].shape[0]
    cut = length // 2
    halves = []
    for half, extra in ((0, low), (1, top)):
        rows = slice(half * cut, (half + 1) * cut)
        total = sum(t[rows, :].astype(F32) for t in whole)
        halves.append(sum((t[...].astype(F32) for t in extra), total))
    total = jnp.concatenate(halves, 0)
    if kind == "middle":
        x_ref, gain_ref, middle_ref, h_ref = rest
        middle = x_ref[...].astype(F32) + total
        middle_ref[...] = middle
        h_ref[...] = (middle * inverse_rms(middle) * gain_ref[...]).astype(BF16)
    elif kind == "output":
        middle_ref, out_ref = rest
        out_ref[...] = (middle_ref[...] + total).astype(BF16)
    else:
        rows_ref, base_ref, gain_ref, *outs = rest
        rows = rows_ref[...].astype(F32)
        inverse = inverse_rms(rows)
        scaled = total * gain_ref[...]
        mean = jnp.mean(scaled * rows, -1, keepdims=True)
        made = base_ref[...].astype(F32) + inverse * scaled - rows * inverse**3 * mean
        for out in outs:
            out[...] = made.astype(out.dtype)


def finish(kind, terms, extras, kinds):
    counts = [len(t) for t in terms]
    shape = terms[0][0].shape
    return call(
        functools.partial(finish_kernel, kind, counts),
        [*flat(terms), *extras],
        [(shape, k) for k in kinds],
        flops=16 * math.prod(shape),
    )


def spread_wide_kernel(counts, at_ref, *refs):
    blocks, (wg_ref, wu_ref, gate_out, up_out, gain_out) = take(refs, counts)
    j, part = pl.program_id(0), pl.program_id(1)
    tile, parts = gate_out.shape[1], pl.num_programs(1)

    @pl.when((j == 0) & (part == 0))
    def _():
        gain_out[...] = jnp.zeros_like(gain_out)

    here = pl.multiple_of(part * tile, tile)
    over = pl.multiple_of((parts + part) * tile, tile)
    for k, block in enumerate(blocks):

        @pl.when(j == k)
        def _(block=block):
            at = 0
            for piece in block:
                rows = slice(at, at + piece.shape[0])
                gate_out[rows, :] = piece[:, pl.ds(here, tile)].astype(F32)
                up_out[rows, :] = piece[:, pl.ds(over, tile)].astype(F32)
                at += piece.shape[0]

    gain_out[...] += gate_out[...] * wg_ref[...].astype(F32) + up_out[...] * wu_ref[...].astype(F32)


def spread_wide(at, blocks, w_gate, w_up, parts):
    counts, pieces, count = [len(b) for b in blocks], flat(blocks), len(blocks)
    width, total = w_gate.shape
    tile = total // count // parts
    columns = pl.BlockSpec((width, tile), lambda j, s, at: (0, s * count + (j ^ at[0])))
    return pl.pallas_call(
        functools.partial(spread_wide_kernel, counts),
        grid_spec=pltpu.PrefetchScalarGridSpec(
            num_scalar_prefetch=1,
            grid=(count, parts),
            in_specs=[
                pl.BlockSpec(p.shape, lambda j, s, at: (0, 0), pipeline_mode=pl.Buffered(1))
                for p in pieces
            ]
            + [columns, columns],
            out_specs=[columns, columns, pl.BlockSpec((width, tile), lambda j, s, at: (0, 0))],
        ),
        out_shape=[
            jax.ShapeDtypeStruct((width, total), F32),
            jax.ShapeDtypeStruct((width, total), F32),
            jax.ShapeDtypeStruct((width, tile), F32),
        ],
        compiler_params=pltpu.CompilerParams(
            dimension_semantics=("arbitrary", "arbitrary"), vmem_limit_bytes=VMEM_BYTES
        ),
        cost_estimate=pl.CostEstimate(flops=0, bytes_accessed=16 * width * total, transcendentals=0),
        name="sw",
    )(at, *pieces, w_gate, w_up)


def spread_rows_kernel(counts, at_ref, *refs):
    blocks, (down_out, o_out) = take(refs, counts)
    j, short = pl.program_id(0), down_out.shape[0]
    for k, block in enumerate(blocks):

        @pl.when(j == k)
        def _(block=block):
            values = load(block).astype(F32)
            down_out[...] = values[:short]
            o_out[...] = values[short:]


def spread_rows(at, blocks, short):
    counts, pieces, count = [len(b) for b in blocks], flat(blocks), len(blocks)
    rows, width = sum(p.shape[0] for p in blocks[0]), pieces[0].shape[1]
    place = lambda j, at: (j ^ at[0], 0)
    return pl.pallas_call(
        functools.partial(spread_rows_kernel, counts),
        grid_spec=pltpu.PrefetchScalarGridSpec(
            num_scalar_prefetch=1,
            grid=(count,),
            in_specs=[
                pl.BlockSpec(p.shape, lambda j, at: (0, 0), pipeline_mode=pl.Buffered(1))
                for p in pieces
            ],
            out_specs=[pl.BlockSpec((short, width), place), pl.BlockSpec((rows - short, width), place)],
        ),
        out_shape=[
            jax.ShapeDtypeStruct((count * short, width), F32),
            jax.ShapeDtypeStruct((count * (rows - short), width), F32),
        ],
        compiler_params=pltpu.CompilerParams(
            dimension_semantics=("arbitrary",), vmem_limit_bytes=VMEM_BYTES
        ),
        cost_estimate=pl.CostEstimate(flops=0, bytes_accessed=6 * count * rows * width, transcendentals=0),
        name="sr",
    )(at, *pieces)


def spread_attn_kernel(counts, count, cuts, at_ref, *refs):
    blocks, rest = take(refs, counts)
    (wq_ref, wk_ref, wv_ref), (q_out, k_out, v_out, gain_out, stack) = rest[:3], rest[3:]
    step = pl.program_id(0)

    @pl.when(step == 0)
    def _():
        gain_out[...] = jnp.zeros_like(gain_out)
        for j, block in enumerate(blocks):
            stack[j ^ at_ref[0]] = load(block)

    total = 0.0
    spans = ((0, cuts[0]), (cuts[0], cuts[1]), (cuts[1], stack.shape[2]))
    held = [stack[step * count + i].astype(F32) for i in range(count)]
    for (low, high), out, w_ref in zip(spans, (q_out, k_out, v_out), (wq_ref, wk_ref, wv_ref)):
        made = jnp.concatenate([b[:, low:high] for b in held], 1)
        out[...] = made
        total += jnp.sum(made * w_ref[...].astype(F32), 1, keepdims=True)
    gain_out[...] += total


def spread_attn(at, blocks, weights, cuts):
    counts, pieces, group = [len(b) for b in blocks], flat(blocks), len(blocks)
    slab, narrow = weights[0].shape[0], pieces[0].shape[1]
    count = math.gcd(group, LANES // math.gcd(LANES, HEAD_DIM))
    widths = (cuts[0], cuts[1] - cuts[0], narrow - cuts[1])
    columns = [pl.BlockSpec((slab, count * w), lambda p, at: (0, p)) for w in widths]
    return pl.pallas_call(
        functools.partial(spread_attn_kernel, counts, count, cuts),
        grid_spec=pltpu.PrefetchScalarGridSpec(
            num_scalar_prefetch=1,
            grid=(group // count,),
            in_specs=[
                pl.BlockSpec(p.shape, lambda p_, at: (0, 0), pipeline_mode=pl.Buffered(1))
                for p in pieces
            ]
            + columns,
            out_specs=columns + [pl.BlockSpec((slab, 1), lambda p, at: (0, 0))],
            scratch_shapes=[pltpu.VMEM((group, slab, narrow), BF16)],
        ),
        out_shape=[jax.ShapeDtypeStruct((slab, group * w), F32) for w in widths]
        + [jax.ShapeDtypeStruct((slab, 1), F32)],
        compiler_params=pltpu.CompilerParams(
            dimension_semantics=("arbitrary",), vmem_limit_bytes=VMEM_BYTES
        ),
        cost_estimate=pl.CostEstimate(
            flops=0, bytes_accessed=8 * group * slab * narrow, transcendentals=0
        ),
        name="sa",
    )(at, *pieces, *weights)


def pick_wide_kernel(parts, at_ref, gate_ref, up_ref, out_ref):
    @pl.when(pl.program_id(0) < parts)
    def _():
        out_ref[...] = gate_ref[...]

    @pl.when(pl.program_id(0) >= parts)
    def _():
        out_ref[...] = up_ref[...]


def pick_wide(at, w_gate, w_up, group, parts):
    width, total = w_gate.shape
    tile = total // group // parts
    columns = pl.BlockSpec((width, tile), lambda k, at: (0, lax.rem(k, parts) * group + at[0]))
    return pl.pallas_call(
        functools.partial(pick_wide_kernel, parts),
        grid_spec=pltpu.PrefetchScalarGridSpec(
            num_scalar_prefetch=1,
            grid=(2 * parts,),
            in_specs=[columns, columns],
            out_specs=pl.BlockSpec((width, tile), lambda k, at: (0, k)),
        ),
        out_shape=jax.ShapeDtypeStruct((width, 2 * parts * tile), BF16),
        compiler_params=pltpu.CompilerParams(dimension_semantics=("arbitrary",)),
        cost_estimate=pl.CostEstimate(
            flops=0, bytes_accessed=12 * width * parts * tile, transcendentals=0
        ),
        name="pick",
    )(at, w_gate, w_up)


def head_columns(queries, keys):
    half, lane = HEAD_DIM // 2, jnp.arange(LANES)
    place = lane % (LANES // 2)
    turned = jnp.where(place < half, (lane // (LANES // 2)) * half + place, -1)
    plain = jnp.where(lane < HEAD_DIM, lane, -1)
    columns = []
    for k in range(queries + 2 * keys):
        inside = turned if k < queries + keys else plain
        columns.append(jnp.where(inside >= 0, inside + k * HEAD_DIM, -1))
    return jnp.concatenate(columns)


def gather_shard(x):
    return lax.all_gather(x, "shard", axis=0, tiled=True)


def scatter_shard(x):
    return lax.psum_scatter(x, "shard", scatter_dimension=0, tiled=True)


def after(x, *others):
    return lax.optimization_barrier((x, *others))[0]


def layer(
    tokens, cotangent, attn_gain, w_query, w_key, w_value, w_out, mlp_gain, w_gate, w_up, w_down
):
    replicas, shards = lax.axis_size("replica"), lax.axis_size("shard")
    length, width = tokens.shape
    slab = w_query.shape[0]
    kv_heads = w_key.shape[1] // HEAD_DIM
    group = math.gcd(replicas, kv_heads)
    keys = kv_heads // group
    queries = w_query.shape[1] // HEAD_DIM // group
    high = [1 << k for k in range(1, group.bit_length() - 1)]
    place = lax.axis_index("replica") % group
    hidden = w_down.shape[0] // group
    narrow = (queries + 2 * keys) * HEAD_DIM

    x = plane_gather(tokens, high)

    wq = lax.dynamic_slice_in_dim(w_query, place * queries * HEAD_DIM, queries * HEAD_DIM, 1)
    wk = lax.dynamic_slice_in_dim(w_key, place * keys * HEAD_DIM, keys * HEAD_DIM, 1)
    wv = lax.dynamic_slice_in_dim(w_value, place * keys * HEAD_DIM, keys * HEAD_DIM, 1)
    spare = 16
    gain_rows = -(-slab // narrow)
    gains = jnp.stack([attn_gain, mlp_gain])
    gains = jnp.pad(gains, ((0, 0), (0, gain_rows * narrow - slab))).reshape(2 * gain_rows, narrow)
    gains = jnp.pad(gains, ((0, spare - 2 * gain_rows), (0, 0)))
    sent = jnp.concatenate([jnp.concatenate([wq, wk, wv], 1), gains], 0)
    both = gather_shard(sent).reshape(shards, slab + spare, narrow)
    w_out, w_gate_s, w_up_s, w_down_s, _ = lax.optimization_barrier((w_out, w_gate, w_up, w_down, sent))

    turns = group // shards
    chunk = w_out.shape[0] // group
    mine = lax.dynamic_slice_in_dim(w_out, place * chunk, chunk, 0)
    routes = []
    for turn_by in range(shards):
        route = []
        for i in range(replicas):
            base, q = i - i % group, i % group
            for z in range(shards):
                to = (base + z * turns + q // shards) * shards + (q + turn_by) % shards
                route.append((i * shards + z, to))
        routes.append(route)
    back = [(b, a) for a, b in routes[0]]
    came = []
    for route in routes:
        came.append(lax.ppermute(mine, ("replica", "shard"), route))
    here = lax.axis_index("shard")
    came = jnp.stack(came)[(here - jnp.arange(shards)) % shards]
    wo = came.reshape(shards * chunk, width)

    columns = head_columns(queries, keys)
    pick = (jnp.arange(narrow)[:, None] == columns[None, :]).astype(BF16)
    wqkv = nn(both[:, :slab].reshape(width, narrow), pick).astype(BF16)
    gains = both[:, slab : slab + 2 * gain_rows].reshape(shards, 2, gain_rows * narrow)[:, :, :slab]
    gains = jnp.moveaxis(gains, 1, 0).reshape(2, 1, width).astype(F32)
    gain_a, gain_m = gains[0], gains[1]
    lanes = jnp.arange(queries * LANES)
    heads = (lanes // LANES) * HEAD_DIM + lanes % LANES
    heads = jnp.where(lanes % LANES < HEAD_DIM, heads, -1)
    pick_o = (jnp.arange(queries * HEAD_DIM)[None, :] == heads[:, None]).astype(BF16)

    wgu = pick_wide(place.reshape(1), w_gate_s, w_up_s, group, shards)
    wd = lax.dynamic_slice_in_dim(w_down_s, place * hidden, hidden, 0)
    wgu = gather_shard(wgu)
    wd = gather_shard(wd)

    c = plane_gather(after(cotangent, *x[high[0]], *x[high[-1]]), high)

    pairs = [j for j in sorted(x, reverse=True) if j % 2 == 0]
    tables = rope_tables(length)
    parts, saved = {}, {}
    for j in pairs:
        (parts[j ^ 1], parts[j]), saved[j] = attn_forward(
            [x[j ^ 1], x[j]], gain_a, wqkv, wo, pick_o, tables, queries, keys
        )
    middle, h_own = finish("middle", plane_scatter(parts, high), [tokens, gain_m], [F32, BF16])
    h = plane_gather(h_own, high)

    order = list(reversed(pairs))
    order = order[:-2] + [order[-1], order[-2]] if len(order) > 2 else order
    outs, dhs, dgus, acrosses = {}, {}, [], []
    for j in order:
        (outs[j ^ 1], outs[j]), (dhs[j ^ 1], dhs[j]), dgu, across = mlp_both(
            [h[j ^ 1], h[j]], [c[j ^ 1], c[j]], wgu, wd
        )
        dgus.append(dgu)
        acrosses.append(across)
    d_middle, dm_own = finish(
        "back", plane_scatter(dhs, high), [middle, cotangent, gain_m], [F32, BF16]
    )
    all_h = flat(h[k] for j in order for k in (j ^ 1, j))
    all_c = flat(c[k] for j in order for k in (j ^ 1, j))
    rows = group * length
    g_gu = grads_call(
        functools.partial(wide_grads_kernel, len(dgus), len(all_h)),
        all_h, dgus, [], wgu.shape, 0, 2 * rows * width * wgu.shape[1],
    )
    g_d = grads_call(
        functools.partial(down_grads_kernel, len(acrosses), len(all_c)),
        all_c, acrosses, [], wd.shape, 1, 2 * rows * width * wd.shape[0],
        (wd.shape[0], rows),
    )
    g_gu = scatter_shard(g_gu)
    dm = plane_gather(dm_own, high)
    all_dm = flat(dm[k] for j in order for k in (j ^ 1, j))
    g_o = grads_call(
        functools.partial(out_grads_kernel, len(pairs), len(all_dm)),
        all_dm, [saved[j][2] for j in order], [], wo.shape, 1,
        2 * rows * width * wo.shape[0],
    )
    g_rows = [g.reshape(shards, -1, width) for g in (g_d, g_o)]
    g_rows = scatter_shard(jnp.concatenate(g_rows, 1).reshape(-1, width))
    g_o = lax.ppermute(g_rows[hidden:], ("replica", "shard"), back)
    g_rows = jnp.concatenate([g_rows[:hidden], g_o], 0)

    das, dqkvs = {}, []
    for j in order:
        (das[j ^ 1], das[j]), dqkv = attn_backward(
            [dm[j ^ 1], dm[j]], saved[j][1], wqkv, wo, pick_o, tables, queries, keys
        )
        dqkvs.append(dqkv)
    g_w = grads_call(
        functools.partial(attn_grads_kernel, len(pairs)),
        [saved[j][0] for j in order], dqkvs, [pick], (width, narrow), 0,
        2 * rows * width * pick.shape[1],
    )
    g_w = scatter_shard(g_w)
    (input_grad,) = finish("back", plane_scatter(das, high), [tokens, d_middle, gain_a], [F32])

    outs = dict(zip(outs, (after(y, *all_dm) for y in outs.values())))
    (block_output,) = finish("output", plane_scatter(outs, high), [middle], [BF16])

    bit = group
    while bit < replicas:
        g_gu, g_rows, g_w = (g + swap(g, bit) for g in (g_gu, g_rows, g_w))
        bit *= 2

    def blocks(g):
        got = plane_gather(g, high)
        return [got[j] for j in range(group)]

    here = place.reshape(1)
    gate_grad, up_grad, gain_terms = spread_wide(here, blocks(g_gu), w_gate, w_up, shards)
    mlp_gain_grad = jnp.sum(gain_terms, 1) / mlp_gain.astype(F32)
    down_grad, out_grad = spread_rows(here, blocks(g_rows), hidden)
    cuts = (queries * HEAD_DIM, (queries + keys) * HEAD_DIM)
    query_grad, key_grad, value_grad, gain_terms = spread_attn(
        here, blocks(g_w), (w_query, w_key, w_value), cuts
    )
    attn_gain_grad = gain_terms[:, 0] / attn_gain.astype(F32)
    return (
        block_output,
        input_grad,
        attn_gain_grad,
        query_grad,
        key_grad,
        value_grad,
        out_grad,
        mlp_gain_grad,
        gate_grad,
        up_grad,
        down_grad,
    )


def solution(mesh):
    tokens, weights, gains = P(("replica", "shard"), None), P("shard", None), P("shard")
    return jax.shard_map(
        layer,
        mesh=mesh,
        in_specs=(tokens, tokens, gains, weights, weights, weights, weights, gains, weights, weights, weights),
        out_specs=(tokens, tokens, gains, weights, weights, weights, weights, gains, weights, weights, weights),
        check_vma=False,
    )
```

```python
import functools
import math

import jax
import jax.numpy as jnp
from jax import lax
from jax.experimental import pallas as pl
from jax.experimental.pallas import tpu as pltpu
from jax.sharding import PartitionSpec as P


HEAD_DIM = 96
LANES = 128
NORM_EPS = 1e-05
ROPE_BASE = 100000.0
VMEM_BYTES = 40 * 1024 * 1024
MLP_VMEM_BYTES = 40 * 1024 * 1024
GRADS_VMEM_BYTES = 60 * 1024 * 1024
F32 = jnp.float32
BF16 = jnp.bfloat16


def nn(left, right):
    return jnp.dot(left, right, preferred_element_type=F32)


def nt(left, right):
    return lax.dot_general(left, right, (((1,), (1,)), ((), ())), preferred_element_type=F32)


def tn(left, right):
    return lax.dot_general(left, right, (((0,), (0,)), ((), ())), preferred_element_type=F32)


def swap(x, bit):
    size = lax.axis_size("replica")
    return lax.ppermute(x, "replica", [(i, i ^ bit) for i in range(size)])


def plane_gather(x, high):
    cut = x.shape[0] // 2
    got = {0: (x,)}
    if len(high) == 2:
        a, b = high
        from_a, from_b = swap(x, a), swap(x, b)
        got[a], got[b] = (from_a,), (from_b,)
        got[1] = (swap(x, 1),)
        far = swap(from_b[:cut], a), swap(from_a[cut:], b)
        got[a ^ b] = far
    else:
        for bit in high:
            more = {j ^ bit: tuple(swap(p, bit) for p in got[j]) for j in list(got)}
            got.update(more)
    for j in list(got):
        if j ^ 1 not in got:
            got[j ^ 1] = tuple(swap(p, 1) for p in got[j])
    return got


def plane_scatter(parts, high):
    cut = parts[0].shape[0] // 2
    even = [j for j in parts if j % 2 == 0]
    both = {j: (parts[j], swap(parts[j ^ 1], 1)) for j in even}

    def total(terms, rows):
        return sum(t[rows].astype(F32) for t in terms).astype(BF16)

    low, top, full = slice(0, cut), slice(cut, 2 * cut), slice(0, 2 * cut)
    if len(high) == 2:
        a, b = high
        far, near_a, near_b = both[a ^ b], both[a], both[b]
        via_a = swap(total(far, low), a)
        via_b = swap(total(far, top), b)
        first_a = swap(total(near_a, low), a)
        first_b = swap(total(near_b, top), b)
        last_a = (total32(near_a, top) + via_b.astype(F32)).astype(BF16)
        last_b = (total32(near_b, low) + via_a.astype(F32)).astype(BF16)
        last_a, last_b = swap(last_a, a), swap(last_b, b)
        return both[0], (first_a, last_b), (last_a, first_b)
    sums = {j: total(both[j], full) for j in even}
    for bit in reversed(high):
        sums = {j: total((sums[j], swap(sums[j ^ bit], bit)), full) for j in sums if not j & bit}
    return (sums[0],), (), ()


def total32(terms, rows):
    return sum(t[rows].astype(F32) for t in terms)


def flat(terms):
    return [y for group in terms for y in group]


def call(kernel, inputs, outputs, scratch=(), flops=0, exps=0, limit=VMEM_BYTES):
    outputs = [jax.ShapeDtypeStruct(shape, kind) for shape, kind in outputs]
    moved = sum(math.prod(y.shape) * y.dtype.itemsize for y in [*inputs, *outputs])
    return pl.pallas_call(
        kernel,
        out_shape=outputs,
        scratch_shapes=list(scratch),
        compiler_params=pltpu.CompilerParams(vmem_limit_bytes=limit),
        cost_estimate=pl.CostEstimate(flops=flops, bytes_accessed=moved, transcendentals=exps),
    )(*inputs)


def rope_tables(length):
    half = HEAD_DIM // 2
    position = jnp.arange(length, dtype=F32)
    freqs = jnp.power(ROPE_BASE, -jnp.arange(half, dtype=F32) / half)
    angles = position[:, None] * freqs[None, :]
    pad = ((0, 0), (0, LANES // 2 - half))
    cosine, sine = jnp.pad(jnp.cos(angles), pad), jnp.pad(jnp.sin(angles), pad)
    return jnp.concatenate([cosine, cosine], 1), jnp.concatenate([-sine, sine], 1)


def turn(values, cosine, sine):
    return values * cosine + pltpu.roll(values, LANES // 2, 1) * sine


def turn_back(values, cosine, sine):
    return values * cosine - pltpu.roll(values, LANES // 2, 1) * sine


def head_probs(query, key):
    length = query.shape[0]
    scores = nt(query, key) * HEAD_DIM ** (-0.5)
    rows = lax.broadcasted_iota(jnp.int32, (length, length), 0)
    columns = lax.broadcasted_iota(jnp.int32, (length, length), 1)
    scores = jnp.where(rows >= columns, scores, -jnp.inf)
    raised = jnp.exp(scores - jnp.max(scores, -1, keepdims=True))
    return raised / jnp.sum(raised, -1, keepdims=True)


def head_span(k):
    return slice(k * LANES, (k + 1) * LANES)


def load(refs):
    parts = [r[...] for r in refs]
    return parts[0] if len(parts) == 1 else jnp.concatenate(parts, 0)


def take(refs, counts):
    refs, out = list(refs), []
    for count in counts:
        out.append(refs[:count])
        refs = refs[count:]
    return out, refs


def inverse_rms(rows):
    return lax.rsqrt(jnp.mean(rows * rows, -1, keepdims=True) + NORM_EPS)


def attn_forward_kernel(queries, keys, counts, *refs):
    blocks, rest = take(refs, counts)
    gain_ref, w_ref, wo_ref, pick_ref, cos_ref, sin_ref = rest[:6]
    parts, (h_ref, qkv_ref, o_ref) = rest[6 : 6 + len(blocks)], rest[6 + len(blocks) :]
    cosine, sine = cos_ref[...], sin_ref[...]
    length = cosine.shape[0]
    for n, block in enumerate(blocks):
        at_rows = slice(n * length, (n + 1) * length)
        x = load(block).astype(F32)
        normed = (x * inverse_rms(x) * gain_ref[...]).astype(BF16)
        h_ref[at_rows, :] = normed
        mixed = nn(normed, w_ref[...])
        made = []
        for k in range(queries + 2 * keys):
            piece = mixed[:, head_span(k)]
            made.append((turn(piece, cosine, sine) if k < queries + keys else piece).astype(BF16))
            qkv_ref[at_rows, head_span(k)] = made[k]
        heads = []
        for k in range(queries):
            at = k * keys // queries
            probs = head_probs(made[k], made[queries + at])
            heads.append(nn(probs.astype(BF16), made[queries + keys + at]).astype(BF16))
        heads = nn(jnp.concatenate(heads, 1), pick_ref[...]).astype(BF16)
        o_ref[at_rows, :] = heads
        parts[n][...] = nn(heads, wo_ref[...]).astype(BF16)


def attn_forward(blocks, gain, w, wo, pick, tables, queries, keys):
    counts = [len(b) for b in blocks]
    length, width = tables[0].shape[0], w.shape[0]
    rows = length * len(blocks)
    *parts, h, qkv, o = call(
        functools.partial(attn_forward_kernel, queries, keys, counts),
        [*flat(blocks), gain, w, wo, pick, *tables],
        [((length, width), BF16)] * len(blocks)
        + [((rows, width), BF16), ((rows, w.shape[1]), BF16), ((rows, wo.shape[0]), BF16)],
        flops=2 * rows * width * (w.shape[1] + wo.shape[0]) + 4 * rows * length * queries * LANES,
        exps=rows * length * queries,
    )
    return parts, (h, qkv, o)


def mlp_kernel(counts, *refs):
    blocks, rest = take(refs, counts)
    half = len(blocks) // 2
    wgu_ref, wd_ref = rest[:2]
    outs, dhs = rest[2 : 2 + half], rest[2 + half : 2 + 2 * half]
    dgu_ref, at_ref, h_ref, c_ref, a_ref = rest[2 + 2 * half :]
    length = outs[0].shape[0]
    for n in range(half):
        h_ref[n * length : (n + 1) * length, :] = load(blocks[n])
        c_ref[n * length : (n + 1) * length, :] = load(blocks[half + n])
    hidden, width = wd_ref.shape
    tile = min(hidden, 2 * LANES)

    def first(k, carry):
        at = pl.multiple_of(k * tile, tile)
        over = pl.multiple_of(hidden + k * tile, tile)
        gate = nn(h_ref[...], wgu_ref[:, pl.ds(at, tile)])
        upward = nn(h_ref[...], wgu_ref[:, pl.ds(over, tile)])
        d_active = nt(c_ref[...], wd_ref[pl.ds(at, tile), :])
        sigmoid = jax.nn.sigmoid(gate)
        silu = gate * sigmoid
        active = (silu * upward).astype(BF16)
        a_ref[:, pl.ds(at, tile)] = active
        at_ref[pl.ds(at, tile), :] = active.T
        d_gate = d_active * upward * sigmoid * (1.0 + gate * (1.0 - sigmoid))
        dgu_ref[:, pl.ds(at, tile)] = d_gate.astype(BF16)
        dgu_ref[:, pl.ds(over, tile)] = (d_active * silu).astype(BF16)
        return carry

    lax.fori_loop(0, hidden // tile, first, 0)
    wtile = 2 * LANES

    def second(k, carry):
        at = pl.ds(pl.multiple_of(k * wtile, wtile), wtile)
        d_normed = nt(dgu_ref[...], wgu_ref[at, :]).astype(BF16)
        output = nn(a_ref[...], wd_ref[:, at]).astype(BF16)
        for n in range(half):
            dhs[n][:, at] = d_normed[n * length : (n + 1) * length]
            outs[n][:, at] = output[n * length : (n + 1) * length]
        return carry

    lax.fori_loop(0, width // wtile, second, 0)


def mlp_both(h, c, wgu, wd):
    counts = [len(b) for b in [*h, *c]]
    half = len(h)
    length, width, hidden = sum(p.shape[0] for p in h[0]), wgu.shape[0], wd.shape[0]
    rows = half * length
    made = call(
        functools.partial(mlp_kernel, counts),
        [*flat(h), *flat(c), wgu, wd],
        [((length, width), BF16)] * (2 * half)
        + [((rows, 2 * hidden), BF16), ((hidden, rows), BF16)],
        scratch=[
            pltpu.VMEM((rows, width), BF16),
            pltpu.VMEM((rows, width), BF16),
            pltpu.VMEM((rows, hidden), BF16),
        ],
        flops=12 * rows * width * hidden,
        exps=rows * hidden,
        limit=MLP_VMEM_BYTES,
    )
    return made[:half], made[half : 2 * half], made[2 * half], made[2 * half + 1]


def stack_rows(parts, out):
    at = 0
    for part in parts:
        out[at : at + part.shape[0], :] = part[...]
        at += part.shape[0]


def wide_grads_kernel(count, pieces, *refs):
    hs, ds, (g_ref, h_all, d_all) = refs[:pieces], refs[pieces : pieces + count], refs[pieces + count :]

    @pl.when(pl.program_id(0) == 0)
    def _():
        stack_rows(ds, d_all)

    stack_rows(hs, h_all)
    g_ref[...] = tn(h_all[...], d_all[...]).astype(BF16)


def down_grads_kernel(count, pieces, *refs):
    ats, cs, (g_ref, at_all, c_all) = refs[:count], refs[count : count + pieces], refs[count + pieces :]

    @pl.when(pl.program_id(0) == 0)
    def _():
        at = 0
        for across in ats:
            at_all[:, at : at + across.shape[1]] = across[...]
            at += across.shape[1]

    stack_rows(cs, c_all)
    g_ref[...] = nn(at_all[...], c_all[...]).astype(BF16)


def attn_backward_kernel(queries, keys, counts, *refs):
    blocks, rest = take(refs, counts)
    qkv_ref, w_ref, wo_ref, pick_ref, cos_ref, sin_ref = rest[:6]
    dhs, (dqkv_ref,) = rest[6 : 6 + len(blocks)], rest[6 + len(blocks) :]
    cosine, sine = cos_ref[...], sin_ref[...]
    length = cosine.shape[0]
    each = queries // keys
    scale = HEAD_DIM ** (-0.5)
    for n, block in enumerate(blocks):
        at_rows = slice(n * length, (n + 1) * length)
        d_heads = nt(load(block), wo_ref[...]).astype(BF16)
        d_heads = nt(d_heads, pick_ref[...]).astype(BF16)
        for at in range(keys):
            key = qkv_ref[at_rows, head_span(queries + at)]
            value = qkv_ref[at_rows, head_span(queries + keys + at)]
            d_key, d_value = 0.0, 0.0
            for k in range(at * each, (at + 1) * each):
                query = qkv_ref[at_rows, head_span(k)]
                d_head = d_heads[:, head_span(k)]
                probs = head_probs(query, key)
                d_value += tn(probs.astype(BF16), d_head)
                d_probs = nt(d_head, value)
                delta = jnp.sum(probs * d_probs, -1, keepdims=True)
                d_scores = (probs * (d_probs - delta) * scale).astype(BF16)
                d_query = nn(d_scores, key)
                d_key += tn(d_scores, query)
                dqkv_ref[at_rows, head_span(k)] = turn_back(d_query, cosine, sine).astype(BF16)
            dqkv_ref[at_rows, head_span(queries + at)] = turn_back(d_key, cosine, sine).astype(BF16)
            dqkv_ref[at_rows, head_span(queries + keys + at)] = d_value.astype(BF16)
    wtile = 2 * LANES

    def second(k, carry):
        at = pl.ds(pl.multiple_of(k * wtile, wtile), wtile)
        d_normed = nt(dqkv_ref[...], w_ref[at, :]).astype(BF16)
        for n in range(len(blocks)):
            dhs[n][:, at] = d_normed[n * length : (n + 1) * length]
        return carry

    lax.fori_loop(0, w_ref.shape[0] // wtile, second, 0)


def attn_backward(blocks, qkv, w, wo, pick, tables, queries, keys):
    counts = [len(b) for b in blocks]
    length, width = tables[0].shape[0], w.shape[0]
    rows = length * len(blocks)
    *dhs, dqkv = call(
        functools.partial(attn_backward_kernel, queries, keys, counts),
        [*flat(blocks), qkv, w, wo, pick, *tables],
        [((length, width), BF16)] * len(blocks) + [((rows, w.shape[1]), BF16)],
        flops=2 * rows * width * (w.shape[1] + wo.shape[0]) + 10 * rows * length * queries * LANES,
        exps=rows * length * queries,
    )
    return dhs, dqkv


def attn_grads_kernel(count, *refs):
    hs, ds, pick_ref = refs[:count], refs[count : 2 * count], refs[2 * count]
    g_ref, h_all, d_all = refs[2 * count + 1 :]

    @pl.when(pl.program_id(0) == 0)
    def _():
        stack_rows(ds, d_all)

    stack_rows(hs, h_all)
    grad = tn(h_all[...], d_all[...]).astype(BF16)
    g_ref[...] = nt(grad, pick_ref[...]).astype(BF16)


def out_grads_kernel(count, pieces, *refs):
    os, ms, (g_ref, o_all, m_all) = refs[:count], refs[count : count + pieces], refs[count + pieces :]

    @pl.when(pl.program_id(0) == 0)
    def _():
        stack_rows(os, o_all)

    stack_rows(ms, m_all)
    g_ref[...] = tn(o_all[...], m_all[...]).astype(BF16)


def grads_call(kernel, tiled, fixed, consts, out, along, flops, held=None):
    tile = 2 * LANES
    rows, width = sum(y.shape[0] for y in tiled), tiled[0].shape[1]
    held = held or (rows, fixed[0].shape[1])
    whole = lambda y: pl.BlockSpec(y.shape, lambda i: (0, 0), pipeline_mode=pl.Buffered(1))
    part = lambda y: pl.BlockSpec((y.shape[0], tile), lambda i: (0, i))
    moving, resident = pltpu.VMEM((rows, tile), BF16), pltpu.VMEM(held, BF16)
    if along == 0:
        inputs = [*tiled, *fixed, *consts]
        specs = [part(y) for y in tiled] + [whole(y) for y in [*fixed, *consts]]
        out_spec = pl.BlockSpec((tile, out[1]), lambda i: (i, 0))
        scratch = [moving, resident]
    else:
        inputs, specs = [*fixed, *tiled], [whole(y) for y in fixed] + [part(y) for y in tiled]
        out_spec = pl.BlockSpec((out[0], tile), lambda i: (0, i))
        scratch = [resident, moving]
    return pl.pallas_call(
        kernel,
        grid=(width // tile,),
        in_specs=specs,
        out_specs=out_spec,
        out_shape=jax.ShapeDtypeStruct(out, BF16),
        scratch_shapes=scratch,
        compiler_params=pltpu.CompilerParams(
            dimension_semantics=("arbitrary",), vmem_limit_bytes=GRADS_VMEM_BYTES
        ),
        cost_estimate=pl.CostEstimate(flops=flops, bytes_accessed=3 * rows * width, transcendentals=0),
    )(*inputs)


def finish_kernel(kind, counts, *refs):
    (whole, low, top), rest = take(refs, counts)
    length = whole[0].shape[0]
    cut = length // 2
    halves = []
    for half, extra in ((0, low), (1, top)):
        rows = slice(half * cut, (half + 1) * cut)
        total = sum(t[rows, :].astype(F32) for t in whole)
        halves.append(sum((t[...].astype(F32) for t in extra), total))
    total = jnp.concatenate(halves, 0)
    if kind == "middle":
        x_ref, gain_ref, middle_ref, h_ref = rest
        middle = x_ref[...].astype(F32) + total
        middle_ref[...] = middle
        h_ref[...] = (middle * inverse_rms(middle) * gain_ref[...]).astype(BF16)
    elif kind == "output":
        middle_ref, out_ref = rest
        out_ref[...] = (middle_ref[...] + total).astype(BF16)
    else:
        rows_ref, base_ref, gain_ref, *outs = rest
        rows = rows_ref[...].astype(F32)
        inverse = inverse_rms(rows)
        scaled = total * gain_ref[...]
        mean = jnp.mean(scaled * rows, -1, keepdims=True)
        made = base_ref[...].astype(F32) + inverse * scaled - rows * inverse**3 * mean
        for out in outs:
            out[...] = made.astype(out.dtype)


def finish(kind, terms, extras, kinds):
    counts = [len(t) for t in terms]
    shape = terms[0][0].shape
    return call(
        functools.partial(finish_kernel, kind, counts),
        [*flat(terms), *extras],
        [(shape, k) for k in kinds],
        flops=16 * math.prod(shape),
    )


def spread_wide_kernel(counts, at_ref, *refs):
    blocks, (wg_ref, wu_ref, gate_out, up_out, gain_out) = take(refs, counts)
    j, part = pl.program_id(0), pl.program_id(1)
    tile, parts = gate_out.shape[1], pl.num_programs(1)

    @pl.when((j == 0) & (part == 0))
    def _():
        gain_out[...] = jnp.zeros_like(gain_out)

    here = pl.multiple_of(part * tile, tile)
    over = pl.multiple_of((parts + part) * tile, tile)
    for k, block in enumerate(blocks):

        @pl.when(j == k)
        def _(block=block):
            at = 0
            for piece in block:
                rows = slice(at, at + piece.shape[0])
                gate_out[rows, :] = piece[:, pl.ds(here, tile)].astype(F32)
                up_out[rows, :] = piece[:, pl.ds(over, tile)].astype(F32)
                at += piece.shape[0]

    gain_out[...] += gate_out[...] * wg_ref[...].astype(F32) + up_out[...] * wu_ref[...].astype(F32)


def spread_wide(at, blocks, w_gate, w_up, parts):
    counts, pieces, count = [len(b) for b in blocks], flat(blocks), len(blocks)
    width, total = w_gate.shape
    tile = total // count // parts
    columns = pl.BlockSpec((width, tile), lambda j, s, at: (0, s * count + (j ^ at[0])))
    return pl.pallas_call(
        functools.partial(spread_wide_kernel, counts),
        grid_spec=pltpu.PrefetchScalarGridSpec(
            num_scalar_prefetch=1,
            grid=(count, parts),
            in_specs=[
                pl.BlockSpec(p.shape, lambda j, s, at: (0, 0), pipeline_mode=pl.Buffered(1))
                for p in pieces
            ]
            + [columns, columns],
            out_specs=[columns, columns, pl.BlockSpec((width, tile), lambda j, s, at: (0, 0))],
        ),
        out_shape=[
            jax.ShapeDtypeStruct((width, total), F32),
            jax.ShapeDtypeStruct((width, total), F32),
            jax.ShapeDtypeStruct((width, tile), F32),
        ],
        compiler_params=pltpu.CompilerParams(
            dimension_semantics=("arbitrary", "arbitrary"), vmem_limit_bytes=VMEM_BYTES
        ),
        cost_estimate=pl.CostEstimate(flops=0, bytes_accessed=16 * width * total, transcendentals=0),
        name="sw",
    )(at, *pieces, w_gate, w_up)


def spread_rows_kernel(counts, at_ref, *refs):
    blocks, (down_out, o_out) = take(refs, counts)
    j, short = pl.program_id(0), down_out.shape[0]
    for k, block in enumerate(blocks):

        @pl.when(j == k)
        def _(block=block):
            values = load(block).astype(F32)
            down_out[...] = values[:short]
            o_out[...] = values[short:]


def spread_rows(at, blocks, short):
    counts, pieces, count = [len(b) for b in blocks], flat(blocks), len(blocks)
    rows, width = sum(p.shape[0] for p in blocks[0]), pieces[0].shape[1]
    place = lambda j, at: (j ^ at[0], 0)
    return pl.pallas_call(
        functools.partial(spread_rows_kernel, counts),
        grid_spec=pltpu.PrefetchScalarGridSpec(
            num_scalar_prefetch=1,
            grid=(count,),
            in_specs=[
                pl.BlockSpec(p.shape, lambda j, at: (0, 0), pipeline_mode=pl.Buffered(1))
                for p in pieces
            ],
            out_specs=[pl.BlockSpec((short, width), place), pl.BlockSpec((rows - short, width), place)],
        ),
        out_shape=[
            jax.ShapeDtypeStruct((count * short, width), F32),
            jax.ShapeDtypeStruct((count * (rows - short), width), F32),
        ],
        compiler_params=pltpu.CompilerParams(
            dimension_semantics=("arbitrary",), vmem_limit_bytes=VMEM_BYTES
        ),
        cost_estimate=pl.CostEstimate(flops=0, bytes_accessed=6 * count * rows * width, transcendentals=0),
        name="sr",
    )(at, *pieces)


def spread_attn_kernel(counts, count, cuts, at_ref, *refs):
    blocks, rest = take(refs, counts)
    (wq_ref, wk_ref, wv_ref), (q_out, k_out, v_out, gain_out, stack) = rest[:3], rest[3:]
    step = pl.program_id(0)

    @pl.when(step == 0)
    def _():
        gain_out[...] = jnp.zeros_like(gain_out)
        for j, block in enumerate(blocks):
            stack[j ^ at_ref[0]] = load(block)

    total = 0.0
    spans = ((0, cuts[0]), (cuts[0], cuts[1]), (cuts[1], stack.shape[2]))
    held = [stack[step * count + i].astype(F32) for i in range(count)]
    for (low, high), out, w_ref in zip(spans, (q_out, k_out, v_out), (wq_ref, wk_ref, wv_ref)):
        made = jnp.concatenate([b[:, low:high] for b in held], 1)
        out[...] = made
        total += jnp.sum(made * w_ref[...].astype(F32), 1, keepdims=True)
    gain_out[...] += total


def spread_attn(at, blocks, weights, cuts):
    counts, pieces, group = [len(b) for b in blocks], flat(blocks), len(blocks)
    slab, narrow = weights[0].shape[0], pieces[0].shape[1]
    count = math.gcd(group, LANES // math.gcd(LANES, HEAD_DIM))
    widths = (cuts[0], cuts[1] - cuts[0], narrow - cuts[1])
    columns = [pl.BlockSpec((slab, count * w), lambda p, at: (0, p)) for w in widths]
    return pl.pallas_call(
        functools.partial(spread_attn_kernel, counts, count, cuts),
        grid_spec=pltpu.PrefetchScalarGridSpec(
            num_scalar_prefetch=1,
            grid=(group // count,),
            in_specs=[
                pl.BlockSpec(p.shape, lambda p_, at: (0, 0), pipeline_mode=pl.Buffered(1))
                for p in pieces
            ]
            + columns,
            out_specs=columns + [pl.BlockSpec((slab, 1), lambda p, at: (0, 0))],
            scratch_shapes=[pltpu.VMEM((group, slab, narrow), BF16)],
        ),
        out_shape=[jax.ShapeDtypeStruct((slab, group * w), F32) for w in widths]
        + [jax.ShapeDtypeStruct((slab, 1), F32)],
        compiler_params=pltpu.CompilerParams(
            dimension_semantics=("arbitrary",), vmem_limit_bytes=VMEM_BYTES
        ),
        cost_estimate=pl.CostEstimate(
            flops=0, bytes_accessed=8 * group * slab * narrow, transcendentals=0
        ),
        name="sa",
    )(at, *pieces, *weights)


def pick_wide_kernel(parts, at_ref, gate_ref, up_ref, out_ref):
    @pl.when(pl.program_id(0) < parts)
    def _():
        out_ref[...] = gate_ref[...]

    @pl.when(pl.program_id(0) >= parts)
    def _():
        out_ref[...] = up_ref[...]


def pick_wide(at, w_gate, w_up, group, parts):
    width, total = w_gate.shape
    tile = total // group // parts
    columns = pl.BlockSpec((width, tile), lambda k, at: (0, lax.rem(k, parts) * group + at[0]))
    return pl.pallas_call(
        functools.partial(pick_wide_kernel, parts),
        grid_spec=pltpu.PrefetchScalarGridSpec(
            num_scalar_prefetch=1,
            grid=(2 * parts,),
            in_specs=[columns, columns],
            out_specs=pl.BlockSpec((width, tile), lambda k, at: (0, k)),
        ),
        out_shape=jax.ShapeDtypeStruct((width, 2 * parts * tile), BF16),
        compiler_params=pltpu.CompilerParams(dimension_semantics=("arbitrary",)),
        cost_estimate=pl.CostEstimate(
            flops=0, bytes_accessed=12 * width * parts * tile, transcendentals=0
        ),
        name="pick",
    )(at, w_gate, w_up)


def head_columns(queries, keys):
    half, lane = HEAD_DIM // 2, jnp.arange(LANES)
    place = lane % (LANES // 2)
    turned = jnp.where(place < half, (lane // (LANES // 2)) * half + place, -1)
    plain = jnp.where(lane < HEAD_DIM, lane, -1)
    columns = []
    for k in range(queries + 2 * keys):
        inside = turned if k < queries + keys else plain
        columns.append(jnp.where(inside >= 0, inside + k * HEAD_DIM, -1))
    return jnp.concatenate(columns)


def gather_shard(x):
    return lax.all_gather(x, "shard", axis=0, tiled=True)


def scatter_shard(x):
    return lax.psum_scatter(x, "shard", scatter_dimension=0, tiled=True)


def after(x, *others):
    return lax.optimization_barrier((x, *others))[0]


def layer(
    tokens, cotangent, attn_gain, w_query, w_key, w_value, w_out, mlp_gain, w_gate, w_up, w_down
):
    replicas, shards = lax.axis_size("replica"), lax.axis_size("shard")
    length, width = tokens.shape
    slab = w_query.shape[0]
    kv_heads = w_key.shape[1] // HEAD_DIM
    group = math.gcd(replicas, kv_heads)
    keys = kv_heads // group
    queries = w_query.shape[1] // HEAD_DIM // group
    high = [1 << k for k in range(1, group.bit_length() - 1)]
    place = lax.axis_index("replica") % group
    hidden = w_down.shape[0] // group
    narrow = (queries + 2 * keys) * HEAD_DIM

    x = plane_gather(tokens, high)

    wq = lax.dynamic_slice_in_dim(w_query, place * queries * HEAD_DIM, queries * HEAD_DIM, 1)
    wk = lax.dynamic_slice_in_dim(w_key, place * keys * HEAD_DIM, keys * HEAD_DIM, 1)
    wv = lax.dynamic_slice_in_dim(w_value, place * keys * HEAD_DIM, keys * HEAD_DIM, 1)
    spare = 16
    gain_rows = -(-slab // narrow)
    gains = jnp.stack([attn_gain, mlp_gain])
    gains = jnp.pad(gains, ((0, 0), (0, gain_rows * narrow - slab))).reshape(2 * gain_rows, narrow)
    gains = jnp.pad(gains, ((0, spare - 2 * gain_rows), (0, 0)))
    sent = jnp.concatenate([jnp.concatenate([wq, wk, wv], 1), gains], 0)
    both = gather_shard(sent).reshape(shards, slab + spare, narrow)
    w_out, w_gate_s, w_up_s, w_down_s, _ = lax.optimization_barrier((w_out, w_gate, w_up, w_down, sent))

    turns = group // shards
    chunk = w_out.shape[0] // group
    mine = lax.dynamic_slice_in_dim(w_out, place * chunk, chunk, 0)
    routes = []
    for turn_by in range(shards):
        route = []
        for i in range(replicas):
            base, q = i - i % group, i % group
            for z in range(shards):
                to = (base + z * turns + q // shards) * shards + (q + turn_by) % shards
                route.append((i * shards + z, to))
        routes.append(route)
    back = [(b, a) for a, b in routes[0]]
    came = []
    for route in routes:
        came.append(lax.ppermute(mine, ("replica", "shard"), route))
    here = lax.axis_index("shard")
    came = jnp.stack(came)[(here - jnp.arange(shards)) % shards]
    wo = came.reshape(shards * chunk, width)

    columns = head_columns(queries, keys)
    pick = (jnp.arange(narrow)[:, None] == columns[None, :]).astype(BF16)
    wqkv = nn(both[:, :slab].reshape(width, narrow), pick).astype(BF16)
    gains = both[:, slab : slab + 2 * gain_rows].reshape(shards, 2, gain_rows * narrow)[:, :, :slab]
    gains = jnp.moveaxis(gains, 1, 0).reshape(2, 1, width).astype(F32)
    gain_a, gain_m = gains[0], gains[1]
    lanes = jnp.arange(queries * LANES)
    heads = (lanes // LANES) * HEAD_DIM + lanes % LANES
    heads = jnp.where(lanes % LANES < HEAD_DIM, heads, -1)
    pick_o = (jnp.arange(queries * HEAD_DIM)[None, :] == heads[:, None]).astype(BF16)

    wgu = pick_wide(place.reshape(1), w_gate_s, w_up_s, group, shards)
    wd = lax.dynamic_slice_in_dim(w_down_s, place * hidden, hidden, 0)
    wgu = gather_shard(wgu)
    wd = gather_shard(wd)

    c = plane_gather(after(cotangent, *x[high[0]], *x[high[-1]]), high)

    pairs = [j for j in sorted(x, reverse=True) if j % 2 == 0]
    tables = rope_tables(length)
    parts, saved = {}, {}
    for j in pairs:
        (parts[j ^ 1], parts[j]), saved[j] = attn_forward(
            [x[j ^ 1], x[j]], gain_a, wqkv, wo, pick_o, tables, queries, keys
        )
    middle, h_own = finish("middle", plane_scatter(parts, high), [tokens, gain_m], [F32, BF16])
    h = plane_gather(h_own, high)

    order = list(reversed(pairs))
    order = order[:-2] + [order[-1], order[-2]] if len(order) > 2 else order
    outs, dhs, dgus, acrosses = {}, {}, [], []
    for j in order:
        (outs[j ^ 1], outs[j]), (dhs[j ^ 1], dhs[j]), dgu, across = mlp_both(
            [h[j ^ 1], h[j]], [c[j ^ 1], c[j]], wgu, wd
        )
        dgus.append(dgu)
        acrosses.append(across)
    d_middle, dm_own = finish(
        "back", plane_scatter(dhs, high), [middle, cotangent, gain_m], [F32, BF16]
    )
    all_h = flat(h[k] for j in order for k in (j ^ 1, j))
    all_c = flat(c[k] for j in order for k in (j ^ 1, j))
    rows = group * length
    g_gu = grads_call(
        functools.partial(wide_grads_kernel, len(dgus), len(all_h)),
        all_h, dgus, [], wgu.shape, 0, 2 * rows * width * wgu.shape[1],
    )
    g_d = grads_call(
        functools.partial(down_grads_kernel, len(acrosses), len(all_c)),
        all_c, acrosses, [], wd.shape, 1, 2 * rows * width * wd.shape[0],
        (wd.shape[0], rows),
    )
    g_gu = scatter_shard(g_gu)
    dm = plane_gather(dm_own, high)
    all_dm = flat(dm[k] for j in order for k in (j ^ 1, j))
    g_o = grads_call(
        functools.partial(out_grads_kernel, len(pairs), len(all_dm)),
        all_dm, [saved[j][2] for j in order], [], wo.shape, 1,
        2 * rows * width * wo.shape[0],
    )
    g_rows = [g.reshape(shards, -1, width) for g in (g_d, g_o)]
    g_rows = scatter_shard(jnp.concatenate(g_rows, 1).reshape(-1, width))
    g_o = lax.ppermute(g_rows[hidden:], ("replica", "shard"), back)
    g_rows = jnp.concatenate([g_rows[:hidden], g_o], 0)

    das, dqkvs = {}, []
    for j in order:
        (das[j ^ 1], das[j]), dqkv = attn_backward(
            [dm[j ^ 1], dm[j]], saved[j][1], wqkv, wo, pick_o, tables, queries, keys
        )
        dqkvs.append(dqkv)
    g_w = grads_call(
        functools.partial(attn_grads_kernel, len(pairs)),
        [saved[j][0] for j in order], dqkvs, [pick], (width, narrow), 0,
        2 * rows * width * pick.shape[1],
    )
    g_w = scatter_shard(g_w)
    da_terms = plane_scatter(das, high)
    (input_grad,) = finish("back", da_terms, [tokens, d_middle, gain_a], [F32])

    outs = dict(zip(outs, (after(y, *all_dm) for y in outs.values())))
    out_terms = plane_scatter(outs, high)
    (block_output,) = finish("output", out_terms, [middle], [BF16])

    bit = group
    while bit < replicas:
        g_gu, g_rows, g_w = (g + swap(g, bit) for g in (g_gu, g_rows, g_w))
        bit *= 2

    def blocks(g):
        got = plane_gather(g, high)
        return [got[j] for j in range(group)]

    here = place.reshape(1)
    gate_grad, up_grad, gain_terms = spread_wide(here, blocks(g_gu), w_gate, w_up, shards)
    mlp_gain_grad = jnp.sum(gain_terms, 1) / mlp_gain.astype(F32)
    down_grad, out_grad = spread_rows(here, blocks(g_rows), hidden)
    cuts = (queries * HEAD_DIM, (queries + keys) * HEAD_DIM)
    query_grad, key_grad, value_grad, gain_terms = spread_attn(
        here, blocks(g_w), (w_query, w_key, w_value), cuts
    )
    attn_gain_grad = gain_terms[:, 0] / attn_gain.astype(F32)
    return (
        block_output,
        input_grad,
        attn_gain_grad,
        query_grad,
        key_grad,
        value_grad,
        out_grad,
        mlp_gain_grad,
        gate_grad,
        up_grad,
        down_grad,
    )


def solution(mesh):
    tokens, weights, gains = P(("replica", "shard"), None), P("shard", None), P("shard")
    return jax.shard_map(
        layer,
        mesh=mesh,
        in_specs=(tokens, tokens, gains, weights, weights, weights, weights, gains, weights, weights, weights),
        out_specs=(tokens, tokens, gains, weights, weights, weights, weights, gains, weights, weights, weights),
        check_vma=False,
    )
```
